32 devices in a mesh: seq: 16 (over z, y, x), batch: 2 (over core).
Axes of the slice: x: 2, y: 2, z: 4, core: 2. Of those that a mesh axis runs over, the one named last changes fastest.
Arguments:
- tokens: bfloat16 [2, 2048, 768], P('batch', 'seq'), may hold values from -6 to 6
- cotangent: bfloat16 [2, 2048, 768], P('batch', 'seq'), may hold values from -6 to 6
- prefix_len: int32 [2], P('batch'), may hold values from 204 to 1024
- gain_one: bfloat16 [768], P(('seq', 'batch')), may hold values from 0.25 to 1.75
- shift_one: bfloat16 [768], P(('seq', 'batch')), may hold values from -1.75 to 1.75
- w_query: bfloat16 [768, 768], P(('seq', 'batch')), may hold values from -0.21875 to 0.21875
- b_query: bfloat16 [768], P(('seq', 'batch')), may hold values from -3 to 3
- w_key: bfloat16 [768, 768], P(('seq', 'batch')), may hold values from -0.21875 to 0.21875
- w_value: bfloat16 [768, 768], P(('seq', 'batch')), may hold values from -0.21875 to 0.21875
- b_value: bfloat16 [768], P(('seq', 'batch')), may hold values from -3 to 3
- w_output: bfloat16 [768, 768], P(('seq', 'batch')), may hold values from -3.5 to 3.5
- b_output: bfloat16 [768], P(('seq', 'batch')), may hold values from -1.75 to 1.75
- gain_two: bfloat16 [768], P(('seq', 'batch')), may hold values from 0.25 to 1.75
- shift_two: bfloat16 [768], P(('seq', 'batch')), may hold values from -1.75 to 1.75
- w_up: bfloat16 [768, 3072], P(('seq', 'batch')), may hold values from -0.21875 to 0.21875
- b_up: bfloat16 [3072], P(('seq', 'batch')), may hold values from -3 to 3
- w_down: bfloat16 [3072, 768], P(('seq', 'batch')), may hold values from -0.109375 to 0.109375
- b_down: bfloat16 [768], P(('seq', 'batch')), may hold values from -1.75 to 1.75
Outputs:
- layer_out: bfloat16 [2, 2048, 768], P('batch', 'seq')
- grad_tokens: float32 [2, 2048, 768], P('batch', 'seq')
- grad_gain_one: float32 [768], P(('seq', 'batch'))
- grad_shift_one: float32 [768], P(('seq', 'batch'))
- grad_w_query: float32 [768, 768], P(('seq', 'batch'))
- grad_b_query: float32 [768], P(('seq', 'batch'))
- grad_w_key: float32 [768, 768], P(('seq', 'batch'))
- grad_w_value: float32 [768, 768], P(('seq', 'batch'))
- grad_b_value: float32 [768], P(('seq', 'batch'))
- grad_w_output: float32 [768, 768], P(('seq', 'batch'))
- grad_b_output: float32 [768], P(('seq', 'batch'))
- grad_gain_two: float32 [768], P(('seq', 'batch'))
- grad_shift_two: float32 [768], P(('seq', 'batch'))
- grad_w_up: float32 [768, 3072], P(('seq', 'batch'))
- grad_b_up: float32 [3072], P(('seq', 'batch'))
- grad_w_down: float32 [3072, 768], P(('seq', 'batch'))
- grad_b_down: float32 [768], P(('seq', 'batch'))
The draws below stay inside these ranges and needn't reach their ends.
Inputs may be any that keep to these rules, and one draw needn't show every extreme that they name: `prefix_len`: one prefix length per sequence.
All inputs are finite; a program needn't handle non-finite values.
Results may differ from the reference program's by a relative error of at most 0.014.
Values may be sent and summed in bfloat16 or wider, within the bound.
No kernel may reach another device: no remote copies, remote signals or barrier semaphores. Data moves between devices by JAX's collectives and lax.ppermute only.
A program may use at most 192 MiB of HBM per device.

```python
import jax
import jax.numpy as jnp
from jax import lax

D = 768
HEADS = 12
HD = 64
FF = 3072
LEN = 2048
SEQS = 2


def shard_levels(own_key, dims, pieces, least, largest):
    factor_of, own = 1.0, jax.random.fold_in(own_key, 6)
    for position, shards_of in pieces:
        draws = jnp.exp(jax.random.uniform(jax.random.fold_in(own, position), (shards_of,), jnp.float32, least / len(pieces), largest / len(pieces)))
        factor_of = factor_of * jnp.repeat(draws, dims[position] // shards_of).reshape([-1 if axis == position else 1 for axis in range(len(dims))])
    return factor_of


def bell_draw(key, dims, scale, most, cuts=(), kind=jnp.bfloat16):
    loudness = shard_levels(key, dims, cuts, -0.22, 0.18) if cuts else 1.0
    drawn = jax.random.normal(key, dims, jnp.float32) * scale * loudness
    return jnp.minimum(jnp.maximum(drawn, -most), most).astype(kind)


def setup_inputs(seed: int = 0) -> dict:
    seeds = jax.random.split(jax.random.key(seed), 19)
    return {
        "tokens": bell_draw(seeds[0], (SEQS, LEN, D), 1.0, 6.0, ((0, 2), (1, 16))),
        "cotangent": bell_draw(seeds[1], (SEQS, LEN, D), 1.0, 6.0, ((0, 2), (1, 16))),
        "prefix_len": jax.random.randint(seeds[2], (SEQS,), LEN // 10, LEN // 2 + 1).astype(jnp.int32),
        "gain_one": jnp.clip(1.0 + 0.15 * jax.random.normal(seeds[3], (D,), jnp.float32), 0.25, 1.75).astype(jnp.bfloat16),
        "shift_one": bell_draw(seeds[4], (D,), 0.3, 1.75, ((0, 32),)),
        "w_query": bell_draw(seeds[5], (D, D), D ** -0.5, 0.21875, ((0, 32),)),
        "b_query": bell_draw(seeds[6], (D,), 0.5, 3.0, ((0, 32),)),
        "w_key": bell_draw(seeds[7], (D, D), D ** -0.5, 0.21875, ((0, 32),)),
        "w_value": bell_draw(seeds[8], (D, D), D ** -0.5, 0.21875, ((0, 32),)),
        "b_value": bell_draw(seeds[9], (D,), 0.5, 3.0, ((0, 32),)),
        "w_output": bell_draw(seeds[10], (D, D), (D // 256) ** -0.5, 3.5, ((0, 32),)),
        "b_output": bell_draw(seeds[11], (D,), 0.3, 1.75, ((0, 32),)),
        "gain_two": jnp.clip(1.0 + 0.15 * jax.random.normal(seeds[12], (D,), jnp.float32), 0.25, 1.75).astype(jnp.bfloat16),
        "shift_two": bell_draw(seeds[13], (D,), 0.3, 1.75, ((0, 32),)),
        "w_up": bell_draw(seeds[14], (D, FF), D ** -0.5, 0.21875, ((0, 32),)),
        "b_up": bell_draw(seeds[15], (FF,), 0.5, 3.0, ((0, 32),)),
        "w_down": bell_draw(seeds[16], (FF, D), FF ** -0.5, 0.109375, ((0, 32),)),
        "b_down": bell_draw(seeds[17], (D,), 0.3, 1.75, ((0, 32),)),
    }


EPS = 1e-05

@jax.custom_vjp
def low(v):
    return lax.optimization_barrier(v.astype(jnp.bfloat16)).astype(jnp.float32)

@jax.custom_vjp
def low_back(v):
    return v

def low_keep(v):
    return (low(v), None)

def low_pass(kept, grad):
    return (grad,)

def back_keep(v):
    return (v, None)

def back_low(kept, grad):
    return (low(grad),)
low.defvjp(low_keep, low_pass)
low_back.defvjp(back_keep, back_low)

def round_both(values):
    return low(low_back(values))

def matmul(left, right):
    return jnp.dot(left, right, precision=lax.Precision.HIGHEST)

def layer_norm(values, gain, shift):
    centre = lax.optimization_barrier(jnp.mean(values, axis=-1, keepdims=True))
    centred = values - centre
    spread = lax.optimization_barrier(jnp.mean(centred * centred, axis=-1, keepdims=True))
    return centred * lax.rsqrt(spread + EPS) * gain + shift

def attend(queries, key_rows, values, prefix):
    block_rows = min(512, LEN)
    block_count = LEN // block_rows
    q_heads = queries.reshape(block_count, block_rows, HEADS, HD)
    k_heads = key_rows.reshape(LEN, HEADS, HD)
    v_heads = values.reshape(LEN, HEADS, HD)
    starts = jnp.arange(block_count, dtype=jnp.int32) * block_rows
    col_ids = jnp.arange(LEN, dtype=jnp.int32)

    def one_block(item):
        q_part, first_row = item
        scores = 0.125 * jnp.einsum('qhd,khd->hqk', q_part, k_heads, precision=lax.Precision.HIGHEST)
        scores = low_back(scores)
        row_ids = first_row + jnp.arange(block_rows, dtype=jnp.int32)
        allowed = (col_ids[None, :] <= row_ids[:, None]) | (col_ids[None, :] < prefix)
        scores = jnp.where(allowed[None], scores, -1e+30)
        top = lax.optimization_barrier(jnp.max(scores, axis=-1, keepdims=True))
        expo = jnp.exp(scores - top)
        attn_prob = low(expo / lax.optimization_barrier(jnp.sum(expo, axis=-1, keepdims=True)))
        context = jnp.einsum('hqk,khd->qhd', attn_prob, v_heads, precision=lax.Precision.HIGHEST)
        return context.reshape(block_rows, HEADS * HD)
    return lax.map(jax.checkpoint(one_block), (q_heads, starts)).reshape(LEN, HEADS * HD)

def forward(hidden, params, prefix):
    gain_one, shift_one, w_query, b_query, w_key, w_value, b_value, w_output, b_output, gain_two, shift_two, w_up, b_up, w_down, b_down = params
    norm_one = low(layer_norm(hidden, gain_one, shift_one))
    queries = round_both(matmul(norm_one, w_query) + b_query)
    key_rows = round_both(matmul(norm_one, w_key))
    values = round_both(matmul(norm_one, w_value) + b_value)
    context = round_both(attend(queries, key_rows, values, prefix))
    branch = low_back(matmul(context, w_output) + b_output)
    middle = hidden + branch
    norm_two = low(layer_norm(middle, gain_two, shift_two))
    pre_act = low_back(matmul(norm_two, w_up) + b_up)
    act = low(0.5 * pre_act * (1.0 + jax.scipy.special.erf(pre_act * 0.7071067811865476)))
    return middle + matmul(act, w_down) + b_down

def reference(tokens, cotangent, prefix_len, gain_one, shift_one, w_query, b_query, w_key, w_value, b_value, w_output, b_output, gain_two, shift_two, w_up, b_up, w_down, b_down):
    params = tuple((weight.astype(jnp.float32) for weight in (gain_one, shift_one, w_query, b_query, w_key, w_value, b_value, w_output, b_output, gain_two, shift_two, w_up, b_up, w_down, b_down)))

    def per_sequence(totals, item):
        seq_tokens, seq_cot, prefix = item
        hidden = seq_tokens.astype(jnp.float32)
        result, pullback = jax.vjp(lambda inner, weights: forward(inner, weights, prefix), hidden, params)
        grad_in, grad_params = pullback(seq_cot.astype(jnp.float32))
        totals = tuple((left + right for left, right in zip(totals, grad_params)))
        return (totals, (result.astype(jnp.bfloat16), grad_in))
    start = tuple((jnp.zeros_like(weight) for weight in params))
    final, (outputs, grad_inputs) = lax.scan(per_sequence, start, (tokens, cotangent, prefix_len))
    return (outputs, grad_inputs, final[0], final[1], final[2], final[3], final[4], final[5], final[6], final[7], final[8], final[9], final[10], final[11], final[12], final[13], final[14])
```

```python
import functools

import jax
import jax.numpy as jnp
from jax import lax
from jax.experimental import pallas as pl
from jax.experimental.pallas import tpu as pltpu
from jax.sharding import Mesh
from jax.sharding import PartitionSpec as P

HD = 64
EPS = 1e-05
LOG2E = 1.4426950408889634
SEQ = ("zo", "y", "x")
BAT = ("bo", "bi")
ALL = SEQ + BAT
TP = ("x", "bi")
WIDE = 4 * HD
NVEC = 12
F32 = jnp.float32
BF16 = jnp.bfloat16


def normalize(values):
    centre = jnp.mean(values, axis=-1, keepdims=True)
    centred = values - centre
    spread = jnp.mean(centred * centred, axis=-1, keepdims=True)
    factor = lax.rsqrt(spread + EPS)
    return (centred * factor, factor)


def norm_backward(grad_out, normed, factor, gain):
    grad_gain = jnp.sum(grad_out * normed, axis=0)
    grad_shift = jnp.sum(grad_out, axis=0)
    scaled = grad_out * gain
    grad_in = factor * (
        scaled
        - jnp.mean(scaled, axis=-1, keepdims=True)
        - normed * jnp.mean(scaled * normed, axis=-1, keepdims=True)
    )
    return (grad_in, grad_gain, grad_shift)


def dot(left, right, dims=((1,), (0,))):
    return lax.dot_general(left, right, (dims, ((), ())), preferred_element_type=F32)


NN = ((1,), (0,))
NT = ((1,), (1,))
TN = ((0,), (0,))


def swap(value, axis, step=1):
    size = lax.axis_size(axis)
    return lax.ppermute(value, axis, [(i, i ^ step) for i in range(size)])


def pick(value, index, axis):
    return lax.dynamic_index_in_dim(value, index, axis, keepdims=False)


def split(length):
    return 512 if length % 512 == 0 else length


def forward_kernel(
    outer, heads, scal, zc, xc, yc, xya, xyb, w, n1, qkvt, ctxc, ctxt, lse, wt_s, k_s
):
    place, prefix = (scal[0], scal[1])
    rows = zc.shape[1]
    length = n1.shape[0]
    blk = split(length)
    wide = jnp.transpose(w[...].astype(F32))
    wt_s[...] = wide[: 3 * HD].astype(BF16)
    gain = wide[3 * HD : 3 * HD + 1]
    shift = wide[3 * HD + 1 : 3 * HD + 2]

    def norm_piece(src, first, low):
        def one(k, carry):
            value = src[k].astype(F32)
            normed, _ = normalize(value)
            at = jnp.bitwise_xor(place, (first + k) * 4 + low) * rows
            n1[pl.ds(pl.multiple_of(at, rows), rows), :] = (normed * gain + shift).astype(BF16)
            return carry

        lax.fori_loop(0, src.shape[0], one, 0)

    norm_piece(zc, 0, 0)
    norm_piece(xc, 0, 1)
    norm_piece(yc, 0, 2)
    norm_piece(xya, 0, 3)
    norm_piece(xyb, outer // 2, 3)
    head = jnp.minimum(place, heads - 1)
    at = pl.multiple_of(head * HD, HD)
    bias_q = w[pl.ds(at, HD), 3 * HD + 2 : 3 * HD + 3].astype(F32)
    bias_v = w[pl.ds(at, HD), 3 * HD + 3 : 3 * HD + 4].astype(F32)
    for i in range(length // blk):
        part = dot(wt_s[...], n1[i * blk : (i + 1) * blk, :], NT)
        q_part = (part[:HD] + bias_q).astype(BF16)
        k_part = part[HD : 2 * HD].astype(BF16)
        v_part = (part[2 * HD :] + bias_v).astype(BF16)
        qkvt[:HD, i * blk : (i + 1) * blk] = q_part
        qkvt[HD : 2 * HD, i * blk : (i + 1) * blk] = k_part
        qkvt[2 * HD :, i * blk : (i + 1) * blk] = v_part
        k_s[i * blk : (i + 1) * blk, :] = jnp.transpose(k_part.astype(F32)).astype(BF16)
    scale = 0.125 * LOG2E

    def one_query(i, carry):
        first = pl.multiple_of(i * blk, blk)
        q_now = qkvt[:HD, pl.ds(first, blk)]

        def step(masked, j, state):
            top, total, acc = state
            start = pl.multiple_of(j * blk, blk)
            scores = dot(k_s[pl.ds(start, blk), :], q_now) * scale
            if masked:
                key = start + lax.broadcasted_iota(jnp.int32, (blk, blk), 0)
                query = first + lax.broadcasted_iota(jnp.int32, (blk, blk), 1)
                scores = jnp.where((key <= query) | (key < prefix), scores, -1e30)
            new_top = jnp.maximum(top, jnp.max(scores, axis=0, keepdims=True))
            prob = jnp.exp2(scores - new_top)
            fade = jnp.exp2(top - new_top)
            total = total * fade + jnp.sum(prob, axis=0, keepdims=True)
            acc = acc * fade + dot(qkvt[2 * HD :, pl.ds(start, blk)], prob.astype(BF16))
            return (new_top, total, acc)

        state = (
            jnp.full((1, blk), -1e30, F32),
            jnp.zeros((1, blk), F32),
            jnp.zeros((HD, blk), F32),
        )
        full = jnp.maximum(prefix // blk, i)
        needed = jnp.maximum((prefix + blk - 1) // blk, i + 1)
        state = lax.fori_loop(0, full, functools.partial(step, False), state)
        top, total, acc = lax.fori_loop(full, needed, functools.partial(step, True), state)
        out = acc / total
        ctxt[:, pl.ds(first, blk)] = out
        lse[:, pl.ds(first, blk)] = top + jnp.log2(total)
        for r in range(blk // rows):
            ctxc[i * (blk // rows) + r] = out[:, r * rows : (r + 1) * rows].astype(BF16)
        return carry

    lax.fori_loop(0, length // blk, one_query, 0)


def backward_kernel(
    scal, qkvt, dcr, ctxt, lse, dchunk, dall, q_s, k_s, v_s, dc_s, dct_s, del_s, dq_s, dk_s, dv_s
):
    prefix = scal[1]
    rows = dcr.shape[2]
    length = qkvt.shape[1]
    blk = split(length)
    count = length // blk
    for i in range(count):
        sl = slice(i * blk, (i + 1) * blk)
        turned = jnp.transpose(qkvt[:, sl].astype(F32)).astype(BF16)
        q_s[sl, :] = turned[:, :HD]
        k_s[sl, :] = turned[:, HD : 2 * HD]
        v_s[sl, :] = turned[:, 2 * HD :]
    for i in range(length // rows):
        sl = slice(i * rows, (i + 1) * rows)
        dct_s[:, sl] = dcr[i]
        dc_s[sl, :] = jnp.transpose(dcr[i].astype(F32)).astype(BF16)
    del_s[...] = jnp.sum(dct_s[...].astype(F32) * ctxt[...], axis=0, keepdims=True)
    dq_s[...] = jnp.zeros_like(dq_s)
    scale = 0.125 * LOG2E

    def one_key(j, carry):
        start = pl.multiple_of(j * blk, blk)
        dk_s[...] = jnp.zeros_like(dk_s)
        dv_s[...] = jnp.zeros_like(dv_s)

        def step(masked, i, inner):
            first = pl.multiple_of(i * blk, blk)
            here = pl.ds(first, blk)
            scores = dot(k_s[pl.ds(start, blk), :], qkvt[:HD, here]) * scale
            prob = jnp.exp2(scores - lse[:, here])
            if masked:
                key = start + lax.broadcasted_iota(jnp.int32, (blk, blk), 0)
                query = first + lax.broadcasted_iota(jnp.int32, (blk, blk), 1)
                prob = jnp.where((key <= query) | (key < prefix), prob, 0.0)
            d_prob = dot(v_s[pl.ds(start, blk), :], dct_s[:, here])
            d_score = (prob * (d_prob - del_s[:, here])).astype(BF16)
            dv_s[...] += dot(prob.astype(BF16), dc_s[here, :])
            dk_s[...] += dot(d_score, q_s[here, :])
            dq_s[:, here] += dot(qkvt[HD : 2 * HD, pl.ds(start, blk)], d_score)
            return inner

        begin = jnp.where(start < prefix, 0, j)
        middle = jnp.where(start + blk <= prefix, begin, j + 1)
        lax.fori_loop(begin, middle, functools.partial(step, True), 0)
        lax.fori_loop(middle, count, functools.partial(step, False), 0)
        d_key = jnp.transpose(dk_s[...] * 0.125).astype(BF16)
        d_value = jnp.transpose(dv_s[...]).astype(BF16)
        dall[HD : 2 * HD, pl.ds(start, blk)] = d_key
        dall[2 * HD :, pl.ds(start, blk)] = d_value
        for r in range(blk // rows):
            at = j * (blk // rows) + r
            dchunk[at, HD : 2 * HD, :] = d_key[:, r * rows : (r + 1) * rows]
            dchunk[at, 2 * HD :, :] = d_value[:, r * rows : (r + 1) * rows]
        return carry

    lax.fori_loop(0, count, one_key, 0)
    for i in range(count):
        sl = slice(i * blk, (i + 1) * blk)
        d_query = (dq_s[:, sl] * 0.125).astype(BF16)
        dall[:HD, sl] = d_query
        for r in range(blk // rows):
            dchunk[i * (blk // rows) + r, :HD, :] = d_query[:, r * rows : (r + 1) * rows]


def vmem(count):
    return [pl.BlockSpec(memory_space=pltpu.VMEM)] * count


SMEM_SPEC = pl.BlockSpec(memory_space=pltpu.SMEM)


def attend_forward(scal, zc, xc, yc, xya, xyb, w, heads):
    outer, rows, width = zc.shape
    seq = 4 * outer
    length = seq * rows
    return pl.pallas_call(
        functools.partial(forward_kernel, outer, heads),
        out_shape=(
            jax.ShapeDtypeStruct((length, width), BF16),
            jax.ShapeDtypeStruct((3 * HD, length), BF16),
            jax.ShapeDtypeStruct((seq, HD, rows), BF16),
            jax.ShapeDtypeStruct((HD, length), F32),
            jax.ShapeDtypeStruct((1, length), F32),
        ),
        in_specs=[SMEM_SPEC] + vmem(6),
        out_specs=tuple(vmem(5)),
        scratch_shapes=[pltpu.VMEM((3 * HD, width), BF16), pltpu.VMEM((length, HD), BF16)],
        compiler_params=pltpu.CompilerParams(vmem_limit_bytes=40 << 20),
        cost_estimate=pl.CostEstimate(
            flops=2 * length * width * 3 * HD + 4 * length * length * HD,
            bytes_accessed=6 * length * width,
            transcendentals=length * length,
        ),
    )(scal, zc, xc, yc, xya, xyb, w)


def attend_backward(scal, qkvt, dcr, ctxt, lse):
    seq, _, rows = dcr.shape
    length = seq * rows
    blk = split(length)
    return pl.pallas_call(
        backward_kernel,
        out_shape=(
            jax.ShapeDtypeStruct((seq, 3 * HD, rows), BF16),
            jax.ShapeDtypeStruct((3 * HD, length), BF16),
        ),
        in_specs=[SMEM_SPEC] + vmem(4),
        out_specs=tuple(vmem(2)),
        scratch_shapes=[
            pltpu.VMEM((length, HD), BF16),
            pltpu.VMEM((length, HD), BF16),
            pltpu.VMEM((length, HD), BF16),
            pltpu.VMEM((length, HD), BF16),
            pltpu.VMEM((HD, length), BF16),
            pltpu.VMEM((1, length), F32),
            pltpu.VMEM((HD, length), F32),
            pltpu.VMEM((blk, HD), F32),
            pltpu.VMEM((blk, HD), F32),
        ],
        compiler_params=pltpu.CompilerParams(vmem_limit_bytes=40 << 20),
        cost_estimate=pl.CostEstimate(
            flops=10 * length * length * HD,
            bytes_accessed=16 * length * HD,
            transcendentals=length * length,
        ),
    )(scal, qkvt, dcr, ctxt, lse)


def body(
    tokens, cotangent, prefix_len, gain_one, shift_one, w_query, b_query, w_key, w_value, b_value,
    w_output, b_output, gain_two, shift_two, w_up, b_up, w_down, b_down,
):
    outer, pairs = (lax.axis_size("zo"), lax.axis_size("bo"))
    seq, batch = (4 * outer, 2 * pairs)
    zi, yi, xi, ci = (lax.axis_index(a) for a in ("zo", "y", "x", "bi"))
    si = lax.axis_index(SEQ)
    token, d_out = (tokens[0], cotangent[0])
    rows, width = token.shape
    heads = width // HD
    cut = w_query.shape[0]
    wide_cut = w_down.shape[0]
    hidden_width = w_up.shape[1]
    local_width = hidden_width // 4

    zc = jnp.stack([token] + [swap(token, "zo", k) for k in range(1, outer)])
    xc = swap(zc, "x")
    yc = swap(zc, "y")
    xya = swap(xc[: outer // 2], "y")
    xyb = swap(yc[outer // 2 :], "x")

    vectors = jnp.stack(
        [gain_one, shift_one, b_query, b_value, b_output, gain_two, shift_two, b_down], axis=1
    )
    vectors = jnp.concatenate([vectors, b_up.reshape(4, cut).T], axis=1)
    vectors = jnp.pad(vectors, ((0, 0), (0, HD - NVEC)))
    by_head = jnp.concatenate(
        [w.reshape(cut, heads, HD) for w in (w_query, w_key, w_value)], axis=2
    ).transpose(1, 0, 2)
    by_head = jnp.pad(by_head, ((0, seq - heads), (0, 0), (0, 0)))
    send = jnp.concatenate(
        [by_head, jnp.broadcast_to(vectors[None], (seq, cut, HD))], axis=2
    )
    head_w = lax.all_to_all(send, SEQ, split_axis=0, concat_axis=0, tiled=True)
    head_w = lax.all_gather(head_w, BAT, axis=0, tiled=False)
    head_w = head_w.transpose(1, 0, 2, 3).reshape(width, WIDE)
    full = head_w[:, 3 * HD : 3 * HD + NVEC].astype(F32).T
    gain_one_f, shift_one_f, _, _, b_out_f, gain_two_f, shift_two_f, b_down_f = (
        full[i : i + 1] for i in range(8)
    )
    up = head_w[:, 3 * HD + 8 : 3 * HD + NVEC].reshape(outer, 2, 2, pairs, 2, cut, 4)
    up = pick(pick(up, xi, 2), ci, 3)
    b_up_t = up.transpose(0, 1, 2, 4, 3).reshape(1, local_width).astype(F32)

    up_send = (
        w_up.reshape(cut, outer, 2, 2, pairs, 2, wide_cut)
        .transpose(3, 5, 0, 1, 2, 4, 6)
        .reshape(4, cut, local_width)
    )
    up_part = lax.all_to_all(up_send, TP, split_axis=0, concat_axis=0, tiled=True)
    ff = jnp.concatenate([w_down, up_part.reshape(4 * cut, local_width)])
    ff = jnp.stack([ff] + [swap(ff, "zo", k) for k in range(1, outer)])
    ff = jnp.stack([ff, swap(ff, "y")])
    ff = jnp.stack(
        [
            pick(pick(ff, jnp.bitwise_xor(yi, b), 0), jnp.bitwise_xor(zi, a), 0)
            for a in range(outer)
            for b in range(2)
        ]
    )
    if pairs > 1:
        ff = lax.all_gather(ff, "bo", axis=1)
    ff = ff.reshape(2 * outer, pairs, wide_cut + 4 * cut, width)
    down_t = ff[:, :, :wide_cut].reshape(local_width, width)
    up_t = (
        ff[:, :, wide_cut:]
        .reshape(2 * outer, pairs, 2, 2, cut, local_width)
        .transpose(0, 2, 1, 3, 4, 5)
        .reshape(width, local_width)
    )

    square = lax.all_gather(
        jnp.concatenate([w_query, w_key, w_value, w_output]), ALL, axis=0, tiled=False
    )
    square = square.reshape(-1, 4, cut, width).transpose(1, 0, 2, 3).reshape(4, width, width)
    w_out_f = square[3]

    def group(value):
        both = jnp.stack([value, swap(value, "x")])
        return jnp.stack([both, swap(both, "bi")]).reshape(4 * rows, width)

    d_out_t = group(d_out)

    scal = jnp.stack([si, prefix_len[0]]).astype(jnp.int32)
    norm_one, qkvt, ctxc, ctxt, lse = attend_forward(scal, zc, xc, yc, xya, xyb, head_w, heads)
    ctx = lax.all_to_all(ctxc, SEQ, split_axis=0, concat_axis=0, tiled=True)
    ctx = ctx[:heads].reshape(width, rows)
    middle = token.astype(F32) + dot(ctx, w_out_f, TN) + b_out_f
    normed_two, factor_two = normalize(middle)
    norm_two = (normed_two * gain_two_f + shift_two_f).astype(BF16)
    norm_two_t = group(norm_two)

    pre_act = dot(norm_two_t, up_t) + b_up_t
    cdf = 0.5 * (1.0 + lax.erf(pre_act * 0.7071067811865476))
    act = (pre_act * cdf).astype(BF16)
    slope = cdf + pre_act * jnp.exp(-0.5 * pre_act * pre_act) * 0.3989422804014327
    d_pre = (dot(d_out_t, down_t, NT) * slope).astype(BF16)

    def ungroup(value):
        value = value.reshape(2, 2, rows, width)
        value = value[0] + swap(value[1].astype(BF16), "bi").astype(F32)
        return value[0] + swap(value[1].astype(BF16), "x").astype(F32)

    d_norm_two = ungroup(dot(d_pre, up_t, NT))
    d_mid_norm, grad_gain_two, grad_shift_two = norm_backward(
        d_norm_two, normed_two, factor_two, gain_two_f
    )
    d_middle = d_out.astype(F32) + d_mid_norm
    d_branch = d_middle.astype(BF16)
    d_ctx = dot(w_out_f, d_branch, NT).astype(BF16).reshape(heads, HD, rows)
    d_ctx = jnp.pad(d_ctx, ((0, seq - heads), (0, 0), (0, 0)))
    d_ctx = lax.all_to_all(d_ctx, SEQ, split_axis=0, concat_axis=0, tiled=True)

    layer_out = (middle + ungroup(dot(act, down_t)) + b_down_f).astype(BF16)

    grad_down = dot(act, d_out_t, TN).reshape(outer, 2, pairs, wide_cut, width)
    grad_up = dot(norm_two_t, d_pre, TN)
    grad_up = (
        grad_up.reshape(2 * outer, 2, pairs, 2, cut, local_width)
        .transpose(0, 2, 1, 3, 4, 5)
        .reshape(outer, 2, pairs, 4 * cut, local_width)
    )
    grad_b_up = jnp.sum(d_pre.astype(F32), axis=0)
    grad_out = dot(ctx, d_branch).reshape(outer, 2, 2, pairs, 2, cut, width)
    grad_out = pick(grad_out, ci, 4) + swap(
        pick(grad_out, 1 - ci, 4).astype(BF16), "bi"
    ).astype(F32)
    grad_out = pick(grad_out, xi, 2) + swap(
        pick(grad_out, 1 - xi, 2).astype(BF16), "x"
    ).astype(F32)
    grads = jnp.concatenate([grad_down, grad_up, grad_out], axis=3)
    if pairs > 1:
        grads = lax.psum_scatter(grads, "bo", scatter_dimension=2, tiled=True)
    grads = grads.reshape(outer, 2, wide_cut + 5 * cut, width)
    grads = pick(grads, yi, 1) + swap(pick(grads, 1 - yi, 1).astype(BF16), "y").astype(F32)
    total = pick(grads, zi, 0)
    for k in range(1, outer):
        away = pick(grads, jnp.bitwise_xor(zi, k), 0).astype(BF16)
        total = total + swap(away, "zo", k).astype(F32)
    grad_w_down = total[:wide_cut]
    grad_w_output = total[wide_cut + 4 * cut :]
    up_back = total[wide_cut : wide_cut + 4 * cut].astype(BF16).reshape(4, cut, local_width)
    up_back = lax.all_to_all(up_back, TP, split_axis=0, concat_axis=0, tiled=True)
    grad_w_up = (
        up_back.reshape(2, 2, cut, outer, 2, pairs, wide_cut)
        .transpose(2, 3, 4, 0, 5, 1, 6)
        .reshape(cut, hidden_width)
        .astype(F32)
    )

    dchunk, dall = attend_backward(scal, qkvt, d_ctx, ctxt, lse)
    d_rows = lax.all_to_all(dchunk, SEQ, split_axis=0, concat_axis=0, tiled=True)
    d_rows = d_rows[:heads].reshape(heads, 3, HD, rows).transpose(1, 0, 2, 3)
    d_rows = d_rows.reshape(3, width, rows)
    grad_head = dot(dall, norm_one)
    grad_b_qv = jnp.sum(d_rows.astype(F32), axis=2)
    d_norm_one = sum(dot(d_rows[i], square[i], ((0,), (1,))) for i in range(3))
    normed_one, factor_one = normalize(token.astype(F32))
    d_in_norm, grad_gain_one, grad_shift_one = norm_backward(
        d_norm_one, normed_one, factor_one, gain_one_f
    )
    grad_tokens = d_middle + d_in_norm

    mine = (
        (jnp.arange(2, dtype=jnp.int32)[:, None] == xi)
        & (jnp.arange(2, dtype=jnp.int32)[None, :] == ci)
    ).astype(F32)
    b_up_cols = grad_b_up.reshape(outer, 2, 1, pairs, 1, 4, cut).transpose(0, 1, 2, 3, 4, 6, 5)
    b_up_cols = b_up_cols * mine[None, None, :, None, :, None, None]
    vec_cols = jnp.stack(
        [
            grad_gain_one,
            grad_shift_one,
            grad_b_qv[0],
            grad_b_qv[2],
            jnp.sum(d_branch.astype(F32), axis=0),
            grad_gain_two,
            grad_shift_two,
            jnp.sum(d_out.astype(F32), axis=0),
        ],
        axis=1,
    )
    vec_cols = jnp.concatenate([vec_cols, b_up_cols.reshape(width, 4)], axis=1)
    vec_cols = jnp.pad(vec_cols, ((0, 0), (0, HD - NVEC)))
    last = jnp.concatenate([grad_head.T, vec_cols], axis=1).reshape(seq, batch, cut, WIDE)
    if pairs > 1:
        last = lax.psum_scatter(last, BAT, scatter_dimension=1, tiled=True)[:, 0]
    else:
        last = pick(last, ci, 1) + swap(pick(last, 1 - ci, 1).astype(BF16), "bi").astype(F32)
    last = lax.all_to_all(last.astype(BF16), SEQ, split_axis=0, concat_axis=0, tiled=True)
    last = last.astype(F32)
    grad_qkv = last[:heads, :, : 3 * HD].reshape(heads, cut, 3, HD).transpose(2, 1, 0, 3)
    grad_qkv = grad_qkv.reshape(3, cut, width)
    vec = jnp.sum(last[:, :, 3 * HD : 3 * HD + NVEC], axis=0)
    vec_of = [vec[:, i] for i in range(8)]
    grad_bu = vec[:, 8:].T.reshape(4 * cut)
    return (
        layer_out[None],
        grad_tokens[None],
        vec_of[0],
        vec_of[1],
        grad_qkv[0],
        vec_of[2],
        grad_qkv[1],
        grad_qkv[2],
        vec_of[3],
        grad_w_output,
        vec_of[4],
        vec_of[5],
        vec_of[6],
        grad_w_up,
        grad_bu,
        grad_w_down,
        vec_of[7],
    )


def solution(mesh):
    seq, batch = (mesh.shape["seq"], mesh.shape["batch"])
    fine = Mesh(mesh.devices.reshape(seq // 4, 2, 2, batch // 2, 2), ALL)
    act, mat, vec = (P(BAT, SEQ, None), P(ALL, None), P(ALL))
    return jax.shard_map(
        body,
        mesh=fine,
        in_specs=(
            act, act, P(BAT), vec, vec, mat, vec, mat, mat, vec, mat, vec, vec, vec, mat, vec, mat, vec,
        ),
        out_specs=(
            act, act, vec, vec, mat, vec, mat, mat, vec, mat, vec, vec, vec, mat, vec, mat, vec,
        ),
        check_vma=False,
    )
```

```python
import functools

import jax
import jax.numpy as jnp
from jax import lax
from jax.experimental import pallas as pl
from jax.experimental.pallas import tpu as pltpu
from jax.sharding import Mesh
from jax.sharding import PartitionSpec as P

HD = 64
EPS = 1e-05
LOG2E = 1.4426950408889634
SEQ = ("zo", "y", "x")
BAT = ("bo", "bi")
ALL = SEQ + BAT
PLANE = ("y", "x", "bi")
WIDE = 4 * HD
F32 = jnp.float32
BF16 = jnp.bfloat16


def normalize(values):
    centre = jnp.mean(values, axis=-1, keepdims=True)
    centred = values - centre
    spread = jnp.mean(centred * centred, axis=-1, keepdims=True)
    factor = lax.rsqrt(spread + EPS)
    return (centred * factor, factor)


def norm_backward(grad_out, normed, factor, gain):
    grad_gain = jnp.sum(grad_out * normed, axis=0, keepdims=True)
    grad_shift = jnp.sum(grad_out, axis=0, keepdims=True)
    scaled = grad_out * gain
    grad_in = factor * (
        scaled
        - jnp.mean(scaled, axis=-1, keepdims=True)
        - normed * jnp.mean(scaled * normed, axis=-1, keepdims=True)
    )
    return (grad_in, grad_gain, grad_shift)


def dot(left, right, dims=((1,), (0,))):
    return lax.dot_general(left, right, (dims, ((), ())), preferred_element_type=F32)


NN = ((1,), (0,))
NT = ((1,), (1,))
TN = ((0,), (0,))


def swap(value, axis, step=1):
    size = lax.axis_size(axis)
    return lax.ppermute(value, axis, [(i, i ^ step) for i in range(size)])


def swap_plane(value, step):
    return lax.ppermute(value, ("y", "x"), [(i, i ^ step) for i in range(4)])


def after(value, *others):
    return lax.optimization_barrier((value,) + others)[0]


def pick(value, index, axis):
    return lax.dynamic_index_in_dim(value, index, axis, keepdims=False)


def split(length):
    return 512 if length % 512 == 0 else length


def assemble(parts, out):
    seq, cut = (parts.shape[1], parts.shape[2])
    for b in range(2):
        for i in range(seq):
            at = (2 * i + b) * cut
            out[at : at + cut, :] = parts[b, i].astype(F32)


def forward_kernel(
    outer, heads, scal, zc, xc, yc, xya, xyb, w, n1_out, n0_out, qkvt, ctxc, ctxt, lse, rows_out,
    w_head, *rest,
):
    place, prefix = (scal[0], scal[1])
    if w.ndim == 4:
        w_out, n1, n0, wt_s, k_s, sems = rest
        assemble(w, w_head)
    else:
        w_out, (n1, n0, wt_s, k_s, sems) = (None, rest)
        w_head[...] = w[...].astype(F32)
    rows = n1.shape[0] // (4 * outer)
    length = n1.shape[0]
    blk = split(length)
    turned = jnp.transpose(w_head[...])
    wt_s[...] = turned[: 3 * HD].astype(BF16)
    rows_in = turned[3 * HD : 3 * HD + 8]
    rows_out[...] = rows_in
    gain = rows_in[0:1]
    shift = rows_in[1:2]
    if w_out is not None:
        for src, first, low in ((zc, 0, 0), (xc, 0, 1), (yc, 0, 2), (xya, 0, 3), (xyb, outer // 2, 3)):
            for k in range(src.shape[0]):
                w_out[(first + k) * 4 + low] = src[k, rows:, :]

    def norm_piece(src, first, low):
        def one(k, carry):
            value = src[k, :rows, :].astype(F32)
            normed, _ = normalize(value)
            at = jnp.bitwise_xor(place, (first + k) * 4 + low) * rows
            here = pl.ds(pl.multiple_of(at, rows), rows)
            n0[here, :] = normed.astype(BF16)
            n1[here, :] = (normed * gain + shift).astype(BF16)
            return carry

        lax.fori_loop(0, src.shape[0], one, 0)

    norm_piece(zc, 0, 0)
    norm_piece(xc, 0, 1)
    norm_piece(yc, 0, 2)
    norm_piece(xya, 0, 3)
    norm_piece(xyb, outer // 2, 3)
    copies = (
        pltpu.make_async_copy(n1, n1_out, sems.at[0]),
        pltpu.make_async_copy(n0, n0_out, sems.at[1]),
    )
    for copy in copies:
        copy.start()
    head = jnp.minimum(place, heads - 1)
    at = pl.multiple_of(head * HD, HD)
    bias_q = w_head[pl.ds(at, HD), 3 * HD + 2 : 3 * HD + 3]
    bias_v = w_head[pl.ds(at, HD), 3 * HD + 3 : 3 * HD + 4]
    for i in range(length // blk):
        part = dot(wt_s[...], n1[i * blk : (i + 1) * blk, :], NT)
        q_part = (part[:HD] + bias_q).astype(BF16)
        k_part = part[HD : 2 * HD].astype(BF16)
        v_part = (part[2 * HD :] + bias_v).astype(BF16)
        qkvt[:HD, i * blk : (i + 1) * blk] = q_part
        qkvt[HD : 2 * HD, i * blk : (i + 1) * blk] = k_part
        qkvt[2 * HD :, i * blk : (i + 1) * blk] = v_part
        k_s[i * blk : (i + 1) * blk, :] = jnp.transpose(k_part.astype(F32)).astype(BF16)
    scale = 0.125 * LOG2E

    def one_query(i, carry):
        first = pl.multiple_of(i * blk, blk)
        q_now = qkvt[:HD, pl.ds(first, blk)]

        def step(masked, j, state):
            top, total, acc = state
            start = pl.multiple_of(j * blk, blk)
            scores = dot(k_s[pl.ds(start, blk), :], q_now) * scale
            if masked:
                key = start + lax.broadcasted_iota(jnp.int32, (blk, blk), 0)
                query = first + lax.broadcasted_iota(jnp.int32, (blk, blk), 1)
                scores = jnp.where((key <= query) | (key < prefix), scores, -1e30)
            new_top = jnp.maximum(top, jnp.max(scores, axis=0, keepdims=True))
            prob = jnp.exp2(scores - new_top)
            fade = jnp.exp2(top - new_top)
            total = total * fade + jnp.sum(prob, axis=0, keepdims=True)
            acc = acc * fade + dot(qkvt[2 * HD :, pl.ds(start, blk)], prob.astype(BF16))
            return (new_top, total, acc)

        state = (
            jnp.full((1, blk), -1e30, F32),
            jnp.zeros((1, blk), F32),
            jnp.zeros((HD, blk), F32),
        )
        full = jnp.maximum(prefix // blk, i)
        needed = jnp.maximum((prefix + blk - 1) // blk, i + 1)
        state = lax.fori_loop(0, full, functools.partial(step, False), state)
        top, total, acc = lax.fori_loop(full, needed, functools.partial(step, True), state)
        out = acc / total
        ctxt[:, pl.ds(first, blk)] = out
        lse[:, pl.ds(first, blk)] = top + jnp.log2(total)
        for r in range(blk // rows):
            ctxc[i * (blk // rows) + r] = out[:, r * rows : (r + 1) * rows].astype(BF16)
        return carry

    lax.fori_loop(0, length // blk, one_query, 0)
    for copy in copies:
        copy.wait()


def backward_kernel(
    scal, qkvt, dcr, ctxt, lse, dchunk, dall, q_s, k_s, v_s, dc_s, dct_s, del_s, dq_s, dk_s, dv_s
):
    prefix = scal[1]
    rows = dcr.shape[2]
    length = qkvt.shape[1]
    blk = split(length)
    count = length // blk
    for i in range(count):
        sl = slice(i * blk, (i + 1) * blk)
        turned = jnp.transpose(qkvt[:, sl].astype(F32)).astype(BF16)
        q_s[sl, :] = turned[:, :HD]
        k_s[sl, :] = turned[:, HD : 2 * HD]
        v_s[sl, :] = turned[:, 2 * HD :]
    for i in range(length // rows):
        sl = slice(i * rows, (i + 1) * rows)
        dct_s[:, sl] = dcr[i]
        dc_s[sl, :] = jnp.transpose(dcr[i].astype(F32)).astype(BF16)
    del_s[...] = jnp.sum(dct_s[...].astype(F32) * ctxt[...], axis=0, keepdims=True)
    dq_s[...] = jnp.zeros_like(dq_s)
    scale = 0.125 * LOG2E

    def one_key(j, carry):
        start = pl.multiple_of(j * blk, blk)
        dk_s[...] = jnp.zeros_like(dk_s)
        dv_s[...] = jnp.zeros_like(dv_s)

        def step(masked, i, inner):
            first = pl.multiple_of(i * blk, blk)
            here = pl.ds(first, blk)
            scores = dot(k_s[pl.ds(start, blk), :], qkvt[:HD, here]) * scale
            prob = jnp.exp2(scores - lse[:, here])
            if masked:
                key = start + lax.broadcasted_iota(jnp.int32, (blk, blk), 0)
                query = first + lax.broadcasted_iota(jnp.int32, (blk, blk), 1)
                prob = jnp.where((key <= query) | (key < prefix), prob, 0.0)
            d_prob = dot(v_s[pl.ds(start, blk), :], dct_s[:, here])
            d_score = (prob * (d_prob - del_s[:, here])).astype(BF16)
            dv_s[...] += dot(prob.astype(BF16), dc_s[here, :])
            dk_s[...] += dot(d_score, q_s[here, :])
            dq_s[:, here] += dot(qkvt[HD : 2 * HD, pl.ds(start, blk)], d_score)
            return inner

        begin = jnp.where(start < prefix, 0, j)
        middle = jnp.where(start + blk <= prefix, begin, j + 1)
        lax.fori_loop(begin, middle, functools.partial(step, True), 0)
        lax.fori_loop(middle, count, functools.partial(step, False), 0)
        d_key = jnp.transpose(dk_s[...] * 0.125).astype(BF16)
        d_value = jnp.transpose(dv_s[...]).astype(BF16)
        dall[HD : 2 * HD, pl.ds(start, blk)] = d_key
        dall[2 * HD :, pl.ds(start, blk)] = d_value
        for r in range(blk // rows):
            at = j * (blk // rows) + r
            dchunk[at, HD : 2 * HD, :] = d_key[:, r * rows : (r + 1) * rows]
            dchunk[at, 2 * HD :, :] = d_value[:, r * rows : (r + 1) * rows]
        return carry

    lax.fori_loop(0, count, one_key, 0)
    for i in range(count):
        sl = slice(i * blk, (i + 1) * blk)
        d_query = (dq_s[:, sl] * 0.125).astype(BF16)
        dall[:HD, sl] = d_query
        for r in range(blk // rows):
            dchunk[i * (blk // rows) + r, :HD, :] = d_query[:, r * rows : (r + 1) * rows]


def gather_rows(pieces, out):
    rows = pieces[0].shape[0]
    for i, piece in enumerate(pieces):
        out[i * rows : (i + 1) * rows, :] = piece[...]


def feed_kernel(packed, *refs):
    scal, n2_a, n2_b, n2_c, n2_d, dy_a, dy_b, dy_c, dy_d = refs[:9]
    if packed:
        ffz, ffc, w_own = refs[9:12]
        outs, (n2, dy, down, up, bias) = (refs[12:-5], refs[-5:])
        outs, w_qkv = (outs[:-1], outs[-1])
        zi, ci = (scal[0], scal[1])
        outer = ffz.shape[0]
        cut = (ffz.shape[1] - 8) // 8
        half = 4 * cut
        rows = []
        for src, flip in ((ffz, 0), (ffc, 1)):
            for k in range(outer):
                at = jnp.bitwise_xor(zi, k) * 2 + jnp.bitwise_xor(ci, flip)
                here = pl.ds(pl.multiple_of(at * half, half), half)
                down[here, :] = src[k, :half, :]
                up[here, :] = src[k, half : 2 * half, :]
                rows.append((at, src[k, 2 * half : 2 * half + 8, :half].astype(F32)[:1]))
        for d, src in enumerate((None, dy_b, dy_c, dy_d)):
            for k in range(outer):
                if src is None:
                    w_qkv[k * 4] = w_own[k]
                else:
                    w_qkv[k * 4 + d] = src[k * 3 * cut : (k + 1) * 3 * cut, :]
        behind = 3 * cut * outer
        for q in range(2 * outer):
            bias[:, q * half : (q + 1) * half] = sum(
                jnp.where(at == q, row, 0.0) for at, row in rows
            )
    else:
        down, up, bias = refs[9:12]
        outs, (n2, dy) = (refs[12:-2], refs[-2:])
        behind = 0
    gather_rows((n2_a, n2_b, n2_c, n2_d), n2)
    rows = n2_a.shape[0]
    dy[:rows, :] = dy_a[...]
    for d, src in enumerate((dy_b, dy_c, dy_d)):
        dy[(d + 1) * rows : (d + 2) * rows, :] = src[behind:, :]
    act, d_pre, out_keep, out_b, out_c, out_d, dn_keep, dn_b, dn_c, dn_d = outs
    width = down.shape[0]
    tile = 256
    for c in range(width // tile):
        sl = slice(c * tile, (c + 1) * tile)
        pre = dot(n2[...], up[:, sl]) + bias[:, sl]
        cdf = 0.5 * (1.0 + lax.erf(pre * 0.7071067811865476))
        act[:, sl] = (pre * cdf).astype(BF16)
        slope = cdf + pre * jnp.exp(-0.5 * pre * pre) * 0.3989422804014327
        d_pre[:, sl] = (dot(dy[...], down[sl, :], NT) * slope).astype(BF16)
    back = dot(d_pre[...], up[...], NT)
    for i, ref in enumerate((dn_keep, dn_b, dn_c, dn_d)):
        ref[...] = back[i * rows : (i + 1) * rows].astype(ref.dtype)
    out = dot(act[...], down[...])
    for i, ref in enumerate((out_keep, out_b, out_c, out_d)):
        ref[...] = out[i * rows : (i + 1) * rows].astype(ref.dtype)


def feed_forward(scal, n2, dy, weights, local):
    rows, width = n2[0].shape
    packed = weights[0].ndim == 3
    wide = [pltpu.VMEM((4 * rows, width), BF16)] * 2
    if packed:
        wide = wide + [
            pltpu.VMEM((local, width), BF16),
            pltpu.VMEM((width, local), BF16),
            pltpu.VMEM((1, local), F32),
        ]
    more = []
    if packed:
        outer = weights[0].shape[0]
        cut = (weights[0].shape[1] - 8) // 8
        more = [jax.ShapeDtypeStruct((4 * outer, 3 * cut, width), BF16)]
    part = [jax.ShapeDtypeStruct((rows, width), F32)]
    part = part + [jax.ShapeDtypeStruct((rows, width), BF16)] * 3
    return pl.pallas_call(
        functools.partial(feed_kernel, packed),
        out_shape=tuple([jax.ShapeDtypeStruct((4 * rows, local), BF16)] * 2 + part + part + more),
        in_specs=[SMEM_SPEC] + vmem(8 + len(weights)),
        out_specs=tuple(vmem(10 + len(more))),
        scratch_shapes=wide,
        compiler_params=pltpu.CompilerParams(vmem_limit_bytes=14 << 20),
        cost_estimate=SMALL,
        name="feed",
    )(scal, *n2, *dy, *weights)


def rank_row(scal, seq, low, core, cut):
    return pl.multiple_of((2 * jnp.bitwise_xor(scal[0], low) + jnp.bitwise_xor(scal[2], core)) * cut, cut)


def stacked(own, other, first, last):
    rows = [ref[i, first:last, :].astype(F32) for ref in (own, other) for i in range(own.shape[0])]
    return jnp.concatenate(rows, axis=0).astype(BF16)


def middle_kernel(heads, scal, ctx, own, other, token, rows_in, middle, norm_two, plain, moved):
    seq, cut, _ = own.shape
    plain[...] = ctx[:heads].reshape(plain.shape).astype(F32)
    for b in range(2):
        for i in range(seq):
            at = (b * seq + i) * cut
            moved[at : at + cut, :] = plain[pl.ds(rank_row(scal, seq, i, b, cut), cut), :]
    turned = jnp.transpose(moved[...]).astype(BF16)
    product = dot(turned, stacked(own, other, 0, cut))
    value = token[...].astype(F32) + product + rows_in[4:5, :]
    middle[...] = value
    normed, _ = normalize(value)
    norm_two[...] = (normed * rows_in[5:6, :] + rows_in[6:7, :]).astype(BF16)


def attend_output(scal, ctx, own, other, token, rows_in, heads):
    rows, width = token.shape
    return pl.pallas_call(
        functools.partial(middle_kernel, heads),
        out_shape=(
            jax.ShapeDtypeStruct((rows, width), F32),
            jax.ShapeDtypeStruct((rows, width), BF16),
        ),
        in_specs=[SMEM_SPEC] + vmem(5),
        out_specs=tuple(vmem(2)),
        scratch_shapes=[pltpu.VMEM((width, rows), F32)] * 2,
        compiler_params=pltpu.CompilerParams(vmem_limit_bytes=8 << 20),
        cost_estimate=SMALL,
        name="middle",
    )(scal, ctx, own, other, token, rows_in)


def turn_math(keep, got, middle, d_out, rows_in):
    d_norm = keep + (got[0].astype(F32) + got[1].astype(F32)) + got[2].astype(F32)
    normed, factor = normalize(middle)
    grad_in, grad_gain, grad_shift = norm_backward(d_norm, normed, factor, rows_in[5:6])
    grad_up = d_out.astype(F32)
    total = grad_up + grad_in
    low = total.astype(BF16)
    sums = (
        jnp.sum(low.astype(F32), axis=0, keepdims=True),
        grad_gain,
        grad_shift,
        jnp.sum(grad_up, axis=0, keepdims=True),
        jnp.zeros((4, total.shape[1]), F32),
    )
    return (total, low, jnp.concatenate(sums, axis=0))


def turn_kernel(
    heads, scal, keep, got_b, got_c, got_d, middle, d_out, own, other, rows_in,
    d_middle, d_branch, d_ctx, sums, plain,
):
    got = (got_b[...], got_c[...], got_d[...])
    d_middle[...], low, sums[...] = turn_math(keep[...], got, middle[...], d_out[...], rows_in[...])
    d_branch[...] = low
    seq, cut, _ = own.shape
    back = dot(stacked(own, other, 0, cut), low, NT)
    for b in range(2):
        for i in range(seq):
            at = (b * seq + i) * cut
            plain[pl.ds(rank_row(scal, seq, i, b, cut), cut), :] = back[at : at + cut]
    rows = d_ctx.shape[2]
    d_ctx[:heads] = plain[...].astype(BF16).reshape(heads, HD, rows)
    d_ctx[heads:] = jnp.zeros((seq - heads, HD, rows), BF16)


def turn_back(scal, keep, got, middle, d_out, own, other, rows_in, heads, seq):
    rows, width = middle.shape
    return pl.pallas_call(
        functools.partial(turn_kernel, heads),
        out_shape=(
            jax.ShapeDtypeStruct((rows, width), F32),
            jax.ShapeDtypeStruct((rows, width), BF16),
            jax.ShapeDtypeStruct((seq, HD, rows), BF16),
            jax.ShapeDtypeStruct((8, width), F32),
        ),
        in_specs=[SMEM_SPEC] + vmem(9),
        out_specs=tuple(vmem(4)),
        scratch_shapes=[pltpu.VMEM((width, rows), F32)],
        compiler_params=pltpu.CompilerParams(vmem_limit_bytes=8 << 20),
        cost_estimate=SMALL,
        name="turn",
    )(scal, keep, *got, middle, d_out, own, other, rows_in)


def last_kernel(heads, scal, d_rows, own, other, token, d_middle, rows_in, grad_tokens, plain):
    seq, cut = (own.shape[0], own.shape[1] // 3)
    total = 0.0
    for i in range(3):
        part = jnp.concatenate(
            [d_rows[h, i * HD : (i + 1) * HD, :].astype(F32) for h in range(heads)], axis=0
        )
        total = total + dot(stacked(own, other, i * cut, (i + 1) * cut), part.astype(BF16))
    for b in range(2):
        for i in range(seq):
            at = (b * seq + i) * cut
            plain[pl.ds(rank_row(scal, seq, i, b, cut), cut), :] = total[at : at + cut]
    normed, factor = normalize(token[...].astype(F32))
    grad_in, _, _ = norm_backward(jnp.transpose(plain[...]), normed, factor, rows_in[0:1, :])
    grad_tokens[...] = d_middle[...] + grad_in


def input_grad(scal, d_rows, own, other, token, d_middle, rows_in, heads):
    rows, width = token.shape
    return pl.pallas_call(
        functools.partial(last_kernel, heads),
        out_shape=jax.ShapeDtypeStruct((rows, width), F32),
        in_specs=[SMEM_SPEC] + vmem(6),
        out_specs=vmem(1)[0],
        scratch_shapes=[pltpu.VMEM((width, rows), F32)],
        compiler_params=pltpu.CompilerParams(vmem_limit_bytes=12 << 20),
        cost_estimate=SMALL,
        name="last",
    )(scal, d_rows, own, other, token, d_middle, rows_in)


def grads_kernel(
    scal, act, d_pre, n2_a, n2_b, n2_c, n2_d, dy_a, dy_b, dy_c, dy_d, send, keep, n2, dy, down_s, up_s
):
    zi, ci = (scal[0], scal[1])
    outer, rows, width = keep.shape
    half = (rows - 8) // 2
    gather_rows((n2_a, n2_b, n2_c, n2_d), n2)
    count = dy_a.shape[0]
    dy[:count, :] = dy_a[...]
    for d, src in enumerate((dy_b, dy_c, dy_d)):
        dy[(d + 1) * count : (d + 2) * count, :] = src[src.shape[0] - count :, :]
    down_s[...] = dot(act[...], dy[...], TN)
    up_s[...] = dot(n2[...], d_pre[...], TN)
    bias = jnp.sum(d_pre[...].astype(F32), axis=0, keepdims=True)
    for k in range(outer):
        for flip, out in ((0, keep), (1, send)):
            at = jnp.bitwise_xor(zi, k) * 2 + jnp.bitwise_xor(ci, flip)
            here = pl.ds(pl.multiple_of(at * half, half), half)
            out[k, :half, :] = down_s[here, :].astype(out.dtype)
            out[k, half : 2 * half, :] = up_s[here, :].astype(out.dtype)
            part = sum(
                jnp.where(at == q, bias[:, q * half : (q + 1) * half], 0.0)
                for q in range(2 * outer)
            )
            part = jnp.concatenate([part, jnp.zeros((1, width - half), F32)], axis=1)
            out[k, 2 * half :, :] = jnp.broadcast_to(part, (8, width)).astype(out.dtype)


def feed_grads(scal, act, d_pre, n2, dy, outer, half):
    rows, width = n2[0].shape
    local = act.shape[1]
    return pl.pallas_call(
        grads_kernel,
        out_shape=(
            jax.ShapeDtypeStruct((outer, 2 * half + 8, width), BF16),
            jax.ShapeDtypeStruct((outer, 2 * half + 8, width), F32),
        ),
        in_specs=[SMEM_SPEC] + vmem(10),
        out_specs=tuple(vmem(2)),
        scratch_shapes=[
            pltpu.VMEM((4 * rows, width), BF16),
            pltpu.VMEM((4 * rows, width), BF16),
            pltpu.VMEM((local, width), F32),
            pltpu.VMEM((width, local), F32),
        ],
        compiler_params=pltpu.CompilerParams(vmem_limit_bytes=16 << 20),
        cost_estimate=SMALL,
        name="grads",
    )(scal, act, d_pre, *n2, *dy)


def fold_kernel(keep, got, own, *away):
    own[...] = keep[0] + got[0].astype(F32)
    for k, ref in enumerate(away):
        ref[...] = (keep[k + 1] + got[k + 1].astype(F32)).astype(BF16)


def fold(keep, got):
    outer, rows, width = keep.shape
    part = jax.ShapeDtypeStruct((rows, width), BF16)
    own, *away = pl.pallas_call(
        fold_kernel,
        out_shape=tuple([jax.ShapeDtypeStruct((rows, width), F32)] + [part] * (outer - 1)),
        in_specs=vmem(2),
        out_specs=tuple(vmem(outer)),
        compiler_params=pltpu.CompilerParams(vmem_limit_bytes=4 << 20),
        cost_estimate=SMALL,
        name="fold",
    )(keep, got)
    return (own, away)


def pack_kernel(outer, heads, w_up, w_q, w_k, w_v, vec, up_send, send):
    wide = up_send.shape[2] // outer
    for t in range(4):
        for z in range(outer):
            at = (z * 4 + t) * wide
            piece = w_up[:, at : at + wide]
            for b in range(2):
                up_send[t * 2 + b, :, z * wide : (z + 1) * wide] = piece
    for h in range(send.shape[0]):
        for i, w in enumerate((w_q, w_k, w_v)):
            if h < heads:
                piece = w[:, h * HD : (h + 1) * HD]
            else:
                piece = jnp.zeros((w.shape[0], HD), BF16)
            send[h, :, i * HD : (i + 1) * HD] = piece
        send[h, :, 3 * HD :] = vec[...]


def pack(w_up, w_q, w_k, w_v, vec, outer, heads):
    cut = w_up.shape[0]
    return pl.pallas_call(
        functools.partial(pack_kernel, outer, heads),
        out_shape=(
            jax.ShapeDtypeStruct((8, cut, w_up.shape[1] // 4), BF16),
            jax.ShapeDtypeStruct((4 * outer, cut, WIDE), BF16),
        ),
        in_specs=vmem(5),
        out_specs=tuple(vmem(2)),
        compiler_params=pltpu.CompilerParams(vmem_limit_bytes=4 << 20),
        cost_estimate=SMALL,
        name="pack",
    )(w_up, w_q, w_k, w_v, vec)


def unpack_up_kernel(outer, scal, got, out):
    wide = got.shape[2] // outer
    for t in range(4):
        piece = got[2 * t + scal[0]].astype(F32)
        for z in range(outer):
            at = (z * 4 + t) * wide
            out[:, at : at + wide] = piece[:, z * wide : (z + 1) * wide]


def unpack_up(scal, got, outer):
    _, cut, local = got.shape
    return pl.pallas_call(
        functools.partial(unpack_up_kernel, outer),
        out_shape=jax.ShapeDtypeStruct((cut, 4 * local), F32),
        in_specs=[SMEM_SPEC] + vmem(1),
        out_specs=vmem(1)[0],
        compiler_params=pltpu.CompilerParams(vmem_limit_bytes=4 << 20),
        cost_estimate=SMALL,
        name="unpack_up",
    )(scal, got)


def heads_kernel(
    heads, batch, scal, dall, n1, n0, w_head, sums, *refs
):
    outs, (gh, gm, cs, full) = (refs[:-4], refs[-4:])
    step = pl.program_id(0)

    @pl.when(step == 0)
    def _():
        gh[...] = jnp.zeros_like(gh)
        gm[...] = jnp.zeros_like(gm)
        cs[...] = jnp.zeros_like(cs)

    gh[...] += dot(dall[...], n1[...])
    gm[...] += dot(dall[...], n0[...])
    cs[...] += dot(jnp.ones((8, dall.shape[1]), BF16), dall[...], NT)

    @pl.when(step == pl.num_programs(0) - 1)
    def _():
        place, core = (scal[0], scal[2])
        width = gh.shape[1]
        wide = w_head[:, : 3 * HD]
        turned = jnp.transpose(gm[...])
        total = cs[0:1, :]
        gain = jnp.sum(wide * turned, axis=1, keepdims=True)
        shift = jnp.sum(wide * total, axis=1, keepdims=True)
        column = jnp.transpose(cs[...])[:, 0:1]
        head_of = lax.broadcasted_iota(jnp.int32, (width, 1), 0) // HD
        b_q = jnp.where(head_of == place, jnp.concatenate([column[:HD]] * heads, axis=0), 0.0)
        b_v = jnp.where(head_of == place, jnp.concatenate([column[2 * HD :]] * heads, axis=0), 0.0)
        others = jnp.transpose(sums[...])
        pad = jnp.zeros((width, HD - 8), F32)
        vec = jnp.concatenate([gain, shift, b_q, b_v, others[:, :4], pad], axis=1)
        block = jnp.concatenate([jnp.transpose(gh[...]), vec], axis=1)
        if len(outs) == 1:
            outs[0][...] = block
        else:
            full[...] = block.reshape(full.shape)
            keep, send = outs
            for i in range(keep.shape[0]):
                keep[i] = full[i * batch + core]
                send[i] = full[i * batch + 1 - core].astype(BF16)


def head_grads(scal, dall, n1, n0, w_head, sums, heads, seq, batch):
    length, width = n1.shape
    blk = split(length)
    cut = width // (seq * batch)
    if batch == 2:
        shapes = (
            jax.ShapeDtypeStruct((seq, cut, WIDE), F32),
            jax.ShapeDtypeStruct((seq, cut, WIDE), BF16),
        )
        full = (seq * batch, cut, WIDE)
    else:
        shapes = (jax.ShapeDtypeStruct((width, WIDE), F32),)
        full = (8, WIDE)
    return pl.pallas_call(
        functools.partial(heads_kernel, heads, batch),
        out_shape=shapes,
        grid=(length // blk,),
        in_specs=[
            SMEM_SPEC,
            pl.BlockSpec((3 * HD, blk), lambda i: (0, i)),
            pl.BlockSpec((blk, width), lambda i: (i, 0)),
            pl.BlockSpec((blk, width), lambda i: (i, 0)),
            whole((width, WIDE)),
            whole((8, width)),
        ],
        out_specs=tuple(whole(shape.shape) for shape in shapes),
        scratch_shapes=[
            pltpu.VMEM((3 * HD, width), F32),
            pltpu.VMEM((3 * HD, width), F32),
            pltpu.VMEM((8, 3 * HD), F32),
            pltpu.VMEM(full, F32),
        ],
        compiler_params=pltpu.CompilerParams(vmem_limit_bytes=14 << 20),
        cost_estimate=SMALL,
        name="heads",
    )(scal, dall, n1, n0, w_head, sums)


def unpack_heads_kernel(heads, got, g_q, g_k, g_v, vec):
    for i, out in enumerate((g_q, g_k, g_v)):
        for h in range(heads):
            out[:, h * HD : (h + 1) * HD] = got[h, :, i * HD : (i + 1) * HD].astype(F32)
    total = got[0, :, 3 * HD :].astype(F32)
    for s in range(1, got.shape[0]):
        total = total + got[s, :, 3 * HD :].astype(F32)
    vec[...] = total


def unpack_heads(got, heads):
    _, cut, _ = got.shape
    mat = jax.ShapeDtypeStruct((cut, heads * HD), F32)
    return pl.pallas_call(
        functools.partial(unpack_heads_kernel, heads),
        out_shape=(mat, mat, mat, jax.ShapeDtypeStruct((cut, HD), F32)),
        in_specs=vmem(1),
        out_specs=tuple(vmem(4)),
        compiler_params=pltpu.CompilerParams(vmem_limit_bytes=4 << 20),
        cost_estimate=SMALL,
        name="unpack_heads",
    )(got)


def out_grad_kernel(heads, batch, scal, ctx, d_branch, keep, send, full):
    rows = ctx.shape[2]
    turned = ctx[:heads].reshape(heads * HD, rows)
    full[...] = dot(turned, d_branch[...]).reshape(full.shape)
    core = scal[2]
    for i in range(keep.shape[0]):
        keep[i] = full[i * batch + core]
        send[i] = full[i * batch + 1 - core].astype(BF16)


def out_grad(scal, ctx, d_branch, heads, batch):
    seq = ctx.shape[0]
    width = d_branch.shape[1]
    cut = width // (seq * batch)
    return pl.pallas_call(
        functools.partial(out_grad_kernel, heads, batch),
        out_shape=(
            jax.ShapeDtypeStruct((seq, cut, width), F32),
            jax.ShapeDtypeStruct((seq, cut, width), BF16),
        ),
        in_specs=[SMEM_SPEC] + vmem(2),
        out_specs=tuple(vmem(2)),
        scratch_shapes=[pltpu.VMEM((seq * batch, cut, width), F32)],
        compiler_params=pltpu.CompilerParams(vmem_limit_bytes=6 << 20),
        cost_estimate=SMALL,
        name="out_grad",
    )(scal, ctx, d_branch)


def plane_kernel(scal, keep, got, own, *away):
    outer = own.shape[0]
    for z in range(outer):
        for k, ref in enumerate((own,) + away):
            at = z * 4 + jnp.bitwise_xor(scal[3], k)
            ref[z] = (keep[at] + got[at].astype(F32)).astype(ref.dtype)


def plane_fold(scal, keep, got):
    seq, cut, width = keep.shape
    part = (seq // 4, cut, width)
    return pl.pallas_call(
        plane_kernel,
        out_shape=tuple([jax.ShapeDtypeStruct(part, F32)] + [jax.ShapeDtypeStruct(part, BF16)] * 3),
        in_specs=[SMEM_SPEC] + vmem(2),
        out_specs=tuple(vmem(4)),
        compiler_params=pltpu.CompilerParams(vmem_limit_bytes=4 << 20),
        cost_estimate=SMALL,
        name="plane_fold",
    )(scal, keep, got)


def line_kernel(scal, keep, got_b, got_c, got_d, own, *away):
    for k, ref in enumerate((own,) + away):
        at = jnp.bitwise_xor(scal[4], k)
        total = keep[at] + (got_b[at].astype(F32) + got_c[at].astype(F32))
        ref[...] = (total + got_d[at].astype(F32)).astype(ref.dtype)


def line_fold(scal, keep, got):
    outer, cut, width = keep.shape
    part = (cut, width)
    shapes = [jax.ShapeDtypeStruct(part, F32)] + [jax.ShapeDtypeStruct(part, BF16)] * (outer - 1)
    own, *away = pl.pallas_call(
        line_kernel,
        out_shape=tuple(shapes),
        in_specs=[SMEM_SPEC] + vmem(4),
        out_specs=tuple(vmem(outer)),
        compiler_params=pltpu.CompilerParams(vmem_limit_bytes=4 << 20),
        cost_estimate=SMALL,
        name="line_fold",
    )(scal, keep, *got)
    return (own, away)


def vmem(count):
    return [pl.BlockSpec(memory_space=pltpu.VMEM)] * count


SMALL = pl.CostEstimate(flops=1, bytes_accessed=1, transcendentals=0)
SMEM_SPEC = pl.BlockSpec(memory_space=pltpu.SMEM)


def whole(shape):
    return pl.BlockSpec(shape, lambda i: (0,) * len(shape))


def attend_forward(scal, zc, xc, yc, xya, xyb, w, heads, rows):
    outer, extra, width = zc.shape
    seq = 4 * outer
    length = seq * rows
    shapes = [
        jax.ShapeDtypeStruct((length, width), BF16),
        jax.ShapeDtypeStruct((length, width), BF16),
        jax.ShapeDtypeStruct((3 * HD, length), BF16),
        jax.ShapeDtypeStruct((seq, HD, rows), BF16),
        jax.ShapeDtypeStruct((HD, length), F32),
        jax.ShapeDtypeStruct((1, length), F32),
        jax.ShapeDtypeStruct((8, width), F32),
        jax.ShapeDtypeStruct((width, WIDE), F32),
    ]
    if extra > rows:
        shapes.append(jax.ShapeDtypeStruct((seq, extra - rows, width), BF16))
    return pl.pallas_call(
        functools.partial(forward_kernel, outer, heads),
        out_shape=tuple(shapes),
        in_specs=[SMEM_SPEC] + vmem(6),
        out_specs=tuple([pl.BlockSpec(memory_space=pl.ANY)] * 2 + vmem(len(shapes) - 2)),
        scratch_shapes=[
            pltpu.VMEM((length, width), BF16),
            pltpu.VMEM((length, width), BF16),
            pltpu.VMEM((3 * HD, width), BF16),
            pltpu.VMEM((length, HD), BF16),
            pltpu.SemaphoreType.DMA((2,)),
        ],
        compiler_params=pltpu.CompilerParams(vmem_limit_bytes=(14 << 20) + 4 * length * width),
        cost_estimate=SMALL,
        name="forward",
    )(scal, zc, xc, yc, xya, xyb, w)


def attend_backward(scal, qkvt, dcr, ctxt, lse):
    seq, _, rows = dcr.shape
    length = seq * rows
    blk = split(length)
    return pl.pallas_call(
        backward_kernel,
        out_shape=(
            jax.ShapeDtypeStruct((seq, 3 * HD, rows), BF16),
            jax.ShapeDtypeStruct((3 * HD, length), BF16),
        ),
        in_specs=[SMEM_SPEC] + vmem(4),
        out_specs=tuple(vmem(2)),
        scratch_shapes=[
            pltpu.VMEM((length, HD), BF16),
            pltpu.VMEM((length, HD), BF16),
            pltpu.VMEM((length, HD), BF16),
            pltpu.VMEM((length, HD), BF16),
            pltpu.VMEM((HD, length), BF16),
            pltpu.VMEM((1, length), F32),
            pltpu.VMEM((HD, length), F32),
            pltpu.VMEM((blk, HD), F32),
            pltpu.VMEM((blk, HD), F32),
        ],
        compiler_params=pltpu.CompilerParams(vmem_limit_bytes=12 << 20),
        cost_estimate=SMALL,
    )(scal, qkvt, dcr, ctxt, lse)


def body(
    tokens, cotangent, prefix_len, gain_one, shift_one, w_query, b_query, w_key, w_value, b_value,
    w_output, b_output, gain_two, shift_two, w_up, b_up, w_down, b_down,
):
    outer, pairs = (lax.axis_size("zo"), lax.axis_size("bo"))
    seq, batch = (4 * outer, 2 * pairs)
    zi, yi, ci = (lax.axis_index(a) for a in ("zo", "y", "bi"))
    si = lax.axis_index(SEQ)
    token, d_out = (tokens[0], cotangent[0])
    rows, width = token.shape
    heads = width // HD
    cut = w_query.shape[0]
    wide_cut = w_down.shape[0]
    hidden_width = w_up.shape[1]
    local_width = hidden_width // 4

    packed = pairs == 1

    ahead = jnp.concatenate([token, w_output]) if packed else token
    zc = jnp.stack([ahead] + [swap(ahead, "zo", k) for k in range(1, outer)])
    xc = swap(zc, "x")
    yc = swap(zc, "y")
    xya = swap(xc[: outer // 2], "y")
    xyb = swap(yc[outer // 2 :], "x")

    vectors = jnp.stack(
        [gain_one, shift_one, b_query, b_value, b_output, gain_two, shift_two, b_down], axis=1
    )
    vectors = jnp.pad(vectors, ((0, 0), (0, HD - 8)))
    if packed:
        up_send, send = pack(w_up, w_query, w_key, w_value, vectors, outer, heads)
    else:
        by_head = jnp.concatenate(
            [w.reshape(cut, heads, HD) for w in (w_query, w_key, w_value)], axis=2
        ).transpose(1, 0, 2)
        by_head = jnp.pad(by_head, ((0, seq - heads), (0, 0), (0, 0)))
        send = jnp.concatenate(
            [by_head, jnp.broadcast_to(vectors[None], (seq, cut, HD))], axis=2
        )
        up_send = w_up.reshape(cut, outer, 4, local_width // outer).transpose(2, 0, 1, 3)
        up_send = jnp.repeat(up_send.reshape(4, cut, local_width), 2, axis=0)
    head_w = lax.all_to_all(after(send, zc), SEQ, split_axis=0, concat_axis=0, tiled=True)
    up_part = lax.all_to_all(after(up_send, head_w), PLANE, split_axis=0, concat_axis=0, tiled=True)
    head_w = lax.all_gather(head_w, BAT, axis=0, tiled=False)
    if not packed:
        head_w = head_w.transpose(1, 0, 2, 3).reshape(width, WIDE)

    up_part = lax.dynamic_slice_in_dim(up_part, 4 * ci, 4, 0).reshape(4 * cut, local_width)
    b_up_row = jnp.pad(b_up[None], ((0, 7), (0, width - wide_cut)))
    ff = jnp.concatenate([w_down, up_part, b_up_row])
    ff = after(ff, xc, yc)
    ff_got = [swap(ff, "zo", k) for k in range(1, outer)]
    if packed:
        w_qkv = after(jnp.concatenate([w_query, w_key, w_value]), zc)
        w_qkv = jnp.stack([w_qkv] + [swap(w_qkv, "zo", k) for k in range(1, outer)])
        side = jnp.concatenate([w_qkv.reshape(3 * cut * outer, width), d_out])
    else:
        side = d_out
        square = jnp.concatenate([w_query, w_key, w_value, w_output], axis=1)
        square = lax.all_gather(square, ALL, axis=0, tiled=True)
    side = after(side, xya, xyb)
    d_out_t = [d_out] + [swap_plane(side, k) for k in range(1, 4)]

    def group(value):
        return [value] + [swap_plane(value, k) for k in range(1, 4)]

    flat = lax.axis_index(("y", "x"))
    scal = jnp.stack([si, prefix_len[0], ci, flat, zi]).astype(jnp.int32)
    norm_one, norm_raw, qkvt, ctxc, ctxt, lse, rows_in, head_f, *w_out_own = attend_forward(
        scal, zc, xc, yc, xya, xyb, head_w, heads, rows
    )
    b_down_f = rows_in[7:8]
    ctxc, d_out_t, ff_got = lax.optimization_barrier((ctxc, d_out_t, ff_got))
    ffz = jnp.stack([ff] + ff_got)
    ctx = lax.all_to_all(ctxc, SEQ, split_axis=0, concat_axis=0, tiled=True)
    ffc = swap(ffz, "bi")
    if pairs > 1:
        ff = jnp.stack([ffz, ffc])
        ff = jnp.stack(
            [
                pick(pick(ff, jnp.bitwise_xor(ci, b), 0), jnp.bitwise_xor(zi, a), 0)
                for a in range(outer)
                for b in range(2)
            ]
        )
        ff = lax.all_gather(ff, "bo", axis=0).reshape(pairs, outer, 2, 8 * cut + 8, width)
        down_t = ff[:, :, :, :wide_cut].transpose(1, 0, 2, 3, 4).reshape(local_width, width)
        up_t = ff[:, :, :, wide_cut : 2 * wide_cut].reshape(
            pairs, outer, 2, 2, 2, cut, local_width
        )
        up_t = up_t.transpose(1, 2, 3, 0, 4, 5, 6).reshape(width, local_width)
        bias_t = ff[:, :, :, 2 * wide_cut, :wide_cut].transpose(1, 0, 2, 3).reshape(1, local_width)
        weights = (down_t, up_t, bias_t.astype(F32))
    else:
        weights = (ffz, ffc, w_qkv)
    if packed:
        w_out_own = w_out_own[0]
        w_out_other = swap(w_out_own, "bi")
        middle, norm_two = attend_output(
            scal, ctx, w_out_own, w_out_other, token, rows_in, heads
        )
    else:
        ctx_flat = ctx[:heads].reshape(width, rows)
        middle = token.astype(F32) + dot(ctx_flat, square[:, 3 * width :], TN) + rows_in[4:5]
        norm_two = (normalize(middle)[0] * rows_in[5:6] + rows_in[6:7]).astype(BF16)
    norm_two_t = group(norm_two)

    places = jnp.stack([zi, ci]).astype(jnp.int32)
    fed = feed_forward(places, norm_two_t, d_out_t, weights, local_width)
    act, d_pre, out_keep, *out_send = fed[:6]
    dn_keep, *dn_send = fed[6:10]
    dn_got = [swap_plane(part, k + 1) for k, part in enumerate(dn_send)]
    if packed:
        d_middle, d_branch, d_ctx, sums = turn_back(
            scal, dn_keep, dn_got, middle, d_out, w_out_own, w_out_other, rows_in, heads, seq
        )
    else:
        d_middle, d_branch, sums = turn_math(dn_keep, dn_got, middle, d_out, rows_in)
        d_ctx = dot(square[:, 3 * width :], d_branch, NT).astype(BF16).reshape(heads, HD, rows)
        d_ctx = jnp.pad(d_ctx, ((0, seq - heads), (0, 0), (0, 0)))
    act, d_pre = lax.optimization_barrier((act, d_pre, d_ctx))[:2]

    if packed:
        send, keep = feed_grads(places, act, d_pre, norm_two_t, d_out_t, outer, wide_cut)
    else:
        n2_all, dy_all = (jnp.concatenate(norm_two_t), jnp.concatenate(d_out_t))
        grad_down = dot(act, dy_all, TN).reshape(outer, pairs, 2, wide_cut, width)
        grad_up = dot(n2_all, d_pre, TN).reshape(outer, 2, 2, pairs, 2, cut, local_width)
        grad_up = grad_up.transpose(0, 3, 1, 2, 4, 5, 6)
        grad_up = grad_up.reshape(outer, pairs, 2, 4 * cut, local_width)
        grad_b_up = jnp.sum(d_pre.astype(F32), axis=0).reshape(outer, pairs, 2, 1, wide_cut)
        grad_b_up = jnp.pad(
            grad_b_up, ((0, 0), (0, 0), (0, 0), (0, 7), (0, width - wide_cut))
        )
        grads = jnp.concatenate([grad_down, grad_up, grad_b_up], axis=3)
        grads = lax.psum_scatter(grads, "bo", scatter_dimension=1, tiled=True)[:, 0]
        grads = jnp.stack([pick(grads, jnp.bitwise_xor(zi, k), 0) for k in range(outer)])
        send, keep = (pick(grads, 1 - ci, 1).astype(BF16), pick(grads, ci, 1))
    keep, away = fold(keep, swap(send, "bi"))
    back = [swap(part, "zo", k + 1) for k, part in enumerate(away)]
    d_ctx = lax.all_to_all(d_ctx, SEQ, split_axis=0, concat_axis=0, tiled=True)

    scal = after(scal, *away)
    if packed:
        w_qkv_other = swap(after(fed[10], *away), "bi")

    dchunk, dall = attend_backward(scal, qkvt, d_ctx, ctxt, lse)
    *back, dchunk = lax.optimization_barrier(tuple(back) + (dchunk,))
    d_rows = lax.all_to_all(dchunk, SEQ, split_axis=0, concat_axis=0, tiled=True)
    d_branch_late = after(d_branch, dall)
    if packed:
        grad_out, part = out_grad(scal, ctx, d_branch_late, heads, batch)
        grad_out, *part = plane_fold(scal, grad_out, swap(part, "bi"))
        got = [swap_plane(value, k + 1) for k, value in enumerate(part)]
        grad_out, part = line_fold(scal, grad_out, got)
        grad_w_output = grad_out + sum(
            swap(value, "zo", k + 1).astype(F32) for k, value in enumerate(part)
        )
    else:
        grad_out = dot(ctx[:heads].reshape(width, rows), d_branch_late)
        grad_w_output = lax.psum_scatter(grad_out, ALL, scatter_dimension=0, tiled=True)
    out_got = [swap_plane(after(part, dall), k + 1) for k, part in enumerate(out_send)]
    layer_out = middle + out_keep + sum(part.astype(F32) for part in out_got) + b_down_f
    layer_out = layer_out.astype(BF16)
    total = keep + sum(part.astype(F32) for part in back)
    grad_w_down = total[:wide_cut]
    grad_bu = total[wide_cut + 4 * cut, :wide_cut]
    up_back = total[wide_cut : 2 * wide_cut].astype(BF16).reshape(4, cut, local_width)
    up_back = after(jnp.concatenate([up_back, up_back]), d_rows)
    up_back = lax.all_to_all(up_back, PLANE, split_axis=0, concat_axis=0, tiled=True)
    if packed:
        grad_w_up = unpack_up(yi[None].astype(jnp.int32), up_back, outer)
    else:
        up_back = pick(up_back.reshape(4, 2, cut, local_width), yi, 1)
        grad_w_up = (
            up_back.reshape(4, cut, outer, local_width // outer)
            .transpose(1, 2, 0, 3)
            .reshape(cut, hidden_width)
            .astype(F32)
        )
    if packed:
        grad_tokens = input_grad(
            scal, d_rows, fed[10], w_qkv_other, token, d_middle, rows_in, heads
        )
    else:
        d_flat = d_rows[:heads].reshape(heads, 3, HD, rows).transpose(1, 0, 2, 3)
        d_flat = d_flat.reshape(3, width, rows)
        d_norm_one = sum(
            dot(d_flat[i], square[:, i * width : (i + 1) * width], ((0,), (1,)))
            for i in range(3)
        )
        normed_one, factor_one = normalize(token.astype(F32))
        d_in_norm, _, _ = norm_backward(d_norm_one, normed_one, factor_one, rows_in[0:1])
        grad_tokens = d_middle + d_in_norm

    last = head_grads(scal, dall, norm_one, norm_raw, head_f, sums, heads, seq, batch)
    if packed:
        last = last[0] + swap(last[1], "bi").astype(F32)
    else:
        last = last[0].reshape(seq, batch, cut, WIDE)
        last = lax.psum_scatter(last, BAT, scatter_dimension=1, tiled=True)[:, 0]
    last = after(last.astype(BF16), d_rows)
    last = lax.all_to_all(last, SEQ, split_axis=0, concat_axis=0, tiled=True)
    if packed:
        *grad_qkv, vec = unpack_heads(last, heads)
        vec = vec.T
        vec_of = [vec[i] for i in range(8)]
    else:
        last = last.astype(F32)
        grad_qkv = last[:heads, :, : 3 * HD].reshape(heads, cut, 3, HD).transpose(2, 1, 0, 3)
        grad_qkv = grad_qkv.reshape(3, cut, width)
        vec = jnp.sum(last[:, :, 3 * HD : 3 * HD + 8], axis=0)
        vec_of = [vec[:, i] for i in range(8)]
    return (
        layer_out[None],
        grad_tokens[None],
        vec_of[0],
        vec_of[1],
        grad_qkv[0],
        vec_of[2],
        grad_qkv[1],
        grad_qkv[2],
        vec_of[3],
        grad_w_output,
        vec_of[4],
        vec_of[5],
        vec_of[6],
        grad_w_up,
        grad_bu,
        grad_w_down,
        vec_of[7],
    )


def solution(mesh):
    seq, batch = (mesh.shape["seq"], mesh.shape["batch"])
    fine = Mesh(mesh.devices.reshape(seq // 4, 2, 2, batch // 2, 2), ALL)
    act, mat, vec = (P(BAT, SEQ, None), P(ALL, None), P(ALL))
    return jax.shard_map(
        body,
        mesh=fine,
        in_specs=(
            act, act, P(BAT), vec, vec, mat, vec, mat, mat, vec, mat, vec, vec, vec, mat, vec, mat, vec,
        ),
        out_specs=(
            act, act, vec, vec, mat, vec, mat, mat, vec, mat, vec, vec, vec, mat, vec, mat, vec,
        ),
        check_vma=False,
    )
```

```python
import functools

import jax
import jax.numpy as jnp
from jax import lax
from jax.experimental import pallas as pl
from jax.experimental.pallas import tpu as pltpu
from jax.sharding import Mesh
from jax.sharding import PartitionSpec as P

HD = 64
EPS = 1e-05
LOG2E = 1.4426950408889634
SEQ = ("z", "y", "x")
ALL = SEQ + ("batch",)
WIDE = 4 * HD
LIMIT = 58
F32 = jnp.float32
BF16 = jnp.bfloat16
NN = ((1,), (0,))
NT = ((1,), (1,))
TN = ((0,), (0,))


def normalize(values):
    centre = jnp.mean(values, axis=-1, keepdims=True)
    centred = values - centre
    spread = jnp.mean(centred * centred, axis=-1, keepdims=True)
    factor = lax.rsqrt(spread + EPS)
    return (centred * factor, factor)


def norm_backward(grad_out, normed, factor, gain):
    grad_gain = jnp.sum(grad_out * normed, axis=0, keepdims=True)
    grad_shift = jnp.sum(grad_out, axis=0, keepdims=True)
    scaled = grad_out * gain.astype(F32)
    grad_in = factor * (
        scaled
        - jnp.mean(scaled, axis=-1, keepdims=True)
        - normed * jnp.mean(scaled * normed, axis=-1, keepdims=True)
    )
    return (grad_in, grad_gain, grad_shift)


def dot(left, right, dims=NN):
    return lax.dot_general(left, right, (dims, ((), ())), preferred_element_type=F32)


def swap(value, axis, step=1):
    size = lax.axis_size(axis)
    return lax.ppermute(value, axis, [(i, i ^ step) for i in range(size)])


def swap_plane(value, step):
    return lax.ppermute(value, ("y", "x"), [(i, i ^ step) for i in range(4)])


def after(value, *others):
    return lax.optimization_barrier((value,) + others)[0]


def split(length):
    return 512 if length % 512 == 0 else length


SMALL = pl.CostEstimate(flops=1, bytes_accessed=1, transcendentals=0)
SMEM_SPEC = pl.BlockSpec(memory_space=pltpu.SMEM)
HBM_SPEC = pl.BlockSpec(memory_space=pltpu.HBM)


def full_block(shape):
    zeros = (0,) * len(shape)
    return pl.BlockSpec(shape, lambda i: zeros, pipeline_mode=pl.Buffered(1))


def like(shape, dtype):
    return jax.ShapeDtypeStruct(shape, dtype)


def once(name, kernel, args, outs, scratch=(), limit=LIMIT, left=()):
    in_specs = [SMEM_SPEC if a.dtype == jnp.int32 else full_block(a.shape) for a in args]
    out_specs = [HBM_SPEC if i in left else full_block(o.shape) for i, o in enumerate(outs)]
    return pl.pallas_call(
        kernel,
        grid=(1,),
        out_shape=tuple(outs),
        in_specs=in_specs,
        out_specs=tuple(out_specs),
        scratch_shapes=list(scratch),
        compiler_params=pltpu.CompilerParams(vmem_limit_bytes=limit << 20),
        cost_estimate=SMALL,
        name=name,
    )(*args)


PLACE, PREFIX, CORE, FLAT, LINE = range(5)


def rank_of(scal, k, d, other):
    line = jnp.bitwise_xor(scal[LINE], k)
    flat = jnp.bitwise_xor(scal[FLAT], d)
    return (line * 4 + flat) * 2 + jnp.bitwise_xor(scal[CORE], other)


def rows_at(index, size):
    return pl.ds(pl.multiple_of(index * size, size), size)


def square_pieces(wq, other):
    outer = other.shape[0] // 4
    for d in range(4):
        for k in range(outer):
            yield (k, d, 0, wq[d].at[k])
            yield (k, d, 1, other.at[d * outer + k])


def pack_kernel(lines, heads, scal, token, w_out, w_up, w_q, w_k, w_v, *refs):
    vectors, (up_own, out_b, out_c, out_d, send) = (refs[:8], refs[8:])
    wide = w_up.shape[1] // (4 * lines)
    rows, cut = (token.shape[0], w_up.shape[0])
    for out in (out_b, out_c, out_d):
        out[:rows, :] = token[...]
        out[rows : rows + cut, :] = w_out[...]
    for z in range(lines):
        pieces = [w_up[:, (z * 4 + t) * wide : (z * 4 + t + 1) * wide] for t in range(4)]
        for k, (out, first) in enumerate(
            ((up_own, 0), (out_b, rows + cut), (out_c, rows + cut), (out_d, rows + cut))
        ):
            target = jnp.bitwise_xor(scal[FLAT], k)
            value = pieces[0]
            for t in range(1, 4):
                value = jnp.where(target == t, pieces[t], value)
            out[first : first + cut, z * wide : (z + 1) * wide] = value
    lane = jnp.concatenate([ref[...].astype(F32) for ref in vectors], axis=0)
    lane = jnp.concatenate([lane, jnp.zeros((8, 2 * HD - cut), F32)], axis=1)
    vec = jnp.concatenate([jnp.transpose(lane)[:cut], jnp.zeros((cut, HD - 8), F32)], axis=1)
    vec = vec.astype(BF16)
    for h in range(send.shape[0]):
        for i, w in enumerate((w_q, w_k, w_v)):
            if h < heads:
                piece = w[:, h * HD : (h + 1) * HD]
            else:
                piece = jnp.zeros((cut, HD), BF16)
            send[h, :, i * HD : (i + 1) * HD] = piece
        send[h, :, 3 * HD :] = vec


def forward_kernel(
    heads, scal, ahead, own_b, own_c, own_d, zc, xc, yc, xya, xyb, w,
    n1_out, n0_out, qkvt, ctxc, ctxt, lse, rows_out, wt_out, wo_out,
    n1, n0, k_s, w_s, sems,
):
    place, prefix = (scal[PLACE], scal[PREFIX])
    outer = zc.shape[0] + 1
    length, width = n1.shape
    rows = length // (4 * outer)
    cut = w.shape[2]
    blk = split(length)
    copies = []
    near = ((ahead, 0), (own_b, 1), (own_c, 2), (own_d, 3))
    along = ((zc, 1, 0), (xc, 1, 1), (yc, 1, 2), (xya, 1, 3), (xyb, outer // 2 + 1, 3))
    for src, d in near:
        pair = (src.at[rows : rows + cut, :], wo_out.at[d * outer])
        copies.append(pltpu.make_async_copy(*pair, sems.at[2 + len(copies)]))
    for src, k, d in along:
        target = wo_out.at[d * outer + k : d * outer + k + src.shape[0]]
        copies.append(pltpu.make_async_copy(src.at[:, rows:, :], target, sems.at[2 + len(copies)]))
    for copy in copies:
        copy.start()
    head = jnp.minimum(place, heads - 1)
    for b in range(2):
        for i in range(w.shape[1]):
            at = (2 * i + b) * cut
            w_s[at : at + cut, :] = w[b, i].astype(F32)
    turned = jnp.transpose(w_s[...])
    wt_out[...] = turned[: 3 * HD].astype(BF16)
    rows_in = turned[3 * HD : 3 * HD + 8]
    rows_out[...] = rows_in
    gain = rows_in[0:1]
    shift = rows_in[1:2]

    def norm_rows(value, k, d):
        normed, _ = normalize(value.astype(F32))
        here = rows_at(jnp.bitwise_xor(place, k * 4 + d), rows)
        n0[here, :] = normed.astype(BF16)
        n1[here, :] = (normed * gain + shift).astype(BF16)

    for src, d in near:
        norm_rows(src[:rows, :], 0, d)
    for src, first, d in along:

        def one(k, carry, src=src, first=first, d=d):
            norm_rows(src[k, :rows, :], first + k, d)
            return carry

        lax.fori_loop(0, src.shape[0], one, 0)
    for i, (src, dst) in enumerate(((n1, n1_out), (n0, n0_out))):
        copy = pltpu.make_async_copy(src, dst, sems.at[i])
        copy.start()
        copies.append(copy)
    bias_q = w_s[rows_at(head, HD), 3 * HD + 2 : 3 * HD + 3]
    bias_v = w_s[rows_at(head, HD), 3 * HD + 3 : 3 * HD + 4]
    for i in range(length // blk):
        sl = slice(i * blk, (i + 1) * blk)
        part = dot(wt_out[...], n1[sl, :], NT)
        k_part = part[HD : 2 * HD].astype(BF16)
        qkvt[:HD, sl] = (part[:HD] + bias_q).astype(BF16)
        qkvt[HD : 2 * HD, sl] = k_part
        qkvt[2 * HD :, sl] = (part[2 * HD :] + bias_v).astype(BF16)
        k_s[sl, :] = jnp.transpose(k_part.astype(F32)).astype(BF16)
    scale = 0.125 * LOG2E

    def one_query(i, carry):
        first = pl.multiple_of(i * blk, blk)
        q_now = qkvt[:HD, pl.ds(first, blk)]

        def step(masked, j, state):
            top, total, acc = state
            start = pl.multiple_of(j * blk, blk)
            scores = dot(k_s[pl.ds(start, blk), :], q_now) * scale
            if masked:
                key = start + lax.broadcasted_iota(jnp.int32, (blk, blk), 0)
                query = first + lax.broadcasted_iota(jnp.int32, (blk, blk), 1)
                scores = jnp.where((key <= query) | (key < prefix), scores, -1e30)
            new_top = jnp.maximum(top, jnp.max(scores, axis=0, keepdims=True))
            prob = jnp.exp2(scores - new_top)
            fade = jnp.exp2(top - new_top)
            total = total * fade + jnp.sum(prob, axis=0, keepdims=True)
            acc = acc * fade + dot(qkvt[2 * HD :, pl.ds(start, blk)], prob.astype(BF16))
            return (new_top, total, acc)

        state = (
            jnp.full((1, blk), -1e30, F32),
            jnp.zeros((1, blk), F32),
            jnp.zeros((HD, blk), F32),
        )
        full = jnp.maximum(prefix // blk, i)
        needed = jnp.maximum((prefix + blk - 1) // blk, i + 1)
        state = lax.fori_loop(0, full, functools.partial(step, False), state)
        top, total, acc = lax.fori_loop(full, needed, functools.partial(step, True), state)
        out = acc / total
        ctxt[:, pl.ds(first, blk)] = out
        lse[:, pl.ds(first, blk)] = top + jnp.log2(total)
        for r in range(blk // rows):
            ctxc[i * (blk // rows) + r] = out[:, r * rows : (r + 1) * rows].astype(BF16)
        return carry

    lax.fori_loop(0, length // blk, one_query, 0)
    for copy in copies:
        copy.wait()


def backward_kernel(
    scal, qkvt, dcr, ctxt, lse, dchunk, dall, q_s, k_s, v_s, dc_s, dct_s, del_s, dq_s, dk_s, dv_s
):
    prefix = scal[PREFIX]
    rows = dcr.shape[2]
    length = qkvt.shape[1]
    blk = split(length)
    count = length // blk
    for i in range(count):
        sl = slice(i * blk, (i + 1) * blk)
        turned = jnp.transpose(qkvt[:, sl].astype(F32)).astype(BF16)
        q_s[sl, :] = turned[:, :HD]
        k_s[sl, :] = turned[:, HD : 2 * HD]
        v_s[sl, :] = turned[:, 2 * HD :]
    for i in range(length // rows):
        sl = slice(i * rows, (i + 1) * rows)
        dct_s[:, sl] = dcr[i]
        dc_s[sl, :] = jnp.transpose(dcr[i].astype(F32)).astype(BF16)
    del_s[...] = jnp.sum(dct_s[...].astype(F32) * ctxt[...], axis=0, keepdims=True)
    dq_s[...] = jnp.zeros_like(dq_s)
    scale = 0.125 * LOG2E

    def one_key(j, carry):
        start = pl.multiple_of(j * blk, blk)
        dk_s[...] = jnp.zeros_like(dk_s)
        dv_s[...] = jnp.zeros_like(dv_s)

        def step(masked, i, inner):
            first = pl.multiple_of(i * blk, blk)
            here = pl.ds(first, blk)
            scores = dot(k_s[pl.ds(start, blk), :], qkvt[:HD, here]) * scale
            prob = jnp.exp2(scores - lse[:, here])
            if masked:
                key = start + lax.broadcasted_iota(jnp.int32, (blk, blk), 0)
                query = first + lax.broadcasted_iota(jnp.int32, (blk, blk), 1)
                prob = jnp.where((key <= query) | (key < prefix), prob, 0.0)
            d_prob = dot(v_s[pl.ds(start, blk), :], dct_s[:, here])
            d_score = (prob * (d_prob - del_s[:, here])).astype(BF16)
            dv_s[...] += dot(prob.astype(BF16), dc_s[here, :])
            dk_s[...] += dot(d_score, q_s[here, :])
            dq_s[:, here] += dot(qkvt[HD : 2 * HD, pl.ds(start, blk)], d_score)
            return inner

        begin = jnp.where(start < prefix, 0, j)
        middle = jnp.where(start + blk <= prefix, begin, j + 1)
        lax.fori_loop(begin, middle, functools.partial(step, True), 0)
        lax.fori_loop(middle, count, functools.partial(step, False), 0)
        d_key = jnp.transpose(dk_s[...] * 0.125).astype(BF16)
        d_value = jnp.transpose(dv_s[...]).astype(BF16)
        dall[HD : 2 * HD, pl.ds(start, blk)] = d_key
        dall[2 * HD :, pl.ds(start, blk)] = d_value
        for r in range(blk // rows):
            at = j * (blk // rows) + r
            dchunk[at, HD : 2 * HD, :] = d_key[:, r * rows : (r + 1) * rows]
            dchunk[at, 2 * HD :, :] = d_value[:, r * rows : (r + 1) * rows]
        return carry

    lax.fori_loop(0, count, one_key, 0)
    for i in range(count):
        sl = slice(i * blk, (i + 1) * blk)
        d_query = (dq_s[:, sl] * 0.125).astype(BF16)
        dall[:HD, sl] = d_query
        for r in range(blk // rows):
            dchunk[i * (blk // rows) + r, :HD, :] = d_query[:, r * rows : (r + 1) * rows]


def stacked(pieces, first, last):
    return jnp.concatenate([piece[first:last, :].astype(F32) for piece in pieces]).astype(BF16)


def out_pieces(own, other):
    outer = own.shape[0] // 4
    return [
        (i % outer, i // outer, core, ref.at[i])
        for core, ref in ((0, own), (1, other))
        for i in range(own.shape[0])
    ]


def middle_kernel(heads, scal, ctx, own, other, token, rows_in, middle, norm_two, plain, moved):
    pieces = out_pieces(own, other)
    cut = own.shape[1]
    plain[...] = ctx[:heads].reshape(plain.shape).astype(F32)
    for n, (k, d, core, _) in enumerate(pieces):
        moved[n * cut : (n + 1) * cut, :] = plain[rows_at(rank_of(scal, k, d, core), cut), :]
    turned = jnp.transpose(moved[...]).astype(BF16)
    product = dot(turned, stacked([p[3] for p in pieces], 0, cut))
    value = token[...].astype(F32) + product + rows_in[4:5, :]
    middle[...] = value
    normed, _ = normalize(value)
    norm_two[...] = (normed * rows_in[5:6, :] + rows_in[6:7, :]).astype(BF16)


def feed_kernel(
    scal, n2_a, n2_b, n2_c, n2_d, dy_a, dy_b, dy_c, dy_d, ffz, ffc,
    out_keep, out_b, out_c, out_d, dn_keep, dn_b, dn_c, dn_d, send, keep,
    n2, dy, down, up, act, d_pre, down_s, up_s, bias,
):
    outer = ffz.shape[0]
    cut = (ffz.shape[1] - 8) // 8
    half = 4 * cut
    sources = [(src, k, core) for core, src in ((0, ffz), (1, ffc)) for k in range(outer)]

    def block_of(k, core):
        line = jnp.bitwise_xor(scal[LINE], k)
        return line * 2 + jnp.bitwise_xor(scal[CORE], core)

    rows = []
    for src, k, core in sources:
        down[rows_at(block_of(k, core), half), :] = src[k, :half, :]
        for d in range(4):
            here = rows_at(rank_of(scal, k, d, core), cut)
            up_s[here, :] = src[k, half + d * cut : half + (d + 1) * cut, :].astype(F32)
        rows.append((block_of(k, core), src[k, 2 * half :, :half].astype(F32)[:1]))
    up[...] = up_s[...].astype(BF16)
    for q in range(2 * outer):
        bias[:, q * half : (q + 1) * half] = sum(jnp.where(at == q, row, 0.0) for at, row in rows)
    count = n2_a.shape[0]
    for i, piece in enumerate((n2_a, n2_b, n2_c, n2_d)):
        n2[i * count : (i + 1) * count, :] = piece[...]
    for i, piece in enumerate((dy_a, dy_b, dy_c, dy_d)):
        dy[i * count : (i + 1) * count, :] = piece[piece.shape[0] - count :, :]
    tile = 256
    for c in range(down.shape[0] // tile):
        sl = slice(c * tile, (c + 1) * tile)
        pre = dot(n2[...], up[:, sl]) + bias[:, sl]
        cdf = 0.5 * (1.0 + lax.erf(pre * 0.7071067811865476))
        act[:, sl] = (pre * cdf).astype(BF16)
        slope = cdf + pre * jnp.exp(-0.5 * pre * pre) * 0.3989422804014327
        d_pre[:, sl] = (dot(dy[...], down[sl, :], NT) * slope).astype(BF16)
    back = dot(d_pre[...], up[...], NT)
    for i, ref in enumerate((dn_keep, dn_b, dn_c, dn_d)):
        ref[...] = back[i * count : (i + 1) * count].astype(ref.dtype)
    out = dot(act[...], down[...])
    for i, ref in enumerate((out_keep, out_b, out_c, out_d)):
        ref[...] = out[i * count : (i + 1) * count].astype(ref.dtype)
    down_s[...] = dot(act[...], dy[...], TN)
    up_s[...] = dot(n2[...], d_pre[...], TN)
    total = jnp.sum(d_pre[...].astype(F32), axis=0, keepdims=True)
    width = keep.shape[2]
    for k in range(outer):
        for core, ref in ((0, keep), (1, send)):
            at = block_of(k, core)
            ref[k, :half, :] = down_s[rows_at(at, half), :].astype(ref.dtype)
            for t in range(4):
                line = jnp.bitwise_xor(scal[LINE], k)
                rank = (line * 4 + t) * 2 + jnp.bitwise_xor(scal[CORE], core)
                here = slice(half + t * cut, half + (t + 1) * cut)
                ref[k, here, :] = up_s[rows_at(rank, cut), :].astype(ref.dtype)
            part = sum(
                jnp.where(at == q, total[:, q * half : (q + 1) * half], 0.0)
                for q in range(2 * outer)
            )
            part = jnp.concatenate([part, jnp.zeros((1, width - half), F32)], axis=1)
            ref[k, 2 * half :, :] = jnp.broadcast_to(part, (8, width)).astype(ref.dtype)


def turn_kernel(
    heads, scal, keep, got_b, got_c, got_d, middle, d_out, own, other, rows_in, ctx,
    d_middle, d_branch_out, d_ctx, sums, wo_keep, wo_send, plain, full,
):
    d_norm = keep[...] + (got_b[...].astype(F32) + got_c[...].astype(F32)) + got_d[...].astype(F32)
    normed, factor = normalize(middle[...])
    grad_in, grad_gain, grad_shift = norm_backward(d_norm, normed, factor, rows_in[5:6, :])
    grad_up = d_out[...].astype(F32)
    total = grad_up + grad_in
    low = total.astype(BF16)
    d_middle[...] = total
    d_branch_out[...] = low[:8]
    pieces = out_pieces(own, other)
    cut = own.shape[1]
    back = dot(stacked([p[3] for p in pieces], 0, cut), low, NT)
    for n, (k, d, core, _) in enumerate(pieces):
        plain[rows_at(rank_of(scal, k, d, core), cut), :] = back[n * cut : (n + 1) * cut]
    seq, rows = (d_ctx.shape[0], d_ctx.shape[2])
    d_ctx[:heads] = plain[...].astype(BF16).reshape(heads, HD, rows)
    d_ctx[heads:] = jnp.zeros((seq - heads, HD, rows), BF16)
    sums[0:1, :] = jnp.sum(low.astype(F32), axis=0, keepdims=True)
    sums[1:2, :] = grad_gain
    sums[2:3, :] = grad_shift
    sums[3:4, :] = jnp.sum(grad_up, axis=0, keepdims=True)
    sums[4:, :] = jnp.zeros((4, sums.shape[1]), F32)
    full[...] = dot(ctx[:heads].reshape(heads * HD, rows), low).reshape(full.shape)
    for i in range(seq):
        wo_keep[i] = full[2 * i + scal[CORE]]
        wo_send[i] = full[2 * i + 1 - scal[CORE]].astype(BF16)


def fold_kernel(keep, got, own, *away):
    for k, ref in enumerate((own,) + away):
        ref[...] = (keep[k] + got[k].astype(F32)).astype(ref.dtype)


def finish_kernel(scal, keep, *refs):
    got, (wo_keep, wo_got, out_b, out_c, out_d), outs = (refs[:-13], refs[-13:-8], refs[-8:])
    grad_down, bias, own, wo_own, away_b, away_c, away_d, total = outs
    value = keep[...]
    for ref in got:
        value = value + ref[...].astype(F32)
    total[...] = value
    half = grad_down.shape[0]
    cut = half // 4
    lines = wo_own.shape[0]
    grad_down[...] = value[:half]
    bias[...] = value[2 * half :, :half]
    for k, ref in enumerate((own, away_b, away_c, away_d)):
        at = jnp.bitwise_xor(scal[FLAT], k)
        here = pl.ds(pl.multiple_of(half + at * cut, 8), cut)
        ref[:cut, :] = total[here, :].astype(BF16)
        for z in range(lines):
            part = wo_keep[4 * z + at] + wo_got[4 * z + at].astype(F32)
            if k:
                ref[(1 + z) * cut : (2 + z) * cut, :] = part.astype(BF16)
            else:
                wo_own[z] = part
    for src, ref in ((out_b, away_b), (out_c, away_c), (out_d, away_d)):
        ref[(1 + lines) * cut :, :] = src[...]


def close_kernel(
    lines, scal, own, wo_own, got_b, got_c, got_d, middle, out_keep, rows_in,
    layer_out, grad_up, grad_out, *away,
):
    cut = grad_out.shape[0]
    got = (got_b, got_c, got_d)
    value = middle[...] + out_keep[...] + rows_in[7:8, :]
    pieces = [own[...].astype(F32)]
    for ref in got:
        value = value + ref[(1 + lines) * cut :, :].astype(F32)
        pieces.append(ref[:cut, :].astype(F32))
    layer_out[...] = value.astype(BF16)
    for k, out in enumerate((grad_out,) + away):
        at = jnp.bitwise_xor(scal[LINE], k)
        here = pl.ds(pl.multiple_of((1 + at) * cut, 8), cut)
        part = wo_own[at]
        for ref in got:
            part = part + ref[here, :].astype(F32)
        out[...] = part.astype(out.dtype)
    wide = own.shape[1] // lines
    for t in range(4):
        step = jnp.bitwise_xor(scal[FLAT], t)
        piece = pieces[0]
        for k in range(1, 4):
            piece = jnp.where(step == k, pieces[k], piece)
        for z in range(lines):
            at = (z * 4 + t) * wide
            grad_up[:, at : at + wide] = piece[:, z * wide : (z + 1) * wide]


def heads_kernel(heads, scal, dall, n1, n0, wt, sums, keep, send, gh, gm, cs, full):
    step = pl.program_id(0)

    @pl.when(step == 0)
    def _():
        gh[...] = jnp.zeros_like(gh)
        gm[...] = jnp.zeros_like(gm)
        cs[...] = jnp.zeros_like(cs)

    gh[...] += dot(dall[...], n1[...])
    gm[...] += dot(dall[...], n0[...])
    cs[...] += dot(dall[...], jnp.ones((dall.shape[1], 2 * HD), BF16))

    @pl.when(step == pl.num_programs(0) - 1)
    def _():
        place = scal[PLACE]
        width = gh.shape[1]
        live = place < heads
        wide = wt[...].astype(F32)
        gain = jnp.where(live, jnp.sum(wide * gm[...], axis=0, keepdims=True), 0.0)
        shift = jnp.where(live, jnp.sum(wide * cs[:, :1], axis=0, keepdims=True), 0.0)
        line = jnp.transpose(cs[...])[0:1]
        mine = lax.broadcasted_iota(jnp.int32, (1, width), 1) // HD == place
        b_q = jnp.where(mine, jnp.concatenate([line[:, :HD]] * heads, axis=1), 0.0)
        b_v = jnp.where(mine, jnp.concatenate([line[:, 2 * HD :]] * heads, axis=1), 0.0)
        vec = jnp.concatenate([gain, shift, b_q, b_v, sums[:4, :]], axis=0)
        pad = jnp.zeros((width, HD - 8), F32)
        block = jnp.concatenate([jnp.transpose(gh[...]), jnp.transpose(vec), pad], axis=1)
        full[...] = block.reshape(full.shape)
        for i in range(keep.shape[0]):
            keep[i] = full[2 * i + scal[CORE]]
            send[i] = full[2 * i + 1 - scal[CORE]].astype(BF16)


def head_grads(scal, dall, n1, n0, wt, sums, heads, seq):
    length, width = n1.shape
    blk = split(length)
    cut = width // (2 * seq)
    outs = (like((seq, cut, WIDE), F32), like((seq, cut, WIDE), BF16))
    return pl.pallas_call(
        functools.partial(heads_kernel, heads),
        out_shape=outs,
        grid=(length // blk,),
        in_specs=[
            SMEM_SPEC,
            pl.BlockSpec((3 * HD, blk), lambda i: (0, i)),
            pl.BlockSpec((blk, width), lambda i: (i, 0)),
            pl.BlockSpec((blk, width), lambda i: (i, 0)),
            full_block(wt.shape),
            full_block(sums.shape),
        ],
        out_specs=tuple(full_block(out.shape) for out in outs),
        scratch_shapes=[
            pltpu.VMEM((3 * HD, width), F32),
            pltpu.VMEM((3 * HD, width), F32),
            pltpu.VMEM((3 * HD, 2 * HD), F32),
            pltpu.VMEM((2 * seq, cut, WIDE), F32),
        ],
        compiler_params=pltpu.CompilerParams(vmem_limit_bytes=LIMIT << 20),
        cost_estimate=SMALL,
        name="heads",
    )(scal, dall, n1, n0, wt, sums)


def last_kernel(
    heads, scal, d_rows, wq_a, wq_b, wq_c, wq_d, other, token, d_middle, rows_in, grad_tokens, plain
):
    cut = other.shape[1] // 3
    pieces = list(square_pieces((wq_a, wq_b, wq_c, wq_d), other))
    total = 0.0
    for i in range(3):
        part = jnp.concatenate(
            [d_rows[h, i * HD : (i + 1) * HD, :].astype(F32) for h in range(heads)], axis=0
        )
        weights = stacked([p[3] for p in pieces], i * cut, (i + 1) * cut)
        total = total + dot(weights, part.astype(BF16))
    for n, (k, d, core, _) in enumerate(pieces):
        plain[rows_at(rank_of(scal, k, d, core), cut), :] = total[n * cut : (n + 1) * cut]
    normed, factor = normalize(token[...].astype(F32))
    grad_in, _, _ = norm_backward(jnp.transpose(plain[...]), normed, factor, rows_in[0:1, :])
    grad_tokens[...] = d_middle[...] + grad_in


def unpack_kernel(heads, got, g_q, g_k, g_v, vec):
    for i, out in enumerate((g_q, g_k, g_v)):
        for h in range(heads):
            out[:, h * HD : (h + 1) * HD] = got[h, :, i * HD : (i + 1) * HD].astype(F32)
    total = got[0, :, 2 * HD :].astype(F32)
    for s in range(1, got.shape[0]):
        total = total + got[s, :, 2 * HD :].astype(F32)
    cut = total.shape[0]
    total = jnp.concatenate([total, jnp.zeros((2 * HD - cut, 2 * HD), F32)], axis=0)
    vec[...] = jnp.transpose(total)[HD : HD + 8, :cut]


def body(
    tokens, cotangent, prefix_len, gain_one, shift_one, w_query, b_query, w_key, w_value, b_value,
    w_output, b_output, gain_two, shift_two, w_up, b_up, w_down, b_down,
):
    outer = lax.axis_size("z")
    seq = 4 * outer
    token, d_out = (tokens[0], cotangent[0])
    rows, width = token.shape
    length = seq * rows
    heads = width // HD
    cut = w_query.shape[0]
    half = w_down.shape[0]
    local = w_up.shape[1] // 4
    flat = lax.axis_index(("y", "x"))
    places = (lax.axis_index(SEQ), prefix_len[0], lax.axis_index("batch"), flat, lax.axis_index("z"))
    scal = jnp.stack(places).astype(jnp.int32)

    ahead = jnp.concatenate([token, w_output])
    zc = jnp.stack([swap(ahead, "z", k) for k in range(1, outer)])
    vectors = (
        gain_one, shift_one, b_query, b_value, b_output, gain_two, shift_two, b_down,
    )
    vectors = [value[None] for value in vectors]
    up_own, *first, send = once(
        "pack",
        functools.partial(pack_kernel, outer, heads),
        (scal, token, w_output, w_up, w_query, w_key, w_value, *vectors),
        [like((cut, local), BF16)]
        + [like((rows + 2 * cut, width), BF16)] * 3
        + [like((seq, cut, WIDE), BF16)],
    )
    first = [swap_plane(part, k + 1) for k, part in enumerate(first)]
    zc = after(zc, *first)
    xc = swap(zc, "x")
    yc = swap(zc, "y")
    head_w = lax.all_to_all(after(send, zc), SEQ, split_axis=0, concat_axis=0, tiled=True)
    wq = after(jnp.concatenate([w_query, w_key, w_value]), zc)
    wq_got = [swap(wq, "z", k) for k in range(1, outer)]
    xc, yc, head_w, wq_got = lax.optimization_barrier((xc, yc, head_w, wq_got))
    xya = swap(xc[: outer // 2], "y")
    xyb = swap(yc[outer // 2 :], "x")
    head_w = lax.all_gather(head_w, "batch", axis=0, tiled=False)

    b_up_row = jnp.pad(b_up[None], ((0, 7), (0, width - half)))
    ff = [w_down, up_own] + [part[rows + cut :] for part in first] + [b_up_row]
    ff = after(jnp.concatenate(ff), head_w, xc)
    ff_got = [swap(ff, "z", k) for k in range(1, outer)]
    wq = after(jnp.stack([wq] + wq_got), xya, xyb)
    wq = [wq] + [swap_plane(wq, k) for k in range(1, 3)]

    norm_one, norm_raw, qkvt, ctxc, ctxt, lse, rows_in, wt, w_out_own = once(
        "forward",
        functools.partial(forward_kernel, heads),
        (scal, ahead, *first, zc, xc, yc, xya, xyb, head_w),
        [
            like((length, width), BF16),
            like((length, width), BF16),
            like((3 * HD, length), BF16),
            like((seq, HD, rows), BF16),
            like((HD, length), F32),
            like((1, length), F32),
            like((8, width), F32),
            like((3 * HD, width), BF16),
            like((seq, cut, width), BF16),
        ],
        [
            pltpu.VMEM((length, width), BF16),
            pltpu.VMEM((length, width), BF16),
            pltpu.VMEM((length, HD), BF16),
            pltpu.VMEM((width, WIDE), F32),
            pltpu.SemaphoreType.DMA((11,)),
        ],
        left=(0, 1, 8),
    )
    w_out_other = swap(w_out_own, "batch")
    ctxc, wq, ff_got = lax.optimization_barrier((ctxc, wq, ff_got))
    ffz = jnp.stack([ff] + ff_got)
    dy = [d_out] + [swap_plane(after(d_out, ctxc), k) for k in range(1, 4)]
    ctx = lax.all_to_all(ctxc, SEQ, split_axis=0, concat_axis=0, tiled=True)
    ffc = swap(ffz, "batch")
    dy, ctx = lax.optimization_barrier((dy, ctx))
    middle, norm_two = once(
        "middle",
        functools.partial(middle_kernel, heads),
        (scal, ctx, w_out_own, w_out_other, token, rows_in),
        [like((rows, width), F32), like((rows, width), BF16)],
        [pltpu.VMEM((width, rows), F32)] * 2,
    )
    n2 = [norm_two] + [swap_plane(norm_two, k) for k in range(1, 4)]

    part = [like((rows, width), F32)] + [like((rows, width), BF16)] * 3
    fed = once(
        "feed",
        feed_kernel,
        (scal, *n2, *dy, ffz, ffc),
        part + part + [like(ffz.shape, BF16), like(ffz.shape, F32)],
        [
            pltpu.VMEM((4 * rows, width), BF16),
            pltpu.VMEM((4 * rows, width), BF16),
            pltpu.VMEM((local, width), BF16),
            pltpu.VMEM((width, local), BF16),
            pltpu.VMEM((4 * rows, local), BF16),
            pltpu.VMEM((4 * rows, local), BF16),
            pltpu.VMEM((local, width), F32),
            pltpu.VMEM((width, local), F32),
            pltpu.VMEM((1, local), F32),
        ],
    )
    out_keep, *out_send = fed[:4]
    dn_keep, *dn_send = fed[4:8]
    send, keep = fed[8:]
    dn_got = [swap_plane(value, k + 1) for k, value in enumerate(dn_send)]

    count = 2 * half + 8
    own, *away = once(
        "fold",
        fold_kernel,
        (keep, swap(send, "batch")),
        [like((count, width), F32)] + [like((count, width), BF16)] * (outer - 1),
    )
    back = [swap(value, "z", k + 1) for k, value in enumerate(away)]
    dn_keep, _ = lax.optimization_barrier((dn_keep, away))
    d_middle, _, d_ctx, sums, wo_keep, wo_send = once(
        "turn",
        functools.partial(turn_kernel, heads),
        (scal, dn_keep, *dn_got, middle, d_out, w_out_own, w_out_other, rows_in, ctx),
        [
            like((rows, width), F32),
            like((8, width), BF16),
            like((seq, HD, rows), BF16),
            like((8, width), F32),
            like((seq, cut, width), F32),
            like((seq, cut, width), BF16),
        ],
        [pltpu.VMEM((width, rows), F32), pltpu.VMEM((2 * seq, cut, width), F32)],
    )
    d_ctx = lax.all_to_all(d_ctx, SEQ, split_axis=0, concat_axis=0, tiled=True)

    wo_got = swap(wo_send, "batch")
    wq = wq + [swap_plane(after(wq[0], sums), 3)]

    blk = split(length)
    dchunk, dall = once(
        "backward",
        backward_kernel,
        (scal, qkvt, d_ctx, ctxt, lse),
        [like((seq, 3 * HD, rows), BF16), like((3 * HD, length), BF16)],
        [
            pltpu.VMEM((length, HD), BF16),
            pltpu.VMEM((length, HD), BF16),
            pltpu.VMEM((length, HD), BF16),
            pltpu.VMEM((length, HD), BF16),
            pltpu.VMEM((HD, length), BF16),
            pltpu.VMEM((1, length), F32),
            pltpu.VMEM((HD, length), F32),
            pltpu.VMEM((blk, HD), F32),
            pltpu.VMEM((blk, HD), F32),
        ],
    )
    back, wq, dchunk = lax.optimization_barrier((back, wq, dchunk))
    d_rows = lax.all_to_all(dchunk, SEQ, split_axis=0, concat_axis=0, tiled=True)

    grad_w_down, bias, own, wo_own, *away = once(
        "finish",
        finish_kernel,
        (scal, own, *back, wo_keep, wo_got, *out_send),
        [
            like((half, width), F32),
            like((8, half), F32),
            like((cut, width), BF16),
            like((outer, cut, width), F32),
        ]
        + [like(((1 + outer) * cut + rows, width), BF16)] * 3,
        [pltpu.VMEM((count, width), F32)],
    )
    got = [swap_plane(value, k + 1) for k, value in enumerate(away)]
    layer_out, grad_w_up, grad_w_output, *away = once(
        "close",
        functools.partial(close_kernel, outer),
        (scal, own, wo_own, *got, middle, out_keep, rows_in),
        [like((rows, width), BF16), like((cut, 4 * local), F32), like((cut, width), F32)]
        + [like((cut, width), BF16)] * (outer - 1),
    )
    grad_w_output = grad_w_output + sum(
        swap(value, "z", k + 1).astype(F32) for k, value in enumerate(away)
    )

    last, send = head_grads(scal, after(dall, got[0]), norm_one, norm_raw, wt, sums, heads, seq)
    last = last + swap(send, "batch").astype(F32)
    last = after(last.astype(BF16), d_rows, *away)
    other = swap(after(jnp.concatenate(wq), dall), "batch")
    grad_tokens = once(
        "last",
        functools.partial(last_kernel, heads),
        (scal, d_rows, *wq, other, token, d_middle, rows_in),
        [like((rows, width), F32)],
        [pltpu.VMEM((width, rows), F32)],
    )[0]
    last = lax.all_to_all(last, SEQ, split_axis=0, concat_axis=0, tiled=True)
    mat = like((cut, width), F32)
    grad_w_query, grad_w_key, grad_w_value, vec = once(
        "unpack",
        functools.partial(unpack_kernel, heads),
        (last,),
        [mat, mat, mat, like((8, cut), F32)],
    )
    return (
        layer_out[None],
        grad_tokens[None],
        vec[0],
        vec[1],
        grad_w_query,
        vec[2],
        grad_w_key,
        grad_w_value,
        vec[3],
        grad_w_output,
        vec[4],
        vec[5],
        vec[6],
        grad_w_up,
        bias[0],
        grad_w_down,
        vec[7],
    )


def over_rows(left, right):
    return lax.dot_general(
        left, right, (((0,), (0,)), ((), ())), preferred_element_type=jnp.float32
    )


def over_cols(left, right):
    return lax.dot_general(
        left, right, (((1,), (1,)), ((), ())), preferred_element_type=jnp.float32
    )


def pair_scores(q_part, k_part, row_ids, col_ids, prefix):
    scores = jnp.einsum("qhd,khd->hqk", q_part, k_part, preferred_element_type=jnp.float32) * 0.125
    allowed = (col_ids[None, :] <= row_ids[:, None]) | (col_ids[None, :] < prefix)
    return (jnp.where(allowed[None], scores, -1e30), allowed)


def grad_terms(q_part, do_part, lse_part, delta_part, k_part, v_part, row_ids, col_ids, prefix):
    scores, allowed = pair_scores(q_part, k_part, row_ids, col_ids, prefix)
    attn_prob = jnp.where(allowed[None], jnp.exp(scores - lse_part[:, :, None]), 0.0)
    prob_low = attn_prob.astype(jnp.bfloat16)
    d_prob = jnp.einsum("qhd,khd->hqk", do_part, v_part, preferred_element_type=jnp.float32)
    d_score = (attn_prob * (d_prob - delta_part[:, :, None])).astype(jnp.bfloat16)
    return (prob_low, d_score)


def plain_body(
    tokens,
    cotangent,
    prefix_len,
    gain_one,
    shift_one,
    w_query,
    b_query,
    w_key,
    w_value,
    b_value,
    w_output,
    b_output,
    gain_two,
    shift_two,
    w_up,
    b_up,
    w_down,
    b_down,
):
    shards = (
        gain_one,
        shift_one,
        w_query,
        b_query,
        w_key,
        w_value,
        b_value,
        w_output,
        b_output,
        gain_two,
        shift_two,
        w_up,
        b_up,
        w_down,
        b_down,
    )
    gathered = (
        lax.all_gather(shards[0], ("seq", "batch"), axis=0, tiled=True),
        lax.all_gather(shards[1], ("seq", "batch"), axis=0, tiled=True),
        lax.all_gather(shards[2], ("seq", "batch"), axis=0, tiled=True),
        lax.all_gather(shards[3], ("seq", "batch"), axis=0, tiled=True),
        lax.all_gather(shards[4], ("seq", "batch"), axis=0, tiled=True),
        lax.all_gather(shards[5], ("seq", "batch"), axis=0, tiled=True),
        lax.all_gather(shards[6], ("seq", "batch"), axis=0, tiled=True),
        lax.all_gather(shards[7], ("seq", "batch"), axis=0, tiled=True),
        lax.all_gather(shards[8], ("seq", "batch"), axis=0, tiled=True),
        lax.all_gather(shards[9], ("seq", "batch"), axis=0, tiled=True),
        lax.all_gather(shards[10], ("seq", "batch"), axis=0, tiled=True),
        lax.all_gather(shards[11], ("seq", "batch"), axis=0, tiled=True),
        lax.all_gather(shards[12], ("seq", "batch"), axis=0, tiled=True),
        lax.all_gather(shards[13], ("seq", "batch"), axis=0, tiled=True),
        lax.all_gather(shards[14], ("seq", "batch"), axis=0, tiled=True),
    )
    (
        ga_full,
        sa_full,
        wq_full,
        bq_full,
        wk_full,
        wv_full,
        bv_full,
        wo_full,
        bo_full,
        gb_full,
        sb_full,
        wu_full,
        bu_full,
        wd_full,
        bd_full,
    ) = gathered
    hidden = tokens[0].astype(jnp.float32)
    local_rows = hidden.shape[0]
    width = hidden.shape[1]
    heads = width // HD
    prefix = prefix_len[0]
    start_row = lax.axis_index("seq") * local_rows
    last_row = start_row + local_rows - 1
    length = local_rows * lax.axis_size("seq")
    block_rows = min(512, length)
    block_count = length // block_rows
    row_ids = start_row + jnp.arange(local_rows, dtype=jnp.int32)
    block_ids = jnp.arange(block_count, dtype=jnp.int32)
    normed_one, factor_one = normalize(hidden)
    norm_one = (normed_one * ga_full.astype(jnp.float32) + sa_full.astype(jnp.float32)).astype(
        jnp.bfloat16
    )
    q_low = (
        jnp.dot(norm_one, wq_full, preferred_element_type=jnp.float32) + bq_full.astype(jnp.float32)
    ).astype(jnp.bfloat16)
    k_low = jnp.dot(norm_one, wk_full, preferred_element_type=jnp.float32).astype(jnp.bfloat16)
    v_low = (
        jnp.dot(norm_one, wv_full, preferred_element_type=jnp.float32) + bv_full.astype(jnp.float32)
    ).astype(jnp.bfloat16)
    k_all, v_all = (
        lax.all_gather(k_low, "seq", axis=0, tiled=True),
        lax.all_gather(v_low, "seq", axis=0, tiled=True),
    )
    q_heads = q_low.reshape(local_rows, heads, HD)

    def lse_step(state, item):
        k_part, index = item
        col_ids = index * block_rows + jnp.arange(block_rows, dtype=jnp.int32)

        def lse_update(current):
            scores, allowed = pair_scores(q_heads, k_part, row_ids, col_ids, prefix)
            new_top = jnp.maximum(current[0], jnp.max(scores, axis=-1))
            total = current[1] * jnp.exp(current[0] - new_top) + jnp.sum(
                jnp.exp(scores - new_top[:, :, None]), axis=-1
            )
            return (new_top, total)

        needed = (index * block_rows <= last_row) | (index * block_rows < prefix)
        return (lax.cond(needed, lse_update, lambda current: current, state), None)

    k_blocks = k_all.reshape(block_count, block_rows, heads, HD)
    v_blocks = v_all.reshape(block_count, block_rows, heads, HD)
    lse_start = (
        jnp.full((heads, local_rows), -1e30, jnp.float32),
        jnp.zeros((heads, local_rows), jnp.float32),
    )
    (top_all, total_all), _ = lax.scan(lse_step, lse_start, (k_blocks, block_ids))
    lse = top_all + jnp.log(total_all)

    def out_step(acc, item):
        k_part, v_part, index = item
        col_ids = index * block_rows + jnp.arange(block_rows, dtype=jnp.int32)

        def out_update(current):
            scores, allowed = pair_scores(q_heads, k_part, row_ids, col_ids, prefix)
            attn_prob = jnp.where(allowed[None], jnp.exp(scores - lse[:, :, None]), 0.0).astype(
                jnp.bfloat16
            )
            return current + jnp.einsum(
                "hqk,khd->qhd", attn_prob, v_part, preferred_element_type=jnp.float32
            )

        needed = (index * block_rows <= last_row) | (index * block_rows < prefix)
        return (lax.cond(needed, out_update, lambda current: current, acc), None)

    ctx_acc, _ = lax.scan(
        out_step, jnp.zeros((local_rows, heads, HD), jnp.float32), (k_blocks, v_blocks, block_ids)
    )
    ctx_low = ctx_acc.reshape(local_rows, width).astype(jnp.bfloat16)
    middle = (
        hidden
        + jnp.dot(ctx_low, wo_full, preferred_element_type=jnp.float32)
        + bo_full.astype(jnp.float32)
    )
    normed_two, factor_two = normalize(middle)
    norm_two = (normed_two * gb_full.astype(jnp.float32) + sb_full.astype(jnp.float32)).astype(
        jnp.bfloat16
    )
    pre_act = jnp.dot(norm_two, wu_full, preferred_element_type=jnp.float32) + bu_full.astype(
        jnp.float32
    )
    cdf_part = 0.5 * (1.0 + jax.scipy.special.erf(pre_act * 0.7071067811865476))
    act_low = (pre_act * cdf_part).astype(jnp.bfloat16)
    layer_out = (
        middle
        + jnp.dot(act_low, wd_full, preferred_element_type=jnp.float32)
        + bd_full.astype(jnp.float32)
    ).astype(jnp.bfloat16)
    regathered = (
        lax.all_gather(shards[0], ("seq", "batch"), axis=0, tiled=True),
        lax.all_gather(shards[1], ("seq", "batch"), axis=0, tiled=True),
        lax.all_gather(shards[2], ("seq", "batch"), axis=0, tiled=True),
        lax.all_gather(shards[3], ("seq", "batch"), axis=0, tiled=True),
        lax.all_gather(shards[4], ("seq", "batch"), axis=0, tiled=True),
        lax.all_gather(shards[5], ("seq", "batch"), axis=0, tiled=True),
        lax.all_gather(shards[6], ("seq", "batch"), axis=0, tiled=True),
        lax.all_gather(shards[7], ("seq", "batch"), axis=0, tiled=True),
        lax.all_gather(shards[8], ("seq", "batch"), axis=0, tiled=True),
        lax.all_gather(shards[9], ("seq", "batch"), axis=0, tiled=True),
        lax.all_gather(shards[10], ("seq", "batch"), axis=0, tiled=True),
        lax.all_gather(shards[11], ("seq", "batch"), axis=0, tiled=True),
        lax.all_gather(shards[12], ("seq", "batch"), axis=0, tiled=True),
        lax.all_gather(shards[13], ("seq", "batch"), axis=0, tiled=True),
        lax.all_gather(shards[14], ("seq", "batch"), axis=0, tiled=True),
    )
    (
        ga_back,
        sa_back,
        wq_back,
        bq_back,
        wk_back,
        wv_back,
        bv_back,
        wo_back,
        bo_back,
        gb_back,
        sb_back,
        wu_back,
        bu_back,
        wd_back,
        bd_back,
    ) = regathered
    d_out = cotangent[0]
    grad_wd = over_rows(act_low, d_out)
    grad_bd = jnp.sum(d_out.astype(jnp.float32), axis=0)
    d_act = over_cols(d_out, wd_back)
    slope = cdf_part + pre_act * jnp.exp(-0.5 * pre_act * pre_act) * 0.3989422804014327
    d_pre = (d_act * slope).astype(jnp.bfloat16)
    grad_wu = over_rows(norm_two, d_pre)
    grad_bu = jnp.sum(d_pre.astype(jnp.float32), axis=0)
    d_norm_two = over_cols(d_pre, wu_back)
    d_mid_norm, grad_gb, grad_sb = norm_backward(d_norm_two, normed_two, factor_two, gb_back)
    grad_gb, grad_sb = (grad_gb[0], grad_sb[0])
    d_middle = d_out.astype(jnp.float32) + d_mid_norm
    d_branch = d_middle.astype(jnp.bfloat16)
    grad_wo = over_rows(ctx_low, d_branch)
    grad_bo = jnp.sum(d_branch.astype(jnp.float32), axis=0)
    d_ctx = over_cols(d_branch, wo_back).astype(jnp.bfloat16)
    do_heads = d_ctx.reshape(local_rows, heads, HD)
    delta = jnp.sum(d_ctx.astype(jnp.float32).reshape(local_rows, heads, HD) * ctx_acc, axis=-1).T
    k_back, v_back = (k_blocks, v_blocks)
    zero_heads = jnp.zeros((local_rows, heads, HD), jnp.float32)

    def grad_step(acc, item):
        k_part, v_part, index = item
        col_ids = index * block_rows + jnp.arange(block_rows, dtype=jnp.int32)

        def work(current):
            prob_low, d_score = grad_terms(
                q_heads, do_heads, lse, delta, k_part, v_part, row_ids, col_ids, prefix
            )
            current = current + 0.125 * jnp.einsum(
                "hqk,khd->qhd", d_score, k_part, preferred_element_type=jnp.float32
            )
            d_key = 0.125 * jnp.einsum(
                "hqk,qhd->khd", d_score, q_heads, preferred_element_type=jnp.float32
            )
            d_value = jnp.einsum(
                "hqk,qhd->khd", prob_low, do_heads, preferred_element_type=jnp.float32
            )
            return (current, (d_key, d_value))

        def skip(current):
            empty = jnp.zeros((block_rows, heads, HD), jnp.float32)
            return (current, (empty, empty))

        needed = (index * block_rows <= last_row) | (index * block_rows < prefix)
        return lax.cond(needed, work, skip, acc)

    dq_acc, (dk_blocks, dv_blocks) = lax.scan(grad_step, zero_heads, (k_back, v_back, block_ids))
    dk_local, dv_local = (
        lax.psum_scatter(
            dk_blocks.reshape(length, width).astype(jnp.bfloat16),
            "seq",
            scatter_dimension=0,
            tiled=True,
        ).astype(jnp.float32),
        lax.psum_scatter(
            dv_blocks.reshape(length, width).astype(jnp.bfloat16),
            "seq",
            scatter_dimension=0,
            tiled=True,
        ).astype(jnp.float32),
    )
    dq_low = dq_acc.reshape(local_rows, width).astype(jnp.bfloat16)
    dk_low = dk_local.astype(jnp.bfloat16)
    dv_low = dv_local.astype(jnp.bfloat16)
    grad_wq = over_rows(norm_one, dq_low)
    grad_bq = jnp.sum(dq_low.astype(jnp.float32), axis=0)
    grad_wk = over_rows(norm_one, dk_low)
    grad_wv = over_rows(norm_one, dv_low)
    grad_bv = jnp.sum(dv_low.astype(jnp.float32), axis=0)
    d_norm_one = (
        over_cols(dq_low, wq_back) + over_cols(dk_low, wk_back) + over_cols(dv_low, wv_back)
    )
    d_in_norm, grad_ga, grad_sa = norm_backward(d_norm_one, normed_one, factor_one, ga_back)
    grad_ga, grad_sa = (grad_ga[0], grad_sa[0])
    grad_tokens = d_middle + d_in_norm
    summed = (
        lax.psum_scatter(grad_ga, ("seq", "batch"), scatter_dimension=0, tiled=True),
        lax.psum_scatter(grad_sa, ("seq", "batch"), scatter_dimension=0, tiled=True),
        lax.psum_scatter(grad_wq, ("seq", "batch"), scatter_dimension=0, tiled=True),
        lax.psum_scatter(grad_bq, ("seq", "batch"), scatter_dimension=0, tiled=True),
        lax.psum_scatter(grad_wk, ("seq", "batch"), scatter_dimension=0, tiled=True),
        lax.psum_scatter(grad_wv, ("seq", "batch"), scatter_dimension=0, tiled=True),
        lax.psum_scatter(grad_bv, ("seq", "batch"), scatter_dimension=0, tiled=True),
        lax.psum_scatter(grad_wo, ("seq", "batch"), scatter_dimension=0, tiled=True),
        lax.psum_scatter(grad_bo, ("seq", "batch"), scatter_dimension=0, tiled=True),
        lax.psum_scatter(grad_gb, ("seq", "batch"), scatter_dimension=0, tiled=True),
        lax.psum_scatter(grad_sb, ("seq", "batch"), scatter_dimension=0, tiled=True),
        lax.psum_scatter(grad_wu, ("seq", "batch"), scatter_dimension=0, tiled=True),
        lax.psum_scatter(grad_bu, ("seq", "batch"), scatter_dimension=0, tiled=True),
        lax.psum_scatter(grad_wd, ("seq", "batch"), scatter_dimension=0, tiled=True),
        lax.psum_scatter(grad_bd, ("seq", "batch"), scatter_dimension=0, tiled=True),
    )
    return (
        layer_out[None],
        grad_tokens[None],
        summed[0],
        summed[1],
        summed[2],
        summed[3],
        summed[4],
        summed[5],
        summed[6],
        summed[7],
        summed[8],
        summed[9],
        summed[10],
        summed[11],
        summed[12],
        summed[13],
        summed[14],
    )


def solution(mesh):
    seq, batch = (mesh.shape["seq"], mesh.shape["batch"])
    if batch == 2 and seq == 16:
        fine = Mesh(mesh.devices.reshape(seq // 4, 2, 2, batch), ALL)
        along, run = (SEQ, body)
    else:
        fine, along, run = (mesh, "seq", plain_body)
    every = along + ("batch",) if run is body else ("seq", "batch")
    act, mat, vec = (P("batch", along, None), P(every, None), P(every))
    return jax.shard_map(
        run,
        mesh=fine,
        in_specs=(
            act, act, P("batch"), vec, vec, mat, vec, mat, mat, vec, mat, vec, vec, vec, mat, vec, mat,
            vec,
        ),
        out_specs=(
            act, act, vec, vec, mat, vec, mat, mat, vec, mat, vec, vec, vec, mat, vec, mat, vec,
        ),
        check_vma=False,
    )
```

```python
import functools

import jax
import jax.numpy as jnp
from jax import lax
from jax.experimental import pallas as pl
from jax.experimental.pallas import tpu as pltpu
from jax.sharding import Mesh
from jax.sharding import PartitionSpec as P

HD = 64
EPS = 1e-05
LOG2E = 1.4426950408889634
SEQ = ("z", "y", "x")
ALL = SEQ + ("batch",)
WIDE = 4 * HD
LIMIT = 58
F32 = jnp.float32
BF16 = jnp.bfloat16
NN = ((1,), (0,))
NT = ((1,), (1,))
TN = ((0,), (0,))


def normalize(values):
    centre = jnp.mean(values, axis=-1, keepdims=True)
    centred = values - centre
    spread = jnp.mean(centred * centred, axis=-1, keepdims=True)
    factor = lax.rsqrt(spread + EPS)
    return (centred * factor, factor)


def norm_backward(grad_out, normed, factor, gain):
    grad_gain = jnp.sum(grad_out * normed, axis=0, keepdims=True)
    grad_shift = jnp.sum(grad_out, axis=0, keepdims=True)
    scaled = grad_out * gain.astype(F32)
    grad_in = factor * (
        scaled
        - jnp.mean(scaled, axis=-1, keepdims=True)
        - normed * jnp.mean(scaled * normed, axis=-1, keepdims=True)
    )
    return (grad_in, grad_gain, grad_shift)


def dot(left, right, dims=NN):
    return lax.dot_general(left, right, (dims, ((), ())), preferred_element_type=F32)


def swap(value, axis, step=1):
    size = lax.axis_size(axis)
    return lax.ppermute(value, axis, [(i, i ^ step) for i in range(size)])


def swap_plane(value, step):
    return lax.ppermute(value, ("y", "x"), [(i, i ^ step) for i in range(4)])


def after(value, *others):
    return lax.optimization_barrier((value,) + others)[0]


def split(length):
    return 512 if length % 512 == 0 else length


SMALL = pl.CostEstimate(flops=1, bytes_accessed=1, transcendentals=0)
SMEM_SPEC = pl.BlockSpec(memory_space=pltpu.SMEM)
HBM_SPEC = pl.BlockSpec(memory_space=pltpu.HBM)


def full_block(shape):
    zeros = (0,) * len(shape)
    return pl.BlockSpec(shape, lambda i: zeros, pipeline_mode=pl.Buffered(1))


def like(shape, dtype):
    return jax.ShapeDtypeStruct(shape, dtype)


def once(name, kernel, args, outs, scratch=(), limit=LIMIT, left=()):
    in_specs = [SMEM_SPEC if a.dtype == jnp.int32 else full_block(a.shape) for a in args]
    out_specs = [HBM_SPEC if i in left else full_block(o.shape) for i, o in enumerate(outs)]
    return pl.pallas_call(
        kernel,
        grid=(1,),
        out_shape=tuple(outs),
        in_specs=in_specs,
        out_specs=tuple(out_specs),
        scratch_shapes=list(scratch),
        compiler_params=pltpu.CompilerParams(vmem_limit_bytes=limit << 20),
        cost_estimate=SMALL,
        name=name,
    )(*args)


PLACE, PREFIX, CORE, FLAT, LINE = range(5)


def rank_of(scal, k, d, other):
    line = jnp.bitwise_xor(scal[LINE], k)
    flat = jnp.bitwise_xor(scal[FLAT], d)
    return (line * 4 + flat) * 2 + jnp.bitwise_xor(scal[CORE], other)


def rows_at(index, size):
    return pl.ds(pl.multiple_of(index * size, size), size)


def square_pieces(wq, other):
    outer = other.shape[0] // 4
    for d in range(4):
        for k in range(outer):
            yield (k, d, 0, wq[d].at[k])
            yield (k, d, 1, other.at[d * outer + k])


def pack_kernel(lines, heads, scal, token, w_out, w_up, w_q, w_k, w_v, *refs):
    vectors, (up_own, out_b, out_c, out_d, send) = (refs[:8], refs[8:])
    wide = w_up.shape[1] // (4 * lines)
    rows, cut = (token.shape[0], w_up.shape[0])
    for out in (out_b, out_c, out_d):
        out[:rows, :] = token[...]
        out[rows : rows + cut, :] = w_out[...]
    for z in range(lines):
        pieces = [w_up[:, (z * 4 + t) * wide : (z * 4 + t + 1) * wide] for t in range(4)]
        for k, (out, first) in enumerate(
            ((up_own, 0), (out_b, rows + cut), (out_c, rows + cut), (out_d, rows + cut))
        ):
            target = jnp.bitwise_xor(scal[FLAT], k)
            value = pieces[0]
            for t in range(1, 4):
                value = jnp.where(target == t, pieces[t], value)
            out[first : first + cut, z * wide : (z + 1) * wide] = value
    lane = jnp.concatenate([ref[...].astype(F32) for ref in vectors], axis=0)
    lane = jnp.concatenate([lane, jnp.zeros((8, 2 * HD - cut), F32)], axis=1)
    vec = jnp.concatenate([jnp.transpose(lane)[:cut], jnp.zeros((cut, HD - 8), F32)], axis=1)
    vec = vec.astype(BF16)
    for h in range(send.shape[0]):
        for i, w in enumerate((w_q, w_k, w_v)):
            if h < heads:
                piece = w[:, h * HD : (h + 1) * HD]
            else:
                piece = jnp.zeros((cut, HD), BF16)
            send[h, :, i * HD : (i + 1) * HD] = piece
        send[h, :, 3 * HD :] = vec


def forward_kernel(
    heads, scal, ahead, own_b, own_c, own_d, zc, xc, yc, xya, xyb, w,
    n1_out, n0_out, qkvt, ctxc, ctxt, lse, rows_out, wt_out, wo_out,
    n1, n0, k_s, w_s, sems,
):
    place, prefix = (scal[PLACE], scal[PREFIX])
    outer = zc.shape[0] + 1
    length, width = n1.shape
    rows = length // (4 * outer)
    cut = w.shape[2]
    blk = split(length)
    copies = []
    near = ((ahead, 0), (own_b, 1), (own_c, 2), (own_d, 3))
    along = ((zc, 1, 0), (xc, 1, 1), (yc, 1, 2), (xya, 1, 3), (xyb, outer // 2 + 1, 3))
    for src, d in near:
        pair = (src.at[rows : rows + cut, :], wo_out.at[d * outer])
        copies.append(pltpu.make_async_copy(*pair, sems.at[2 + len(copies)]))
    for src, k, d in along:
        target = wo_out.at[d * outer + k : d * outer + k + src.shape[0]]
        copies.append(pltpu.make_async_copy(src.at[:, rows:, :], target, sems.at[2 + len(copies)]))
    for copy in copies:
        copy.start()
    head = jnp.minimum(place, heads - 1)
    for b in range(2):
        for i in range(w.shape[1]):
            at = (2 * i + b) * cut
            w_s[at : at + cut, :] = w[b, i].astype(F32)
    turned = jnp.transpose(w_s[...])
    wt_out[...] = turned[: 3 * HD].astype(BF16)
    rows_in = turned[3 * HD : 3 * HD + 8]
    rows_out[...] = rows_in
    gain = rows_in[0:1]
    shift = rows_in[1:2]

    def norm_rows(value, k, d):
        normed, _ = normalize(value.astype(F32))
        here = rows_at(jnp.bitwise_xor(place, k * 4 + d), rows)
        n0[here, :] = normed.astype(BF16)
        n1[here, :] = (normed * gain + shift).astype(BF16)

    for src, d in near:
        norm_rows(src[:rows, :], 0, d)
    for src, first, d in along:

        def one(k, carry, src=src, first=first, d=d):
            norm_rows(src[k, :rows, :], first + k, d)
            return carry

        lax.fori_loop(0, src.shape[0], one, 0)
    for i, (src, dst) in enumerate(((n1, n1_out), (n0, n0_out))):
        copy = pltpu.make_async_copy(src, dst, sems.at[i])
        copy.start()
        copies.append(copy)
    bias_q = w_s[rows_at(head, HD), 3 * HD + 2 : 3 * HD + 3]
    bias_v = w_s[rows_at(head, HD), 3 * HD + 3 : 3 * HD + 4]
    for i in range(length // blk):
        sl = slice(i * blk, (i + 1) * blk)
        part = dot(wt_out[...], n1[sl, :], NT)
        k_part = part[HD : 2 * HD].astype(BF16)
        qkvt[:HD, sl] = (part[:HD] + bias_q).astype(BF16)
        qkvt[HD : 2 * HD, sl] = k_part
        qkvt[2 * HD :, sl] = (part[2 * HD :] + bias_v).astype(BF16)
        k_s[sl, :] = jnp.transpose(k_part.astype(F32)).astype(BF16)
    scale = 0.125 * LOG2E

    def one_query(i, carry):
        first = pl.multiple_of(i * blk, blk)
        q_now = qkvt[:HD, pl.ds(first, blk)]

        def step(masked, j, state):
            top, total, acc = state
            start = pl.multiple_of(j * blk, blk)
            scores = dot(k_s[pl.ds(start, blk), :], q_now) * scale
            if masked:
                key = start + lax.broadcasted_iota(jnp.int32, (blk, blk), 0)
                query = first + lax.broadcasted_iota(jnp.int32, (blk, blk), 1)
                scores = jnp.where((key <= query) | (key < prefix), scores, -1e30)
            new_top = jnp.maximum(top, jnp.max(scores, axis=0, keepdims=True))
            prob = jnp.exp2(scores - new_top)
            fade = jnp.exp2(top - new_top)
            total = total * fade + jnp.sum(prob, axis=0, keepdims=True)
            acc = acc * fade + dot(qkvt[2 * HD :, pl.ds(start, blk)], prob.astype(BF16))
            return (new_top, total, acc)

        state = (
            jnp.full((1, blk), -1e30, F32),
            jnp.zeros((1, blk), F32),
            jnp.zeros((HD, blk), F32),
        )
        full = jnp.maximum(prefix // blk, i)
        needed = jnp.maximum((prefix + blk - 1) // blk, i + 1)
        state = lax.fori_loop(0, full, functools.partial(step, False), state)
        top, total, acc = lax.fori_loop(full, needed, functools.partial(step, True), state)
        out = acc / total
        ctxt[:, pl.ds(first, blk)] = out
        lse[:, pl.ds(first, blk)] = top + jnp.log2(total)
        for r in range(blk // rows):
            ctxc[i * (blk // rows) + r] = out[:, r * rows : (r + 1) * rows].astype(BF16)
        return carry

    lax.fori_loop(0, length // blk, one_query, 0)
    for copy in copies:
        copy.wait()


def backward_kernel(
    scal, qkvt, dcr, ctxt, lse, dchunk, dall, q_s, k_s, v_s, dc_s, dct_s, del_s, dq_s, dk_s, dv_s
):
    prefix = scal[PREFIX]
    rows = dcr.shape[2]
    length = qkvt.shape[1]
    blk = split(length)
    count = length // blk
    for i in range(count):
        sl = slice(i * blk, (i + 1) * blk)
        turned = jnp.transpose(qkvt[:, sl].astype(F32)).astype(BF16)
        q_s[sl, :] = turned[:, :HD]
        k_s[sl, :] = turned[:, HD : 2 * HD]
        v_s[sl, :] = turned[:, 2 * HD :]
    for i in range(length // rows):
        sl = slice(i * rows, (i + 1) * rows)
        dct_s[:, sl] = dcr[i]
        dc_s[sl, :] = jnp.transpose(dcr[i].astype(F32)).astype(BF16)
    del_s[...] = jnp.sum(dct_s[...].astype(F32) * ctxt[...], axis=0, keepdims=True)
    dq_s[...] = jnp.zeros_like(dq_s)
    scale = 0.125 * LOG2E

    def one_key(j, carry):
        start = pl.multiple_of(j * blk, blk)
        dk_s[...] = jnp.zeros_like(dk_s)
        dv_s[...] = jnp.zeros_like(dv_s)

        def step(masked, i, inner):
            first = pl.multiple_of(i * blk, blk)
            here = pl.ds(first, blk)
            scores = dot(k_s[pl.ds(start, blk), :], qkvt[:HD, here]) * scale
            prob = jnp.exp2(scores - lse[:, here])
            if masked:
                key = start + lax.broadcasted_iota(jnp.int32, (blk, blk), 0)
                query = first + lax.broadcasted_iota(jnp.int32, (blk, blk), 1)
                prob = jnp.where((key <= query) | (key < prefix), prob, 0.0)
            d_prob = dot(v_s[pl.ds(start, blk), :], dct_s[:, here])
            d_score = (prob * (d_prob - del_s[:, here])).astype(BF16)
            dv_s[...] += dot(prob.astype(BF16), dc_s[here, :])
            dk_s[...] += dot(d_score, q_s[here, :])
            dq_s[:, here] += dot(qkvt[HD : 2 * HD, pl.ds(start, blk)], d_score)
            return inner

        begin = jnp.where(start < prefix, 0, j)
        middle = jnp.where(start + blk <= prefix, begin, j + 1)
        lax.fori_loop(begin, middle, functools.partial(step, True), 0)
        lax.fori_loop(middle, count, functools.partial(step, False), 0)
        d_key = jnp.transpose(dk_s[...] * 0.125).astype(BF16)
        d_value = jnp.transpose(dv_s[...]).astype(BF16)
        dall[HD : 2 * HD, pl.ds(start, blk)] = d_key
        dall[2 * HD :, pl.ds(start, blk)] = d_value
        for r in range(blk // rows):
            at = j * (blk // rows) + r
            dchunk[at, HD : 2 * HD, :] = d_key[:, r * rows : (r + 1) * rows]
            dchunk[at, 2 * HD :, :] = d_value[:, r * rows : (r + 1) * rows]
        return carry

    lax.fori_loop(0, count, one_key, 0)
    for i in range(count):
        sl = slice(i * blk, (i + 1) * blk)
        d_query = (dq_s[:, sl] * 0.125).astype(BF16)
        dall[:HD, sl] = d_query
        for r in range(blk // rows):
            dchunk[i * (blk // rows) + r, :HD, :] = d_query[:, r * rows : (r + 1) * rows]


def stacked(pieces, first, last):
    return jnp.concatenate([piece[first:last, :].astype(F32) for piece in pieces]).astype(BF16)


def out_pieces(own, other):
    outer = own.shape[0] // 4
    return [
        (i % outer, i // outer, core, ref.at[i])
        for core, ref in ((0, own), (1, other))
        for i in range(own.shape[0])
    ]


def middle_kernel(heads, scal, ctx, own, other, token, rows_in, middle, norm_two, plain, moved):
    pieces = out_pieces(own, other)
    cut = own.shape[1]
    plain[...] = ctx[:heads].reshape(plain.shape).astype(F32)
    for n, (k, d, core, _) in enumerate(pieces):
        moved[n * cut : (n + 1) * cut, :] = plain[rows_at(rank_of(scal, k, d, core), cut), :]
    turned = jnp.transpose(moved[...]).astype(BF16)
    product = dot(turned, stacked([p[3] for p in pieces], 0, cut))
    value = token[...].astype(F32) + product + rows_in[4:5, :]
    middle[...] = value
    normed, _ = normalize(value)
    norm_two[...] = (normed * rows_in[5:6, :] + rows_in[6:7, :]).astype(BF16)


def feed_kernel(
    scal, n2_a, n2_b, n2_c, n2_d, dy_a, dy_b, dy_c, dy_d, ffz, ffc,
    out_keep, out_b, out_c, out_d, dn_keep, dn_b, dn_c, dn_d, send, keep,
    n2, dy, down, up, act, d_pre, down_s, up_s, bias,
):
    outer = ffz.shape[0]
    cut = (ffz.shape[1] - 8) // 8
    half = 4 * cut
    order = (0, 2, 1, 3)
    sources = [
        (src.at[i], k, core) for core, src in ((0, ffz), (1, ffc)) for i, k in enumerate(order)
    ]

    def block_of(k, core):
        line = jnp.bitwise_xor(scal[LINE], k)
        return line * 2 + jnp.bitwise_xor(scal[CORE], core)

    rows = []
    for src, k, core in sources:
        down[rows_at(block_of(k, core), half), :] = src[:half, :]
        for d in range(4):
            here = rows_at(rank_of(scal, k, d, core), cut)
            up_s[here, :] = src[half + d * cut : half + (d + 1) * cut, :].astype(F32)
        rows.append((block_of(k, core), src[2 * half :, :half].astype(F32)[:1]))
    up[...] = up_s[...].astype(BF16)
    for q in range(2 * outer):
        bias[:, q * half : (q + 1) * half] = sum(jnp.where(at == q, row, 0.0) for at, row in rows)
    count = n2_a.shape[0]
    for i, piece in enumerate((n2_a, n2_b, n2_c, n2_d)):
        n2[i * count : (i + 1) * count, :] = piece[...]
    for i, piece in enumerate((dy_a, dy_b, dy_c, dy_d)):
        dy[i * count : (i + 1) * count, :] = piece[piece.shape[0] - count :, :]
    tile = 256
    for c in range(down.shape[0] // tile):
        sl = slice(c * tile, (c + 1) * tile)
        pre = dot(n2[...], up[:, sl]) + bias[:, sl]
        cdf = 0.5 * (1.0 + lax.erf(pre * 0.7071067811865476))
        act[:, sl] = (pre * cdf).astype(BF16)
        slope = cdf + pre * jnp.exp(-0.5 * pre * pre) * 0.3989422804014327
        d_pre[:, sl] = (dot(dy[...], down[sl, :], NT) * slope).astype(BF16)
    back = dot(d_pre[...], up[...], NT)
    for i, ref in enumerate((dn_keep, dn_b, dn_c, dn_d)):
        ref[...] = back[i * count : (i + 1) * count].astype(ref.dtype)
    out = dot(act[...], down[...])
    for i, ref in enumerate((out_keep, out_b, out_c, out_d)):
        ref[...] = out[i * count : (i + 1) * count].astype(ref.dtype)
    down_s[...] = dot(act[...], dy[...], TN)
    up_s[...] = dot(n2[...], d_pre[...], TN)
    total = jnp.sum(d_pre[...].astype(F32), axis=0, keepdims=True)
    width = keep.shape[2]
    for k in range(outer):
        for core, ref in ((0, keep), (1, send)):
            at = block_of(k, core)
            ref[k, :half, :] = down_s[rows_at(at, half), :].astype(ref.dtype)
            for t in range(4):
                line = jnp.bitwise_xor(scal[LINE], k)
                rank = (line * 4 + t) * 2 + jnp.bitwise_xor(scal[CORE], core)
                here = slice(half + t * cut, half + (t + 1) * cut)
                ref[k, here, :] = up_s[rows_at(rank, cut), :].astype(ref.dtype)
            part = sum(
                jnp.where(at == q, total[:, q * half : (q + 1) * half], 0.0)
                for q in range(2 * outer)
            )
            part = jnp.concatenate([part, jnp.zeros((1, width - half), F32)], axis=1)
            ref[k, 2 * half :, :] = jnp.broadcast_to(part, (8, width)).astype(ref.dtype)


def turn_kernel(
    heads, scal, keep, got_b, got_c, got_d, middle, d_out, own, other, rows_in, ctx,
    d_middle, d_branch_out, d_ctx, sums, wo_keep, wo_send, plain, full,
):
    d_norm = keep[...] + (got_b[...].astype(F32) + got_c[...].astype(F32)) + got_d[...].astype(F32)
    normed, factor = normalize(middle[...])
    grad_in, grad_gain, grad_shift = norm_backward(d_norm, normed, factor, rows_in[5:6, :])
    grad_up = d_out[...].astype(F32)
    total = grad_up + grad_in
    low = total.astype(BF16)
    d_middle[...] = total
    d_branch_out[...] = low[:8]
    pieces = out_pieces(own, other)
    cut = own.shape[1]
    back = dot(stacked([p[3] for p in pieces], 0, cut), low, NT)
    for n, (k, d, core, _) in enumerate(pieces):
        plain[rows_at(rank_of(scal, k, d, core), cut), :] = back[n * cut : (n + 1) * cut]
    seq, rows = (d_ctx.shape[0], d_ctx.shape[2])
    d_ctx[:heads] = plain[...].astype(BF16).reshape(heads, HD, rows)
    d_ctx[heads:] = jnp.zeros((seq - heads, HD, rows), BF16)
    sums[0:1, :] = jnp.sum(low.astype(F32), axis=0, keepdims=True)
    sums[1:2, :] = grad_gain
    sums[2:3, :] = grad_shift
    sums[3:4, :] = jnp.sum(grad_up, axis=0, keepdims=True)
    sums[4:, :] = jnp.zeros((4, sums.shape[1]), F32)
    full[...] = dot(ctx[:heads].reshape(heads * HD, rows), low).reshape(full.shape)
    for i in range(seq):
        wo_keep[i] = full[2 * i + scal[CORE]]
        wo_send[i] = full[2 * i + 1 - scal[CORE]].astype(BF16)


def fold_kernel(keep, got, own, *away):
    for k, ref in enumerate((own,) + away):
        ref[...] = (keep[k] + got[k].astype(F32)).astype(ref.dtype)


def finish_kernel(scal, keep, *refs):
    got, (wo_keep, wo_got, out_b, out_c, out_d), outs = (refs[:-13], refs[-13:-8], refs[-8:])
    grad_down, bias, own, wo_own, away_b, away_c, away_d, total = outs
    value = keep[...]
    for ref in got:
        value = value + ref[...].astype(F32)
    total[...] = value
    half = grad_down.shape[0]
    cut = half // 4
    lines = wo_own.shape[0]
    grad_down[...] = value[:half]
    bias[...] = value[2 * half : 2 * half + 1, :half]
    for k, ref in enumerate((own, away_b, away_c, away_d)):
        at = jnp.bitwise_xor(scal[FLAT], k)
        here = pl.ds(pl.multiple_of(half + at * cut, 8), cut)
        ref[:cut, :] = total[here, :].astype(BF16)
        for z in range(lines):
            part = wo_keep[4 * z + at] + wo_got[4 * z + at].astype(F32)
            if k:
                ref[(1 + z) * cut : (2 + z) * cut, :] = part.astype(BF16)
            else:
                wo_own[z] = part
    for src, ref in ((out_b, away_b), (out_c, away_c), (out_d, away_d)):
        ref[(1 + lines) * cut :, :] = src[...]


def close_kernel(
    lines, scal, own, wo_own, got_b, got_c, got_d, middle, out_keep, rows_in,
    layer_out, grad_up, grad_out, *away,
):
    cut = grad_out.shape[0]
    got = (got_b, got_c, got_d)
    value = middle[...] + out_keep[...] + rows_in[7:8, :]
    pieces = [own[...].astype(F32)]
    for ref in got:
        value = value + ref[(1 + lines) * cut :, :].astype(F32)
        pieces.append(ref[:cut, :].astype(F32))
    layer_out[...] = value.astype(BF16)
    for k, out in enumerate((grad_out,) + away):
        at = jnp.bitwise_xor(scal[LINE], k)
        here = pl.ds(pl.multiple_of((1 + at) * cut, 8), cut)
        part = wo_own[at]
        for ref in got:
            part = part + ref[here, :].astype(F32)
        out[...] = part.astype(out.dtype)
    wide = own.shape[1] // lines
    for t in range(4):
        step = jnp.bitwise_xor(scal[FLAT], t)
        piece = pieces[0]
        for k in range(1, 4):
            piece = jnp.where(step == k, pieces[k], piece)
        for z in range(lines):
            at = (z * 4 + t) * wide
            grad_up[:, at : at + wide] = piece[:, z * wide : (z + 1) * wide]


def heads_kernel(heads, scal, dall, n1, n0, wt, sums, keep, send, gh, gm, cs, full):
    step = pl.program_id(0)

    @pl.when(step == 0)
    def _():
        gh[...] = jnp.zeros_like(gh)
        gm[...] = jnp.zeros_like(gm)
        cs[...] = jnp.zeros_like(cs)

    gh[...] += dot(dall[...], n1[...])
    gm[...] += dot(dall[...], n0[...])
    cs[...] += dot(dall[...], jnp.ones((dall.shape[1], 2 * HD), BF16))

    @pl.when(step == pl.num_programs(0) - 1)
    def _():
        place = scal[PLACE]
        width = gh.shape[1]
        live = place < heads
        wide = wt[...].astype(F32)
        gain = jnp.where(live, jnp.sum(wide * gm[...], axis=0, keepdims=True), 0.0)
        shift = jnp.where(live, jnp.sum(wide * cs[:, :1], axis=0, keepdims=True), 0.0)
        line = jnp.transpose(cs[...])[0:1]
        mine = lax.broadcasted_iota(jnp.int32, (1, width), 1) // HD == place
        b_q = jnp.where(mine, jnp.concatenate([line[:, :HD]] * heads, axis=1), 0.0)
        b_v = jnp.where(mine, jnp.concatenate([line[:, 2 * HD :]] * heads, axis=1), 0.0)
        vec = jnp.concatenate([gain, shift, b_q, b_v, sums[:4, :]], axis=0)
        pad = jnp.zeros((width, HD - 8), F32)
        block = jnp.concatenate([jnp.transpose(gh[...]), jnp.transpose(vec), pad], axis=1)
        full[...] = block.reshape(full.shape)
        for i in range(keep.shape[0]):
            keep[i] = full[2 * i + scal[CORE]]
            send[i] = full[2 * i + 1 - scal[CORE]].astype(BF16)


def head_grads(scal, dall, n1, n0, wt, sums, heads, seq):
    length, width = n1.shape
    blk = split(length)
    cut = width // (2 * seq)
    outs = (like((seq, cut, WIDE), F32), like((seq, cut, WIDE), BF16))
    return pl.pallas_call(
        functools.partial(heads_kernel, heads),
        out_shape=outs,
        grid=(length // blk,),
        in_specs=[
            SMEM_SPEC,
            pl.BlockSpec((3 * HD, blk), lambda i: (0, i)),
            pl.BlockSpec((blk, width), lambda i: (i, 0)),
            pl.BlockSpec((blk, width), lambda i: (i, 0)),
            full_block(wt.shape),
            full_block(sums.shape),
        ],
        out_specs=tuple(full_block(out.shape) for out in outs),
        scratch_shapes=[
            pltpu.VMEM((3 * HD, width), F32),
            pltpu.VMEM((3 * HD, width), F32),
            pltpu.VMEM((3 * HD, 2 * HD), F32),
            pltpu.VMEM((2 * seq, cut, WIDE), F32),
        ],
        compiler_params=pltpu.CompilerParams(vmem_limit_bytes=LIMIT << 20),
        cost_estimate=SMALL,
        name="heads",
    )(scal, dall, n1, n0, wt, sums)


def last_kernel(
    heads, scal, d_rows, wq_a, wq_b, wq_c, wq_d, other, token, d_middle, rows_in, grad_tokens, plain
):
    cut = other.shape[1] // 3
    pieces = list(square_pieces((wq_a, wq_b, wq_c, wq_d), other))
    total = 0.0
    for i in range(3):
        part = jnp.concatenate(
            [d_rows[h, i * HD : (i + 1) * HD, :].astype(F32) for h in range(heads)], axis=0
        )
        weights = stacked([p[3] for p in pieces], i * cut, (i + 1) * cut)
        total = total + dot(weights, part.astype(BF16))
    for n, (k, d, core, _) in enumerate(pieces):
        plain[rows_at(rank_of(scal, k, d, core), cut), :] = total[n * cut : (n + 1) * cut]
    normed, factor = normalize(token[...].astype(F32))
    grad_in, _, _ = norm_backward(jnp.transpose(plain[...]), normed, factor, rows_in[0:1, :])
    grad_tokens[...] = d_middle[...] + grad_in


def unpack_kernel(heads, got, g_q, g_k, g_v, *vec):
    for i, out in enumerate((g_q, g_k, g_v)):
        for h in range(heads):
            out[:, h * HD : (h + 1) * HD] = got[h, :, i * HD : (i + 1) * HD].astype(F32)
    total = got[0, :, 2 * HD :].astype(F32)
    for s in range(1, got.shape[0]):
        total = total + got[s, :, 2 * HD :].astype(F32)
    cut = total.shape[0]
    total = jnp.concatenate([total, jnp.zeros((2 * HD - cut, 2 * HD), F32)], axis=0)
    total = jnp.transpose(total)
    for i, out in enumerate(vec):
        out[...] = total[HD + i : HD + i + 1, :cut]


def body(
    tokens, cotangent, prefix_len, gain_one, shift_one, w_query, b_query, w_key, w_value, b_value,
    w_output, b_output, gain_two, shift_two, w_up, b_up, w_down, b_down,
):
    outer = lax.axis_size("z")
    seq = 4 * outer
    token, d_out = (tokens[0], cotangent[0])
    rows, width = token.shape
    length = seq * rows
    heads = width // HD
    cut = w_query.shape[0]
    half = w_down.shape[0]
    local = w_up.shape[1] // 4
    flat = lax.axis_index(("y", "x"))
    places = (lax.axis_index(SEQ), prefix_len[0], lax.axis_index("batch"), flat, lax.axis_index("z"))
    scal = jnp.stack(places).astype(jnp.int32)

    ahead = jnp.concatenate([token, w_output])
    zc = jnp.stack([swap(ahead, "z", k) for k in range(1, outer)])
    vectors = (
        gain_one, shift_one, b_query, b_value, b_output, gain_two, shift_two, b_down,
    )
    vectors = [value[None] for value in vectors]
    up_own, *first, send = once(
        "pack",
        functools.partial(pack_kernel, outer, heads),
        (scal, token, w_output, w_up, w_query, w_key, w_value, *vectors),
        [like((cut, local), BF16)]
        + [like((rows + 2 * cut, width), BF16)] * 3
        + [like((seq, cut, WIDE), BF16)],
    )
    first = [swap_plane(part, k + 1) for k, part in enumerate(first)]
    zc = after(zc, *first)
    xc = swap(zc, "x")
    yc = swap(zc, "y")
    head_w = lax.all_to_all(after(send, zc), SEQ, split_axis=0, concat_axis=0, tiled=True)
    wq = after(jnp.concatenate([w_query, w_key, w_value]), zc)
    wq_got = [swap(wq, "z", k) for k in range(1, outer)]
    head_w = lax.all_gather(head_w, "batch", axis=0, tiled=False)
    xc, yc, head_w, wq_got = lax.optimization_barrier((xc, yc, head_w, wq_got))
    xya = swap(xc[: outer // 2], "y")
    xyb = swap(yc[outer // 2 :], "x")

    b_up_row = jnp.pad(b_up[None], ((0, 7), (0, width - half)))
    ff = [w_down, up_own] + [part[rows + cut :] for part in first] + [b_up_row]
    ff = after(jnp.concatenate(ff), head_w, xc)
    ff = jnp.stack([ff, swap(ff, "z", 2)])
    ff_got = swap(ff, "z", 1)
    wq = after(jnp.stack([wq] + wq_got), xya, xyb)
    wq = [wq] + [swap_plane(wq, k) for k in range(1, 4)]

    norm_one, norm_raw, qkvt, ctxc, ctxt, lse, rows_in, wt, w_out_own = once(
        "forward",
        functools.partial(forward_kernel, heads),
        (scal, ahead, *first, zc, xc, yc, xya, xyb, head_w),
        [
            like((length, width), BF16),
            like((length, width), BF16),
            like((3 * HD, length), BF16),
            like((seq, HD, rows), BF16),
            like((HD, length), F32),
            like((1, length), F32),
            like((8, width), F32),
            like((3 * HD, width), BF16),
            like((seq, cut, width), BF16),
        ],
        [
            pltpu.VMEM((length, width), BF16),
            pltpu.VMEM((length, width), BF16),
            pltpu.VMEM((length, HD), BF16),
            pltpu.VMEM((width, WIDE), F32),
            pltpu.SemaphoreType.DMA((11,)),
        ],
        left=(0, 1, 8),
    )
    w_out_other = swap(w_out_own, "batch")
    ctxc, wq, ff_got = lax.optimization_barrier((ctxc, wq, ff_got))
    ffz = jnp.concatenate([ff, ff_got])
    dy = [d_out] + [swap_plane(after(d_out, ctxc), k) for k in range(1, 4)]
    ctx = lax.all_to_all(ctxc, SEQ, split_axis=0, concat_axis=0, tiled=True)
    ffc = swap(ffz, "batch")
    dy, ctx = lax.optimization_barrier((dy, ctx))
    middle, norm_two = once(
        "middle",
        functools.partial(middle_kernel, heads),
        (scal, ctx, w_out_own, w_out_other, token, rows_in),
        [like((rows, width), F32), like((rows, width), BF16)],
        [pltpu.VMEM((width, rows), F32)] * 2,
    )
    n2 = [norm_two] + [swap_plane(norm_two, k) for k in range(1, 4)]

    part = [like((rows, width), F32)] + [like((rows, width), BF16)] * 3
    fed = once(
        "feed",
        feed_kernel,
        (scal, *n2, *dy, ffz, ffc),
        part + part + [like(ffz.shape, BF16), like(ffz.shape, F32)],
        [
            pltpu.VMEM((4 * rows, width), BF16),
            pltpu.VMEM((4 * rows, width), BF16),
            pltpu.VMEM((local, width), BF16),
            pltpu.VMEM((width, local), BF16),
            pltpu.VMEM((4 * rows, local), BF16),
            pltpu.VMEM((4 * rows, local), BF16),
            pltpu.VMEM((local, width), F32),
            pltpu.VMEM((width, local), F32),
            pltpu.VMEM((1, local), F32),
        ],
    )
    out_keep, *out_send = fed[:4]
    dn_keep, *dn_send = fed[4:8]
    send, keep = fed[8:]
    dn_got = [swap_plane(value, k + 1) for k, value in enumerate(dn_send)]

    count = 2 * half + 8
    own, *away = once(
        "fold",
        fold_kernel,
        (keep, swap(send, "batch")),
        [like((count, width), F32)] + [like((count, width), BF16)] * (outer - 1),
    )
    back = [swap(value, "z", k + 1) for k, value in enumerate(away)]
    dn_keep, _ = lax.optimization_barrier((dn_keep, away))
    d_middle, _, d_ctx, sums, wo_keep, wo_send = once(
        "turn",
        functools.partial(turn_kernel, heads),
        (scal, dn_keep, *dn_got, middle, d_out, w_out_own, w_out_other, rows_in, ctx),
        [
            like((rows, width), F32),
            like((8, width), BF16),
            like((seq, HD, rows), BF16),
            like((8, width), F32),
            like((seq, cut, width), F32),
            like((seq, cut, width), BF16),
        ],
        [pltpu.VMEM((width, rows), F32), pltpu.VMEM((2 * seq, cut, width), F32)],
    )
    d_ctx = lax.all_to_all(d_ctx, SEQ, split_axis=0, concat_axis=0, tiled=True)

    wo_got = swap(wo_send, "batch")

    blk = split(length)
    dchunk, dall = once(
        "backward",
        backward_kernel,
        (scal, qkvt, d_ctx, ctxt, lse),
        [like((seq, 3 * HD, rows), BF16), like((3 * HD, length), BF16)],
        [
            pltpu.VMEM((length, HD), BF16),
            pltpu.VMEM((length, HD), BF16),
            pltpu.VMEM((length, HD), BF16),
            pltpu.VMEM((length, HD), BF16),
            pltpu.VMEM((HD, length), BF16),
            pltpu.VMEM((1, length), F32),
            pltpu.VMEM((HD, length), F32),
            pltpu.VMEM((blk, HD), F32),
            pltpu.VMEM((blk, HD), F32),
        ],
    )
    back, dchunk = lax.optimization_barrier((back, dchunk))
    d_rows = lax.all_to_all(dchunk, SEQ, split_axis=0, concat_axis=0, tiled=True)

    grad_w_down, bias, own, wo_own, *away = once(
        "finish",
        finish_kernel,
        (scal, own, *back, wo_keep, wo_got, *out_send),
        [
            like((half, width), F32),
            like((1, half), F32),
            like((cut, width), BF16),
            like((outer, cut, width), F32),
        ]
        + [like(((1 + outer) * cut + rows, width), BF16)] * 3,
        [pltpu.VMEM((count, width), F32)],
    )
    got = [swap_plane(value, k + 1) for k, value in enumerate(away)]
    last, send = head_grads(scal, dall, norm_one, norm_raw, wt, sums, heads, seq)
    last = last + swap(send, "batch").astype(F32)
    last = after(last.astype(BF16), d_rows)
    other = swap(after(jnp.concatenate(wq), dall), "batch")
    grad_tokens = once(
        "last",
        functools.partial(last_kernel, heads),
        (scal, d_rows, *wq, other, token, d_middle, rows_in),
        [like((rows, width), F32)],
        [pltpu.VMEM((width, rows), F32)],
    )[0]
    last = lax.all_to_all(last, SEQ, split_axis=0, concat_axis=0, tiled=True)
    mat = like((cut, width), F32)
    grad_w_query, grad_w_key, grad_w_value, *vec = once(
        "unpack",
        functools.partial(unpack_kernel, heads),
        (last,),
        [mat, mat, mat] + [like((1, cut), F32)] * 8,
    )
    layer_out, grad_w_up, grad_w_output, *away = once(
        "close",
        functools.partial(close_kernel, outer),
        (scal, own, wo_own, *got, after(middle, grad_tokens), out_keep, rows_in),
        [like((rows, width), BF16), like((cut, 4 * local), F32), like((cut, width), F32)]
        + [like((cut, width), BF16)] * (outer - 1),
    )
    grad_w_output = grad_w_output + sum(
        swap(value, "z", k + 1).astype(F32) for k, value in enumerate(away)
    )

    return (
        layer_out[None],
        grad_tokens[None],
        vec[0][0],
        vec[1][0],
        grad_w_query,
        vec[2][0],
        grad_w_key,
        grad_w_value,
        vec[3][0],
        grad_w_output,
        vec[4][0],
        vec[5][0],
        vec[6][0],
        grad_w_up,
        bias[0],
        grad_w_down,
        vec[7][0],
    )


def over_rows(left, right):
    return lax.dot_general(
        left, right, (((0,), (0,)), ((), ())), preferred_element_type=jnp.float32
    )


def over_cols(left, right):
    return lax.dot_general(
        left, right, (((1,), (1,)), ((), ())), preferred_element_type=jnp.float32
    )


def pair_scores(q_part, k_part, row_ids, col_ids, prefix):
    scores = jnp.einsum("qhd,khd->hqk", q_part, k_part, preferred_element_type=jnp.float32) * 0.125
    allowed = (col_ids[None, :] <= row_ids[:, None]) | (col_ids[None, :] < prefix)
    return (jnp.where(allowed[None], scores, -1e30), allowed)


def grad_terms(q_part, do_part, lse_part, delta_part, k_part, v_part, row_ids, col_ids, prefix):
    scores, allowed = pair_scores(q_part, k_part, row_ids, col_ids, prefix)
    attn_prob = jnp.where(allowed[None], jnp.exp(scores - lse_part[:, :, None]), 0.0)
    prob_low = attn_prob.astype(jnp.bfloat16)
    d_prob = jnp.einsum("qhd,khd->hqk", do_part, v_part, preferred_element_type=jnp.float32)
    d_score = (attn_prob * (d_prob - delta_part[:, :, None])).astype(jnp.bfloat16)
    return (prob_low, d_score)


def plain_body(
    tokens,
    cotangent,
    prefix_len,
    gain_one,
    shift_one,
    w_query,
    b_query,
    w_key,
    w_value,
    b_value,
    w_output,
    b_output,
    gain_two,
    shift_two,
    w_up,
    b_up,
    w_down,
    b_down,
):
    shards = (
        gain_one,
        shift_one,
        w_query,
        b_query,
        w_key,
        w_value,
        b_value,
        w_output,
        b_output,
        gain_two,
        shift_two,
        w_up,
        b_up,
        w_down,
        b_down,
    )
    gathered = (
        lax.all_gather(shards[0], ("seq", "batch"), axis=0, tiled=True),
        lax.all_gather(shards[1], ("seq", "batch"), axis=0, tiled=True),
        lax.all_gather(shards[2], ("seq", "batch"), axis=0, tiled=True),
        lax.all_gather(shards[3], ("seq", "batch"), axis=0, tiled=True),
        lax.all_gather(shards[4], ("seq", "batch"), axis=0, tiled=True),
        lax.all_gather(shards[5], ("seq", "batch"), axis=0, tiled=True),
        lax.all_gather(shards[6], ("seq", "batch"), axis=0, tiled=True),
        lax.all_gather(shards[7], ("seq", "batch"), axis=0, tiled=True),
        lax.all_gather(shards[8], ("seq", "batch"), axis=0, tiled=True),
        lax.all_gather(shards[9], ("seq", "batch"), axis=0, tiled=True),
        lax.all_gather(shards[10], ("seq", "batch"), axis=0, tiled=True),
        lax.all_gather(shards[11], ("seq", "batch"), axis=0, tiled=True),
        lax.all_gather(shards[12], ("seq", "batch"), axis=0, tiled=True),
        lax.all_gather(shards[13], ("seq", "batch"), axis=0, tiled=True),
        lax.all_gather(shards[14], ("seq", "batch"), axis=0, tiled=True),
    )
    (
        ga_full,
        sa_full,
        wq_full,
        bq_full,
        wk_full,
        wv_full,
        bv_full,
        wo_full,
        bo_full,
        gb_full,
        sb_full,
        wu_full,
        bu_full,
        wd_full,
        bd_full,
    ) = gathered
    hidden = tokens[0].astype(jnp.float32)
    local_rows = hidden.shape[0]
    width = hidden.shape[1]
    heads = width // HD
    prefix = prefix_len[0]
    start_row = lax.axis_index("seq") * local_rows
    last_row = start_row + local_rows - 1
    length = local_rows * lax.axis_size("seq")
    block_rows = min(512, length)
    block_count = length // block_rows
    row_ids = start_row + jnp.arange(local_rows, dtype=jnp.int32)
    block_ids = jnp.arange(block_count, dtype=jnp.int32)
    normed_one, factor_one = normalize(hidden)
    norm_one = (normed_one * ga_full.astype(jnp.float32) + sa_full.astype(jnp.float32)).astype(
        jnp.bfloat16
    )
    q_low = (
        jnp.dot(norm_one, wq_full, preferred_element_type=jnp.float32) + bq_full.astype(jnp.float32)
    ).astype(jnp.bfloat16)
    k_low = jnp.dot(norm_one, wk_full, preferred_element_type=jnp.float32).astype(jnp.bfloat16)
    v_low = (
        jnp.dot(norm_one, wv_full, preferred_element_type=jnp.float32) + bv_full.astype(jnp.float32)
    ).astype(jnp.bfloat16)
    k_all, v_all = (
        lax.all_gather(k_low, "seq", axis=0, tiled=True),
        lax.all_gather(v_low, "seq", axis=0, tiled=True),
    )
    q_heads = q_low.reshape(local_rows, heads, HD)

    def lse_step(state, item):
        k_part, index = item
        col_ids = index * block_rows + jnp.arange(block_rows, dtype=jnp.int32)

        def lse_update(current):
            scores, allowed = pair_scores(q_heads, k_part, row_ids, col_ids, prefix)
            new_top = jnp.maximum(current[0], jnp.max(scores, axis=-1))
            total = current[1] * jnp.exp(current[0] - new_top) + jnp.sum(
                jnp.exp(scores - new_top[:, :, None]), axis=-1
            )
            return (new_top, total)

        needed = (index * block_rows <= last_row) | (index * block_rows < prefix)
        return (lax.cond(needed, lse_update, lambda current: current, state), None)

    k_blocks = k_all.reshape(block_count, block_rows, heads, HD)
    v_blocks = v_all.reshape(block_count, block_rows, heads, HD)
    lse_start = (
        jnp.full((heads, local_rows), -1e30, jnp.float32),
        jnp.zeros((heads, local_rows), jnp.float32),
    )
    (top_all, total_all), _ = lax.scan(lse_step, lse_start, (k_blocks, block_ids))
    lse = top_all + jnp.log(total_all)

    def out_step(acc, item):
        k_part, v_part, index = item
        col_ids = index * block_rows + jnp.arange(block_rows, dtype=jnp.int32)

        def out_update(current):
            scores, allowed = pair_scores(q_heads, k_part, row_ids, col_ids, prefix)
            attn_prob = jnp.where(allowed[None], jnp.exp(scores - lse[:, :, None]), 0.0).astype(
                jnp.bfloat16
            )
            return current + jnp.einsum(
                "hqk,khd->qhd", attn_prob, v_part, preferred_element_type=jnp.float32
            )

        needed = (index * block_rows <= last_row) | (index * block_rows < prefix)
        return (lax.cond(needed, out_update, lambda current: current, acc), None)

    ctx_acc, _ = lax.scan(
        out_step, jnp.zeros((local_rows, heads, HD), jnp.float32), (k_blocks, v_blocks, block_ids)
    )
    ctx_low = ctx_acc.reshape(local_rows, width).astype(jnp.bfloat16)
    middle = (
        hidden
        + jnp.dot(ctx_low, wo_full, preferred_element_type=jnp.float32)
        + bo_full.astype(jnp.float32)
    )
    normed_two, factor_two = normalize(middle)
    norm_two = (normed_two * gb_full.astype(jnp.float32) + sb_full.astype(jnp.float32)).astype(
        jnp.bfloat16
    )
    pre_act = jnp.dot(norm_two, wu_full, preferred_element_type=jnp.float32) + bu_full.astype(
        jnp.float32
    )
    cdf_part = 0.5 * (1.0 + jax.scipy.special.erf(pre_act * 0.7071067811865476))
    act_low = (pre_act * cdf_part).astype(jnp.bfloat16)
    layer_out = (
        middle
        + jnp.dot(act_low, wd_full, preferred_element_type=jnp.float32)
        + bd_full.astype(jnp.float32)
    ).astype(jnp.bfloat16)
    regathered = (
        lax.all_gather(shards[0], ("seq", "batch"), axis=0, tiled=True),
        lax.all_gather(shards[1], ("seq", "batch"), axis=0, tiled=True),
        lax.all_gather(shards[2], ("seq", "batch"), axis=0, tiled=True),
        lax.all_gather(shards[3], ("seq", "batch"), axis=0, tiled=True),
        lax.all_gather(shards[4], ("seq", "batch"), axis=0, tiled=True),
        lax.all_gather(shards[5], ("seq", "batch"), axis=0, tiled=True),
        lax.all_gather(shards[6], ("seq", "batch"), axis=0, tiled=True),
        lax.all_gather(shards[7], ("seq", "batch"), axis=0, tiled=True),
        lax.all_gather(shards[8], ("seq", "batch"), axis=0, tiled=True),
        lax.all_gather(shards[9], ("seq", "batch"), axis=0, tiled=True),
        lax.all_gather(shards[10], ("seq", "batch"), axis=0, tiled=True),
        lax.all_gather(shards[11], ("seq", "batch"), axis=0, tiled=True),
        lax.all_gather(shards[12], ("seq", "batch"), axis=0, tiled=True),
        lax.all_gather(shards[13], ("seq", "batch"), axis=0, tiled=True),
        lax.all_gather(shards[14], ("seq", "batch"), axis=0, tiled=True),
    )
    (
        ga_back,
        sa_back,
        wq_back,
        bq_back,
        wk_back,
        wv_back,
        bv_back,
        wo_back,
        bo_back,
        gb_back,
        sb_back,
        wu_back,
        bu_back,
        wd_back,
        bd_back,
    ) = regathered
    d_out = cotangent[0]
    grad_wd = over_rows(act_low, d_out)
    grad_bd = jnp.sum(d_out.astype(jnp.float32), axis=0)
    d_act = over_cols(d_out, wd_back)
    slope = cdf_part + pre_act * jnp.exp(-0.5 * pre_act * pre_act) * 0.3989422804014327
    d_pre = (d_act * slope).astype(jnp.bfloat16)
    grad_wu = over_rows(norm_two, d_pre)
    grad_bu = jnp.sum(d_pre.astype(jnp.float32), axis=0)
    d_norm_two = over_cols(d_pre, wu_back)
    d_mid_norm, grad_gb, grad_sb = norm_backward(d_norm_two, normed_two, factor_two, gb_back)
    grad_gb, grad_sb = (grad_gb[0], grad_sb[0])
    d_middle = d_out.astype(jnp.float32) + d_mid_norm
    d_branch = d_middle.astype(jnp.bfloat16)
    grad_wo = over_rows(ctx_low, d_branch)
    grad_bo = jnp.sum(d_branch.astype(jnp.float32), axis=0)
    d_ctx = over_cols(d_branch, wo_back).astype(jnp.bfloat16)
    do_heads = d_ctx.reshape(local_rows, heads, HD)
    delta = jnp.sum(d_ctx.astype(jnp.float32).reshape(local_rows, heads, HD) * ctx_acc, axis=-1).T
    k_back, v_back = (k_blocks, v_blocks)
    zero_heads = jnp.zeros((local_rows, heads, HD), jnp.float32)

    def grad_step(acc, item):
        k_part, v_part, index = item
        col_ids = index * block_rows + jnp.arange(block_rows, dtype=jnp.int32)

        def work(current):
            prob_low, d_score = grad_terms(
                q_heads, do_heads, lse, delta, k_part, v_part, row_ids, col_ids, prefix
            )
            current = current + 0.125 * jnp.einsum(
                "hqk,khd->qhd", d_score, k_part, preferred_element_type=jnp.float32
            )
            d_key = 0.125 * jnp.einsum(
                "hqk,qhd->khd", d_score, q_heads, preferred_element_type=jnp.float32
            )
            d_value = jnp.einsum(
                "hqk,qhd->khd", prob_low, do_heads, preferred_element_type=jnp.float32
            )
            return (current, (d_key, d_value))

        def skip(current):
            empty = jnp.zeros((block_rows, heads, HD), jnp.float32)
            return (current, (empty, empty))

        needed = (index * block_rows <= last_row) | (index * block_rows < prefix)
        return lax.cond(needed, work, skip, acc)

    dq_acc, (dk_blocks, dv_blocks) = lax.scan(grad_step, zero_heads, (k_back, v_back, block_ids))
    dk_local, dv_local = (
        lax.psum_scatter(
            dk_blocks.reshape(length, width).astype(jnp.bfloat16),
            "seq",
            scatter_dimension=0,
            tiled=True,
        ).astype(jnp.float32),
        lax.psum_scatter(
            dv_blocks.reshape(length, width).astype(jnp.bfloat16),
            "seq",
            scatter_dimension=0,
            tiled=True,
        ).astype(jnp.float32),
    )
    dq_low = dq_acc.reshape(local_rows, width).astype(jnp.bfloat16)
    dk_low = dk_local.astype(jnp.bfloat16)
    dv_low = dv_local.astype(jnp.bfloat16)
    grad_wq = over_rows(norm_one, dq_low)
    grad_bq = jnp.sum(dq_low.astype(jnp.float32), axis=0)
    grad_wk = over_rows(norm_one, dk_low)
    grad_wv = over_rows(norm_one, dv_low)
    grad_bv = jnp.sum(dv_low.astype(jnp.float32), axis=0)
    d_norm_one = (
        over_cols(dq_low, wq_back) + over_cols(dk_low, wk_back) + over_cols(dv_low, wv_back)
    )
    d_in_norm, grad_ga, grad_sa = norm_backward(d_norm_one, normed_one, factor_one, ga_back)
    grad_ga, grad_sa = (grad_ga[0], grad_sa[0])
    grad_tokens = d_middle + d_in_norm
    summed = (
        lax.psum_scatter(grad_ga, ("seq", "batch"), scatter_dimension=0, tiled=True),
        lax.psum_scatter(grad_sa, ("seq", "batch"), scatter_dimension=0, tiled=True),
        lax.psum_scatter(grad_wq, ("seq", "batch"), scatter_dimension=0, tiled=True),
        lax.psum_scatter(grad_bq, ("seq", "batch"), scatter_dimension=0, tiled=True),
        lax.psum_scatter(grad_wk, ("seq", "batch"), scatter_dimension=0, tiled=True),
        lax.psum_scatter(grad_wv, ("seq", "batch"), scatter_dimension=0, tiled=True),
        lax.psum_scatter(grad_bv, ("seq", "batch"), scatter_dimension=0, tiled=True),
        lax.psum_scatter(grad_wo, ("seq", "batch"), scatter_dimension=0, tiled=True),
        lax.psum_scatter(grad_bo, ("seq", "batch"), scatter_dimension=0, tiled=True),
        lax.psum_scatter(grad_gb, ("seq", "batch"), scatter_dimension=0, tiled=True),
        lax.psum_scatter(grad_sb, ("seq", "batch"), scatter_dimension=0, tiled=True),
        lax.psum_scatter(grad_wu, ("seq", "batch"), scatter_dimension=0, tiled=True),
        lax.psum_scatter(grad_bu, ("seq", "batch"), scatter_dimension=0, tiled=True),
        lax.psum_scatter(grad_wd, ("seq", "batch"), scatter_dimension=0, tiled=True),
        lax.psum_scatter(grad_bd, ("seq", "batch"), scatter_dimension=0, tiled=True),
    )
    return (
        layer_out[None],
        grad_tokens[None],
        summed[0],
        summed[1],
        summed[2],
        summed[3],
        summed[4],
        summed[5],
        summed[6],
        summed[7],
        summed[8],
        summed[9],
        summed[10],
        summed[11],
        summed[12],
        summed[13],
        summed[14],
    )


def solution(mesh):
    seq, batch = (mesh.shape["seq"], mesh.shape["batch"])
    if batch == 2 and seq == 16:
        fine = Mesh(mesh.devices.reshape(seq // 4, 2, 2, batch), ALL)
        along, run = (SEQ, body)
    else:
        fine, along, run = (mesh, "seq", plain_body)
    every = along + ("batch",) if run is body else ("seq", "batch")
    act, mat, vec = (P("batch", along, None), P(every, None), P(every))
    return jax.shard_map(
        run,
        mesh=fine,
        in_specs=(
            act, act, P("batch"), vec, vec, mat, vec, mat, mat, vec, mat, vec, vec, vec, mat, vec, mat,
            vec,
        ),
        out_specs=(
            act, act, vec, vec, mat, vec, mat, mat, vec, mat, vec, vec, vec, mat, vec, mat, vec,
        ),
        check_vma=False,
    )
```

```python
import functools

import jax
import jax.numpy as jnp
from jax import lax
from jax.experimental import pallas as pl
from jax.experimental.pallas import tpu as pltpu
from jax.sharding import Mesh
from jax.sharding import PartitionSpec as P

HD = 64
EPS = 1e-05
LOG2E = 1.4426950408889634
SEQ = ("z", "y", "x")
ALL = SEQ + ("batch",)
WIDE = 4 * HD
LIMIT = 58
F32 = jnp.float32
BF16 = jnp.bfloat16
NN = ((1,), (0,))
NT = ((1,), (1,))
TN = ((0,), (0,))


def normalize(values):
    centre = jnp.mean(values, axis=-1, keepdims=True)
    centred = values - centre
    spread = jnp.mean(centred * centred, axis=-1, keepdims=True)
    factor = lax.rsqrt(spread + EPS)
    return (centred * factor, factor)


def norm_backward(grad_out, normed, factor, gain):
    grad_gain = jnp.sum(grad_out * normed, axis=0, keepdims=True)
    grad_shift = jnp.sum(grad_out, axis=0, keepdims=True)
    scaled = grad_out * gain.astype(F32)
    grad_in = factor * (
        scaled
        - jnp.mean(scaled, axis=-1, keepdims=True)
        - normed * jnp.mean(scaled * normed, axis=-1, keepdims=True)
    )
    return (grad_in, grad_gain, grad_shift)


def dot(left, right, dims=NN):
    return lax.dot_general(left, right, (dims, ((), ())), preferred_element_type=F32)


def swap(value, axis, step=1):
    size = lax.axis_size(axis)
    return lax.ppermute(value, axis, [(i, i ^ step) for i in range(size)])


def swap_plane(value, step):
    return lax.ppermute(value, ("y", "x"), [(i, i ^ step) for i in range(4)])


def after(value, *others):
    return lax.optimization_barrier((value,) + others)[0]


def split(length):
    return 512 if length % 512 == 0 else length


SMALL = pl.CostEstimate(flops=1, bytes_accessed=1, transcendentals=0)
SMEM_SPEC = pl.BlockSpec(memory_space=pltpu.SMEM)
HBM_SPEC = pl.BlockSpec(memory_space=pltpu.HBM)


def full_block(shape):
    zeros = (0,) * len(shape)
    return pl.BlockSpec(shape, lambda i: zeros, pipeline_mode=pl.Buffered(1))


def like(shape, dtype):
    return jax.ShapeDtypeStruct(shape, dtype)


def once(name, kernel, args, outs, scratch=(), limit=LIMIT, left=()):
    in_specs = [SMEM_SPEC if a.dtype == jnp.int32 else full_block(a.shape) for a in args]
    out_specs = [HBM_SPEC if i in left else full_block(o.shape) for i, o in enumerate(outs)]
    return pl.pallas_call(
        kernel,
        grid=(1,),
        out_shape=tuple(outs),
        in_specs=in_specs,
        out_specs=tuple(out_specs),
        scratch_shapes=list(scratch),
        compiler_params=pltpu.CompilerParams(vmem_limit_bytes=limit << 20),
        cost_estimate=SMALL,
        name=name,
    )(*args)


PLACE, PREFIX, CORE, FLAT, LINE = range(5)


def rank_of(scal, k, d, other):
    line = jnp.bitwise_xor(scal[LINE], k)
    flat = jnp.bitwise_xor(scal[FLAT], d)
    return (line * 4 + flat) * 2 + jnp.bitwise_xor(scal[CORE], other)


def rows_at(index, size):
    return pl.ds(pl.multiple_of(index * size, size), size)


def square_pieces(wq, other):
    outer = other.shape[0] // 4
    for d in range(4):
        for k in range(outer):
            yield (k, d, 0, wq[d].at[k])
            yield (k, d, 1, other.at[d * outer + k])


def pack_kernel(lines, heads, scal, token, w_out, w_up, w_q, w_k, w_v, *refs):
    vectors, (up_own, out_b, out_c, out_d, send) = (refs[:8], refs[8:])
    wide = w_up.shape[1] // (4 * lines)
    rows, cut = (token.shape[0], w_up.shape[0])
    for out in (out_b, out_c, out_d):
        out[:rows, :] = token[...]
        out[rows : rows + cut, :] = w_out[...]
    for z in range(lines):
        pieces = [w_up[:, (z * 4 + t) * wide : (z * 4 + t + 1) * wide] for t in range(4)]
        for k, (out, first) in enumerate(
            ((up_own, 0), (out_b, rows + cut), (out_c, rows + cut), (out_d, rows + cut))
        ):
            target = jnp.bitwise_xor(scal[FLAT], k)
            value = pieces[0]
            for t in range(1, 4):
                value = jnp.where(target == t, pieces[t], value)
            out[first : first + cut, z * wide : (z + 1) * wide] = value
    lane = jnp.concatenate([ref[...].astype(F32) for ref in vectors], axis=0)
    lane = jnp.concatenate([lane, jnp.zeros((8, 2 * HD - cut), F32)], axis=1)
    vec = jnp.concatenate([jnp.transpose(lane)[:cut], jnp.zeros((cut, HD - 8), F32)], axis=1)
    vec = vec.astype(BF16)
    for h in range(send.shape[0]):
        for i, w in enumerate((w_q, w_k, w_v)):
            if h < heads:
                piece = w[:, h * HD : (h + 1) * HD]
            else:
                piece = jnp.zeros((cut, HD), BF16)
            send[h, :, i * HD : (i + 1) * HD] = piece
        send[h, :, 3 * HD :] = vec


def forward_kernel(
    heads, scal, ahead, own_b, own_c, own_d, zc, xc, yc, xya, xyb, w,
    n1_out, n0_out, qkvt, ctxc, ctxt, lse, rows_out, wt_out, wo_out,
    n1, n0, k_s, w_s, sems,
):
    place, prefix = (scal[PLACE], scal[PREFIX])
    outer = zc.shape[0] + 1
    length, width = n1.shape
    rows = length // (4 * outer)
    cut = w.shape[2]
    blk = split(length)
    copies = []
    near = ((ahead, 0), (own_b, 1), (own_c, 2), (own_d, 3))
    along = ((zc, 1, 0), (xc, 1, 1), (yc, 1, 2), (xya, 1, 3), (xyb, outer // 2 + 1, 3))
    for src, d in near:
        pair = (src.at[rows : rows + cut, :], wo_out.at[d * outer])
        copies.append(pltpu.make_async_copy(*pair, sems.at[2 + len(copies)]))
    for src, k, d in along:
        target = wo_out.at[d * outer + k : d * outer + k + src.shape[0]]
        copies.append(pltpu.make_async_copy(src.at[:, rows:, :], target, sems.at[2 + len(copies)]))
    for copy in copies:
        copy.start()
    head = jnp.minimum(place, heads - 1)
    for b in range(2):
        for i in range(w.shape[1]):
            at = (2 * i + b) * cut
            w_s[at : at + cut, :] = w[b, i].astype(F32)
    turned = jnp.transpose(w_s[...])
    wt_out[...] = turned[: 3 * HD].astype(BF16)
    rows_in = turned[3 * HD : 3 * HD + 8]
    rows_out[...] = rows_in
    gain = rows_in[0:1]
    shift = rows_in[1:2]

    def norm_rows(value, k, d):
        normed, _ = normalize(value.astype(F32))
        here = rows_at(jnp.bitwise_xor(place, k * 4 + d), rows)
        n0[here, :] = normed.astype(BF16)
        n1[here, :] = (normed * gain + shift).astype(BF16)

    for src, d in near:
        norm_rows(src[:rows, :], 0, d)
    for src, first, d in along:

        def one(k, carry, src=src, first=first, d=d):
            norm_rows(src[k, :rows, :], first + k, d)
            return carry

        lax.fori_loop(0, src.shape[0], one, 0)
    for i, (src, dst) in enumerate(((n1, n1_out), (n0, n0_out))):
        copy = pltpu.make_async_copy(src, dst, sems.at[i])
        copy.start()
        copies.append(copy)
    bias_q = w_s[rows_at(head, HD), 3 * HD + 2 : 3 * HD + 3]
    bias_v = w_s[rows_at(head, HD), 3 * HD + 3 : 3 * HD + 4]
    for i in range(length // blk):
        sl = slice(i * blk, (i + 1) * blk)
        part = dot(wt_out[...], n1[sl, :], NT)
        k_part = part[HD : 2 * HD].astype(BF16)
        qkvt[:HD, sl] = (part[:HD] + bias_q).astype(BF16)
        qkvt[HD : 2 * HD, sl] = k_part
        qkvt[2 * HD :, sl] = (part[2 * HD :] + bias_v).astype(BF16)
        k_s[sl, :] = jnp.transpose(k_part.astype(F32)).astype(BF16)
    scale = 0.125 * LOG2E

    def one_query(i, carry):
        first = pl.multiple_of(i * blk, blk)
        q_now = qkvt[:HD, pl.ds(first, blk)]

        def step(masked, j, state):
            top, total, acc = state
            start = pl.multiple_of(j * blk, blk)
            scores = dot(k_s[pl.ds(start, blk), :], q_now) * scale
            if masked:
                key = start + lax.broadcasted_iota(jnp.int32, (blk, blk), 0)
                query = first + lax.broadcasted_iota(jnp.int32, (blk, blk), 1)
                scores = jnp.where((key <= query) | (key < prefix), scores, -1e30)
            new_top = jnp.maximum(top, jnp.max(scores, axis=0, keepdims=True))
            prob = jnp.exp2(scores - new_top)
            fade = jnp.exp2(top - new_top)
            total = total * fade + jnp.sum(prob, axis=0, keepdims=True)
            acc = acc * fade + dot(qkvt[2 * HD :, pl.ds(start, blk)], prob.astype(BF16))
            return (new_top, total, acc)

        state = (
            jnp.full((1, blk), -1e30, F32),
            jnp.zeros((1, blk), F32),
            jnp.zeros((HD, blk), F32),
        )
        full = jnp.maximum(prefix // blk, i)
        needed = jnp.maximum((prefix + blk - 1) // blk, i + 1)
        state = lax.fori_loop(0, full, functools.partial(step, False), state)
        top, total, acc = lax.fori_loop(full, needed, functools.partial(step, True), state)
        out = acc / total
        ctxt[:, pl.ds(first, blk)] = out
        lse[:, pl.ds(first, blk)] = top + jnp.log2(total)
        for r in range(blk // rows):
            ctxc[i * (blk // rows) + r] = out[:, r * rows : (r + 1) * rows].astype(BF16)
        return carry

    lax.fori_loop(0, length // blk, one_query, 0)
    for copy in copies:
        copy.wait()


def backward_kernel(
    scal, qkvt, dcr, ctxt, lse, dchunk, dall, q_s, k_s, v_s, dc_s, dct_s, del_s, dq_s, dk_s, dv_s
):
    prefix = scal[PREFIX]
    rows = dcr.shape[2]
    length = qkvt.shape[1]
    blk = split(length)
    count = length // blk
    for i in range(count):
        sl = slice(i * blk, (i + 1) * blk)
        turned = jnp.transpose(qkvt[:, sl].astype(F32)).astype(BF16)
        q_s[sl, :] = turned[:, :HD]
        k_s[sl, :] = turned[:, HD : 2 * HD]
        v_s[sl, :] = turned[:, 2 * HD :]
    for i in range(length // rows):
        sl = slice(i * rows, (i + 1) * rows)
        dct_s[:, sl] = dcr[i]
        dc_s[sl, :] = jnp.transpose(dcr[i].astype(F32)).astype(BF16)
    del_s[...] = jnp.sum(dct_s[...].astype(F32) * ctxt[...], axis=0, keepdims=True)
    dq_s[...] = jnp.zeros_like(dq_s)
    scale = 0.125 * LOG2E

    def one_key(j, carry):
        start = pl.multiple_of(j * blk, blk)
        dk_s[...] = jnp.zeros_like(dk_s)
        dv_s[...] = jnp.zeros_like(dv_s)

        def step(masked, i, inner):
            first = pl.multiple_of(i * blk, blk)
            here = pl.ds(first, blk)
            scores = dot(k_s[pl.ds(start, blk), :], qkvt[:HD, here]) * scale
            prob = jnp.exp2(scores - lse[:, here])
            if masked:
                key = start + lax.broadcasted_iota(jnp.int32, (blk, blk), 0)
                query = first + lax.broadcasted_iota(jnp.int32, (blk, blk), 1)
                prob = jnp.where((key <= query) | (key < prefix), prob, 0.0)
            d_prob = dot(v_s[pl.ds(start, blk), :], dct_s[:, here])
            d_score = (prob * (d_prob - del_s[:, here])).astype(BF16)
            dv_s[...] += dot(prob.astype(BF16), dc_s[here, :])
            dk_s[...] += dot(d_score, q_s[here, :])
            dq_s[:, here] += dot(qkvt[HD : 2 * HD, pl.ds(start, blk)], d_score)
            return inner

        begin = jnp.where(start < prefix, 0, j)
        middle = jnp.where(start + blk <= prefix, begin, j + 1)
        lax.fori_loop(begin, middle, functools.partial(step, True), 0)
        lax.fori_loop(middle, count, functools.partial(step, False), 0)
        d_key = jnp.transpose(dk_s[...] * 0.125).astype(BF16)
        d_value = jnp.transpose(dv_s[...]).astype(BF16)
        dall[HD : 2 * HD, pl.ds(start, blk)] = d_key
        dall[2 * HD :, pl.ds(start, blk)] = d_value
        for r in range(blk // rows):
            at = j * (blk // rows) + r
            dchunk[at, HD : 2 * HD, :] = d_key[:, r * rows : (r + 1) * rows]
            dchunk[at, 2 * HD :, :] = d_value[:, r * rows : (r + 1) * rows]
        return carry

    lax.fori_loop(0, count, one_key, 0)
    for i in range(count):
        sl = slice(i * blk, (i + 1) * blk)
        d_query = (dq_s[:, sl] * 0.125).astype(BF16)
        dall[:HD, sl] = d_query
        for r in range(blk // rows):
            dchunk[i * (blk // rows) + r, :HD, :] = d_query[:, r * rows : (r + 1) * rows]


def stacked(pieces, first, last):
    return jnp.concatenate([piece[first:last, :].astype(F32) for piece in pieces]).astype(BF16)


def out_pieces(own, other):
    outer = own.shape[0] // 4
    return [
        (i % outer, i // outer, core, ref.at[i])
        for core, ref in ((0, own), (1, other))
        for i in range(own.shape[0])
    ]


def middle_kernel(heads, scal, ctx, own, other, token, rows_in, middle, norm_two, plain, moved):
    pieces = out_pieces(own, other)
    cut = own.shape[1]
    plain[...] = ctx[:heads].reshape(plain.shape).astype(F32)
    for n, (k, d, core, _) in enumerate(pieces):
        moved[n * cut : (n + 1) * cut, :] = plain[rows_at(rank_of(scal, k, d, core), cut), :]
    turned = jnp.transpose(moved[...]).astype(BF16)
    product = dot(turned, stacked([p[3] for p in pieces], 0, cut))
    value = token[...].astype(F32) + product + rows_in[4:5, :]
    middle[...] = value
    normed, _ = normalize(value)
    norm_two[...] = (normed * rows_in[5:6, :] + rows_in[6:7, :]).astype(BF16)


def feed_kernel(
    scal, n2_a, n2_b, n2_c, n2_d, dy_a, dy_b, dy_c, dy_d, ffz, ffc,
    out_keep, out_b, out_c, out_d, dn_keep, dn_b, dn_c, dn_d, send, keep,
    n2, dy, down, up, act, d_pre, down_s, up_s, bias,
):
    outer = ffz.shape[0]
    cut = (ffz.shape[1] - 8) // 8
    half = 4 * cut
    order = (0, 2, 1, 3)
    sources = [
        (src.at[i], k, core) for core, src in ((0, ffz), (1, ffc)) for i, k in enumerate(order)
    ]

    def block_of(k, core):
        line = jnp.bitwise_xor(scal[LINE], k)
        return line * 2 + jnp.bitwise_xor(scal[CORE], core)

    rows = []
    for src, k, core in sources:
        down[rows_at(block_of(k, core), half), :] = src[:half, :]
        for d in range(4):
            here = rows_at(rank_of(scal, k, d, core), cut)
            up_s[here, :] = src[half + d * cut : half + (d + 1) * cut, :].astype(F32)
        rows.append((block_of(k, core), src[2 * half :, :half].astype(F32)[:1]))
    up[...] = up_s[...].astype(BF16)
    for q in range(2 * outer):
        bias[:, q * half : (q + 1) * half] = sum(jnp.where(at == q, row, 0.0) for at, row in rows)
    count = n2_a.shape[0]
    for i, piece in enumerate((n2_a, n2_b, n2_c, n2_d)):
        n2[i * count : (i + 1) * count, :] = piece[...]
    for i, piece in enumerate((dy_a, dy_b, dy_c, dy_d)):
        dy[i * count : (i + 1) * count, :] = piece[piece.shape[0] - count :, :]
    tile = 256
    for c in range(down.shape[0] // tile):
        sl = slice(c * tile, (c + 1) * tile)
        pre = dot(n2[...], up[:, sl]) + bias[:, sl]
        cdf = 0.5 * (1.0 + lax.erf(pre * 0.7071067811865476))
        act[:, sl] = (pre * cdf).astype(BF16)
        slope = cdf + pre * jnp.exp(-0.5 * pre * pre) * 0.3989422804014327
        d_pre[:, sl] = (dot(dy[...], down[sl, :], NT) * slope).astype(BF16)
    back = dot(d_pre[...], up[...], NT)
    for i, ref in enumerate((dn_keep, dn_b, dn_c, dn_d)):
        ref[...] = back[i * count : (i + 1) * count].astype(ref.dtype)
    out = dot(act[...], down[...])
    for i, ref in enumerate((out_keep, out_b, out_c, out_d)):
        ref[...] = out[i * count : (i + 1) * count].astype(ref.dtype)
    down_s[...] = dot(act[...], dy[...], TN)
    up_s[...] = dot(n2[...], d_pre[...], TN)
    total = jnp.sum(d_pre[...].astype(F32), axis=0, keepdims=True)
    width = keep.shape[2]
    for k in range(outer):
        for core, ref in ((0, keep), (1, send)):
            at = block_of(k, core)
            ref[k, :half, :] = down_s[rows_at(at, half), :].astype(ref.dtype)
            for t in range(4):
                line = jnp.bitwise_xor(scal[LINE], k)
                rank = (line * 4 + t) * 2 + jnp.bitwise_xor(scal[CORE], core)
                here = slice(half + t * cut, half + (t + 1) * cut)
                ref[k, here, :] = up_s[rows_at(rank, cut), :].astype(ref.dtype)
            part = sum(
                jnp.where(at == q, total[:, q * half : (q + 1) * half], 0.0)
                for q in range(2 * outer)
            )
            part = jnp.concatenate([part, jnp.zeros((1, width - half), F32)], axis=1)
            ref[k, 2 * half :, :] = jnp.broadcast_to(part, (8, width)).astype(ref.dtype)


def turn_kernel(
    heads, scal, keep, got_b, got_c, got_d, middle, d_out, own, other, rows_in, ctx,
    d_middle, d_branch_out, d_ctx, sums, wo_keep, wo_send, plain, full,
):
    d_norm = keep[...] + (got_b[...].astype(F32) + got_c[...].astype(F32)) + got_d[...].astype(F32)
    normed, factor = normalize(middle[...])
    grad_in, grad_gain, grad_shift = norm_backward(d_norm, normed, factor, rows_in[5:6, :])
    grad_up = d_out[...].astype(F32)
    total = grad_up + grad_in
    low = total.astype(BF16)
    d_middle[...] = total
    d_branch_out[...] = low[:8]
    pieces = out_pieces(own, other)
    cut = own.shape[1]
    back = dot(stacked([p[3] for p in pieces], 0, cut), low, NT)
    for n, (k, d, core, _) in enumerate(pieces):
        plain[rows_at(rank_of(scal, k, d, core), cut), :] = back[n * cut : (n + 1) * cut]
    seq, rows = (d_ctx.shape[0], d_ctx.shape[2])
    d_ctx[:heads] = plain[...].astype(BF16).reshape(heads, HD, rows)
    d_ctx[heads:] = jnp.zeros((seq - heads, HD, rows), BF16)
    sums[0:1, :] = jnp.sum(low.astype(F32), axis=0, keepdims=True)
    sums[1:2, :] = grad_gain
    sums[2:3, :] = grad_shift
    sums[3:4, :] = jnp.sum(grad_up, axis=0, keepdims=True)
    sums[4:, :] = jnp.zeros((4, sums.shape[1]), F32)
    full[...] = dot(ctx[:heads].reshape(heads * HD, rows), low).reshape(full.shape)
    for i in range(seq):
        wo_keep[i] = full[2 * i + scal[CORE]]
        wo_send[i] = full[2 * i + 1 - scal[CORE]].astype(BF16)


def fold_kernel(keep, got, own, away):
    for i, (k, ref) in enumerate(((0, own), (2, own), (1, away), (3, away))):
        ref[i % 2] = (keep[k] + got[k].astype(F32)).astype(ref.dtype)


def second_kernel(keep, got, own, away):
    own[...] = keep[0] + got[0].astype(F32)
    away[...] = (keep[1] + got[1].astype(F32)).astype(BF16)


def finish_kernel(scal, keep, *refs):
    got, (wo_keep, wo_got, out_b, out_c, out_d), outs = (refs[:-13], refs[-13:-8], refs[-8:])
    grad_down, bias, own, wo_own, away_b, away_c, away_d, total = outs
    value = keep[...]
    for ref in got:
        value = value + ref[...].astype(F32)
    total[...] = value
    half = grad_down.shape[0]
    cut = half // 4
    lines = wo_own.shape[0]
    grad_down[...] = value[:half]
    bias[...] = value[2 * half : 2 * half + 1, :half]
    for k, ref in enumerate((own, away_b, away_c, away_d)):
        at = jnp.bitwise_xor(scal[FLAT], k)
        here = pl.ds(pl.multiple_of(half + at * cut, 8), cut)
        ref[:cut, :] = total[here, :].astype(BF16)
        for z in range(lines):
            part = wo_keep[4 * z + at] + wo_got[4 * z + at].astype(F32)
            if k:
                ref[(1 + z) * cut : (2 + z) * cut, :] = part.astype(BF16)
            else:
                wo_own[z] = part
    for src, ref in ((out_b, away_b), (out_c, away_c), (out_d, away_d)):
        ref[(1 + lines) * cut :, :] = src[...]


def close_kernel(
    lines, scal, own, wo_own, got_b, got_c, got_d, middle, out_keep, rows_in,
    layer_out, grad_up, grad_out, *away,
):
    cut = grad_out.shape[0]
    got = (got_b, got_c, got_d)
    value = middle[...] + out_keep[...] + rows_in[7:8, :]
    pieces = [own[...].astype(F32)]
    for ref in got:
        value = value + ref[(1 + lines) * cut :, :].astype(F32)
        pieces.append(ref[:cut, :].astype(F32))
    layer_out[...] = value.astype(BF16)
    for k, out in enumerate((grad_out,) + away):
        at = jnp.bitwise_xor(scal[LINE], k)
        here = pl.ds(pl.multiple_of((1 + at) * cut, 8), cut)
        part = wo_own[at]
        for ref in got:
            part = part + ref[here, :].astype(F32)
        out[...] = part.astype(out.dtype)
    wide = own.shape[1] // lines
    for t in range(4):
        step = jnp.bitwise_xor(scal[FLAT], t)
        piece = pieces[0]
        for k in range(1, 4):
            piece = jnp.where(step == k, pieces[k], piece)
        for z in range(lines):
            at = (z * 4 + t) * wide
            grad_up[:, at : at + wide] = piece[:, z * wide : (z + 1) * wide]


def heads_kernel(heads, scal, dall, n1, n0, wt, sums, keep, send, gh, gm, cs, full):
    step = pl.program_id(0)

    @pl.when(step == 0)
    def _():
        gh[...] = jnp.zeros_like(gh)
        gm[...] = jnp.zeros_like(gm)
        cs[...] = jnp.zeros_like(cs)

    gh[...] += dot(dall[...], n1[...])
    gm[...] += dot(dall[...], n0[...])
    cs[...] += dot(dall[...], jnp.ones((dall.shape[1], 2 * HD), BF16))

    @pl.when(step == pl.num_programs(0) - 1)
    def _():
        place = scal[PLACE]
        width = gh.shape[1]
        live = place < heads
        wide = wt[...].astype(F32)
        gain = jnp.where(live, jnp.sum(wide * gm[...], axis=0, keepdims=True), 0.0)
        shift = jnp.where(live, jnp.sum(wide * cs[:, :1], axis=0, keepdims=True), 0.0)
        line = jnp.transpose(cs[...])[0:1]
        mine = lax.broadcasted_iota(jnp.int32, (1, width), 1) // HD == place
        b_q = jnp.where(mine, jnp.concatenate([line[:, :HD]] * heads, axis=1), 0.0)
        b_v = jnp.where(mine, jnp.concatenate([line[:, 2 * HD :]] * heads, axis=1), 0.0)
        vec = jnp.concatenate([gain, shift, b_q, b_v, sums[:4, :]], axis=0)
        pad = jnp.zeros((width, HD - 8), F32)
        block = jnp.concatenate([jnp.transpose(gh[...]), jnp.transpose(vec), pad], axis=1)
        full[...] = block.reshape(full.shape)
        for i in range(keep.shape[0]):
            keep[i] = full[2 * i + scal[CORE]]
            send[i] = full[2 * i + 1 - scal[CORE]].astype(BF16)


def head_grads(scal, dall, n1, n0, wt, sums, heads, seq):
    length, width = n1.shape
    blk = split(length)
    cut = width // (2 * seq)
    outs = (like((seq, cut, WIDE), F32), like((seq, cut, WIDE), BF16))
    return pl.pallas_call(
        functools.partial(heads_kernel, heads),
        out_shape=outs,
        grid=(length // blk,),
        in_specs=[
            SMEM_SPEC,
            pl.BlockSpec((3 * HD, blk), lambda i: (0, i)),
            pl.BlockSpec((blk, width), lambda i: (i, 0)),
            pl.BlockSpec((blk, width), lambda i: (i, 0)),
            full_block(wt.shape),
            full_block(sums.shape),
        ],
        out_specs=tuple(full_block(out.shape) for out in outs),
        scratch_shapes=[
            pltpu.VMEM((3 * HD, width), F32),
            pltpu.VMEM((3 * HD, width), F32),
            pltpu.VMEM((3 * HD, 2 * HD), F32),
            pltpu.VMEM((2 * seq, cut, WIDE), F32),
        ],
        compiler_params=pltpu.CompilerParams(vmem_limit_bytes=LIMIT << 20),
        cost_estimate=SMALL,
        name="heads",
    )(scal, dall, n1, n0, wt, sums)


def last_kernel(
    heads, scal, d_rows, wq_a, wq_b, wq_c, wq_d, other, token, d_middle, rows_in, grad_tokens, plain
):
    cut = other.shape[1] // 3
    pieces = list(square_pieces((wq_a, wq_b, wq_c, wq_d), other))
    total = 0.0
    for i in range(3):
        part = jnp.concatenate(
            [d_rows[h, i * HD : (i + 1) * HD, :].astype(F32) for h in range(heads)], axis=0
        )
        weights = stacked([p[3] for p in pieces], i * cut, (i + 1) * cut)
        total = total + dot(weights, part.astype(BF16))
    for n, (k, d, core, _) in enumerate(pieces):
        plain[rows_at(rank_of(scal, k, d, core), cut), :] = total[n * cut : (n + 1) * cut]
    normed, factor = normalize(token[...].astype(F32))
    grad_in, _, _ = norm_backward(jnp.transpose(plain[...]), normed, factor, rows_in[0:1, :])
    grad_tokens[...] = d_middle[...] + grad_in


def unpack_kernel(heads, got, g_q, g_k, g_v, *vec):
    for i, out in enumerate((g_q, g_k, g_v)):
        for h in range(heads):
            out[:, h * HD : (h + 1) * HD] = got[h, :, i * HD : (i + 1) * HD].astype(F32)
    total = got[0, :, 2 * HD :].astype(F32)
    for s in range(1, got.shape[0]):
        total = total + got[s, :, 2 * HD :].astype(F32)
    cut = total.shape[0]
    total = jnp.concatenate([total, jnp.zeros((2 * HD - cut, 2 * HD), F32)], axis=0)
    total = jnp.transpose(total)
    for i, out in enumerate(vec):
        out[...] = total[HD + i : HD + i + 1, :cut]


def body(
    tokens, cotangent, prefix_len, gain_one, shift_one, w_query, b_query, w_key, w_value, b_value,
    w_output, b_output, gain_two, shift_two, w_up, b_up, w_down, b_down,
):
    outer = lax.axis_size("z")
    seq = 4 * outer
    token, d_out = (tokens[0], cotangent[0])
    rows, width = token.shape
    length = seq * rows
    heads = width // HD
    cut = w_query.shape[0]
    half = w_down.shape[0]
    local = w_up.shape[1] // 4
    flat = lax.axis_index(("y", "x"))
    places = (lax.axis_index(SEQ), prefix_len[0], lax.axis_index("batch"), flat, lax.axis_index("z"))
    scal = jnp.stack(places).astype(jnp.int32)

    ahead = jnp.concatenate([token, w_output])
    zc = jnp.stack([swap(ahead, "z", k) for k in range(1, outer)])
    vectors = (
        gain_one, shift_one, b_query, b_value, b_output, gain_two, shift_two, b_down,
    )
    vectors = [value[None] for value in vectors]
    up_own, *first, send = once(
        "pack",
        functools.partial(pack_kernel, outer, heads),
        (scal, token, w_output, w_up, w_query, w_key, w_value, *vectors),
        [like((cut, local), BF16)]
        + [like((rows + 2 * cut, width), BF16)] * 3
        + [like((seq, cut, WIDE), BF16)],
    )
    first = [swap_plane(part, k + 1) for k, part in enumerate(first)]
    zc = after(zc, *first)
    xc = swap(zc, "x")
    yc = swap(zc, "y")
    head_w = lax.all_to_all(after(send, zc), SEQ, split_axis=0, concat_axis=0, tiled=True)
    wq = after(jnp.concatenate([w_query, w_key, w_value]), zc)
    wq_got = [swap(wq, "z", k) for k in range(1, outer)]
    head_w = lax.all_gather(head_w, "batch", axis=0, tiled=False)
    xc, yc, head_w, wq_got = lax.optimization_barrier((xc, yc, head_w, wq_got))
    xya = swap(xc[: outer // 2], "y")
    xyb = swap(yc[outer // 2 :], "x")

    b_up_row = jnp.pad(b_up[None], ((0, 7), (0, width - half)))
    ff = [w_down, up_own] + [part[rows + cut :] for part in first] + [b_up_row]
    ff = after(jnp.concatenate(ff), head_w, xc)
    ff = jnp.stack([ff, swap(ff, "z", 2)])
    ff_got = swap(ff, "z", 1)
    wq = after(jnp.stack([wq] + wq_got), xya, xyb)
    wq = [wq] + [swap_plane(wq, k) for k in range(1, 4)]

    norm_one, norm_raw, qkvt, ctxc, ctxt, lse, rows_in, wt, w_out_own = once(
        "forward",
        functools.partial(forward_kernel, heads),
        (scal, ahead, *first, zc, xc, yc, xya, xyb, head_w),
        [
            like((length, width), BF16),
            like((length, width), BF16),
            like((3 * HD, length), BF16),
            like((seq, HD, rows), BF16),
            like((HD, length), F32),
            like((1, length), F32),
            like((8, width), F32),
            like((3 * HD, width), BF16),
            like((seq, cut, width), BF16),
        ],
        [
            pltpu.VMEM((length, width), BF16),
            pltpu.VMEM((length, width), BF16),
            pltpu.VMEM((length, HD), BF16),
            pltpu.VMEM((width, WIDE), F32),
            pltpu.SemaphoreType.DMA((11,)),
        ],
        left=(0, 1, 8),
    )
    w_out_other = swap(w_out_own, "batch")
    ctxc, wq, ff_got = lax.optimization_barrier((ctxc, wq, ff_got))
    ffz = jnp.concatenate([ff, ff_got])
    dy = [d_out] + [swap_plane(after(d_out, ctxc), k) for k in range(1, 4)]
    ctx = lax.all_to_all(ctxc, SEQ, split_axis=0, concat_axis=0, tiled=True)
    ffc = swap(ffz, "batch")
    dy, ctx = lax.optimization_barrier((dy, ctx))
    middle, norm_two = once(
        "middle",
        functools.partial(middle_kernel, heads),
        (scal, ctx, w_out_own, w_out_other, token, rows_in),
        [like((rows, width), F32), like((rows, width), BF16)],
        [pltpu.VMEM((width, rows), F32)] * 2,
    )
    n2 = [norm_two] + [swap_plane(norm_two, k) for k in range(1, 4)]

    part = [like((rows, width), F32)] + [like((rows, width), BF16)] * 3
    fed = once(
        "feed",
        feed_kernel,
        (scal, *n2, *dy, ffz, ffc),
        part + part + [like(ffz.shape, BF16), like(ffz.shape, F32)],
        [
            pltpu.VMEM((4 * rows, width), BF16),
            pltpu.VMEM((4 * rows, width), BF16),
            pltpu.VMEM((local, width), BF16),
            pltpu.VMEM((width, local), BF16),
            pltpu.VMEM((4 * rows, local), BF16),
            pltpu.VMEM((4 * rows, local), BF16),
            pltpu.VMEM((local, width), F32),
            pltpu.VMEM((width, local), F32),
            pltpu.VMEM((1, local), F32),
        ],
    )
    out_keep, *out_send = fed[:4]
    dn_keep, *dn_send = fed[4:8]
    send, keep = fed[8:]
    dn_got = [swap_plane(value, k + 1) for k, value in enumerate(dn_send)]

    count = 2 * half + 8
    pair = like((2, count, width), F32)
    own, away = once(
        "fold",
        fold_kernel,
        (keep, after(swap(send, "batch"), *dn_got)),
        [pair, like(pair.shape, BF16)],
    )
    dn_keep, _ = lax.optimization_barrier((dn_keep, away))
    d_middle, _, d_ctx, sums, wo_keep, wo_send = once(
        "turn",
        functools.partial(turn_kernel, heads),
        (scal, dn_keep, *dn_got, middle, d_out, w_out_own, w_out_other, rows_in, ctx),
        [
            like((rows, width), F32),
            like((8, width), BF16),
            like((seq, HD, rows), BF16),
            like((8, width), F32),
            like((seq, cut, width), F32),
            like((seq, cut, width), BF16),
        ],
        [pltpu.VMEM((width, rows), F32), pltpu.VMEM((2 * seq, cut, width), F32)],
    )
    d_ctx = lax.all_to_all(d_ctx, SEQ, split_axis=0, concat_axis=0, tiled=True)

    wo_got = swap(wo_send, "batch")
    own, away = once(
        "second",
        second_kernel,
        (own, swap(away, "z", 1)),
        [like((count, width), F32), like((count, width), BF16)],
    )
    back = [swap(away, "z", 2)]

    blk = split(length)
    dchunk, dall = once(
        "backward",
        backward_kernel,
        (after(scal, away), qkvt, d_ctx, ctxt, lse),
        [like((seq, 3 * HD, rows), BF16), like((3 * HD, length), BF16)],
        [
            pltpu.VMEM((length, HD), BF16),
            pltpu.VMEM((length, HD), BF16),
            pltpu.VMEM((length, HD), BF16),
            pltpu.VMEM((length, HD), BF16),
            pltpu.VMEM((HD, length), BF16),
            pltpu.VMEM((1, length), F32),
            pltpu.VMEM((HD, length), F32),
            pltpu.VMEM((blk, HD), F32),
            pltpu.VMEM((blk, HD), F32),
        ],
    )
    back, dchunk = lax.optimization_barrier((back, dchunk))
    d_rows = lax.all_to_all(dchunk, SEQ, split_axis=0, concat_axis=0, tiled=True)

    grad_w_down, bias, own, wo_own, *away = once(
        "finish",
        finish_kernel,
        (scal, own, *back, wo_keep, wo_got, *out_send),
        [
            like((half, width), F32),
            like((1, half), F32),
            like((cut, width), BF16),
            like((outer, cut, width), F32),
        ]
        + [like(((1 + outer) * cut + rows, width), BF16)] * 3,
        [pltpu.VMEM((count, width), F32)],
    )
    got = [swap_plane(value, k + 1) for k, value in enumerate(away)]
    last, send = head_grads(scal, dall, norm_one, norm_raw, wt, sums, heads, seq)
    last = last + swap(send, "batch").astype(F32)
    last = after(last.astype(BF16), d_rows)
    other = swap(after(jnp.concatenate(wq), dall), "batch")
    grad_tokens = once(
        "last",
        functools.partial(last_kernel, heads),
        (scal, d_rows, *wq, other, token, d_middle, rows_in),
        [like((rows, width), F32)],
        [pltpu.VMEM((width, rows), F32)],
    )[0]
    last = lax.all_to_all(last, SEQ, split_axis=0, concat_axis=0, tiled=True)
    mat = like((cut, width), F32)
    grad_w_query, grad_w_key, grad_w_value, *vec = once(
        "unpack",
        functools.partial(unpack_kernel, heads),
        (last,),
        [mat, mat, mat] + [like((1, cut), F32)] * 8,
    )
    layer_out, grad_w_up, grad_w_output, *away = once(
        "close",
        functools.partial(close_kernel, outer),
        (scal, own, wo_own, *got, after(middle, grad_tokens), out_keep, rows_in),
        [like((rows, width), BF16), like((cut, 4 * local), F32), like((cut, width), F32)]
        + [like((cut, width), BF16)] * (outer - 1),
    )
    grad_w_output = grad_w_output + sum(
        swap(value, "z", k + 1).astype(F32) for k, value in enumerate(away)
    )

    return (
        layer_out[None],
        grad_tokens[None],
        vec[0][0],
        vec[1][0],
        grad_w_query,
        vec[2][0],
        grad_w_key,
        grad_w_value,
        vec[3][0],
        grad_w_output,
        vec[4][0],
        vec[5][0],
        vec[6][0],
        grad_w_up,
        bias[0],
        grad_w_down,
        vec[7][0],
    )


def over_rows(left, right):
    return lax.dot_general(
        left, right, (((0,), (0,)), ((), ())), preferred_element_type=jnp.float32
    )


def over_cols(left, right):
    return lax.dot_general(
        left, right, (((1,), (1,)), ((), ())), preferred_element_type=jnp.float32
    )


def pair_scores(q_part, k_part, row_ids, col_ids, prefix):
    scores = jnp.einsum("qhd,khd->hqk", q_part, k_part, preferred_element_type=jnp.float32) * 0.125
    allowed = (col_ids[None, :] <= row_ids[:, None]) | (col_ids[None, :] < prefix)
    return (jnp.where(allowed[None], scores, -1e30), allowed)


def grad_terms(q_part, do_part, lse_part, delta_part, k_part, v_part, row_ids, col_ids, prefix):
    scores, allowed = pair_scores(q_part, k_part, row_ids, col_ids, prefix)
    attn_prob = jnp.where(allowed[None], jnp.exp(scores - lse_part[:, :, None]), 0.0)
    prob_low = attn_prob.astype(jnp.bfloat16)
    d_prob = jnp.einsum("qhd,khd->hqk", do_part, v_part, preferred_element_type=jnp.float32)
    d_score = (attn_prob * (d_prob - delta_part[:, :, None])).astype(jnp.bfloat16)
    return (prob_low, d_score)


def plain_body(
    tokens,
    cotangent,
    prefix_len,
    gain_one,
    shift_one,
    w_query,
    b_query,
    w_key,
    w_value,
    b_value,
    w_output,
    b_output,
    gain_two,
    shift_two,
    w_up,
    b_up,
    w_down,
    b_down,
):
    shards = (
        gain_one,
        shift_one,
        w_query,
        b_query,
        w_key,
        w_value,
        b_value,
        w_output,
        b_output,
        gain_two,
        shift_two,
        w_up,
        b_up,
        w_down,
        b_down,
    )
    gathered = (
        lax.all_gather(shards[0], ("seq", "batch"), axis=0, tiled=True),
        lax.all_gather(shards[1], ("seq", "batch"), axis=0, tiled=True),
        lax.all_gather(shards[2], ("seq", "batch"), axis=0, tiled=True),
        lax.all_gather(shards[3], ("seq", "batch"), axis=0, tiled=True),
        lax.all_gather(shards[4], ("seq", "batch"), axis=0, tiled=True),
        lax.all_gather(shards[5], ("seq", "batch"), axis=0, tiled=True),
        lax.all_gather(shards[6], ("seq", "batch"), axis=0, tiled=True),
        lax.all_gather(shards[7], ("seq", "batch"), axis=0, tiled=True),
        lax.all_gather(shards[8], ("seq", "batch"), axis=0, tiled=True),
        lax.all_gather(shards[9], ("seq", "batch"), axis=0, tiled=True),
        lax.all_gather(shards[10], ("seq", "batch"), axis=0, tiled=True),
        lax.all_gather(shards[11], ("seq", "batch"), axis=0, tiled=True),
        lax.all_gather(shards[12], ("seq", "batch"), axis=0, tiled=True),
        lax.all_gather(shards[13], ("seq", "batch"), axis=0, tiled=True),
        lax.all_gather(shards[14], ("seq", "batch"), axis=0, tiled=True),
    )
    (
        ga_full,
        sa_full,
        wq_full,
        bq_full,
        wk_full,
        wv_full,
        bv_full,
        wo_full,
        bo_full,
        gb_full,
        sb_full,
        wu_full,
        bu_full,
        wd_full,
        bd_full,
    ) = gathered
    hidden = tokens[0].astype(jnp.float32)
    local_rows = hidden.shape[0]
    width = hidden.shape[1]
    heads = width // HD
    prefix = prefix_len[0]
    start_row = lax.axis_index("seq") * local_rows
    last_row = start_row + local_rows - 1
    length = local_rows * lax.axis_size("seq")
    block_rows = min(512, length)
    block_count = length // block_rows
    row_ids = start_row + jnp.arange(local_rows, dtype=jnp.int32)
    block_ids = jnp.arange(block_count, dtype=jnp.int32)
    normed_one, factor_one = normalize(hidden)
    norm_one = (normed_one * ga_full.astype(jnp.float32) + sa_full.astype(jnp.float32)).astype(
        jnp.bfloat16
    )
    q_low = (
        jnp.dot(norm_one, wq_full, preferred_element_type=jnp.float32) + bq_full.astype(jnp.float32)
    ).astype(jnp.bfloat16)
    k_low = jnp.dot(norm_one, wk_full, preferred_element_type=jnp.float32).astype(jnp.bfloat16)
    v_low = (
        jnp.dot(norm_one, wv_full, preferred_element_type=jnp.float32) + bv_full.astype(jnp.float32)
    ).astype(jnp.bfloat16)
    k_all, v_all = (
        lax.all_gather(k_low, "seq", axis=0, tiled=True),
        lax.all_gather(v_low, "seq", axis=0, tiled=True),
    )
    q_heads = q_low.reshape(local_rows, heads, HD)

    def lse_step(state, item):
        k_part, index = item
        col_ids = index * block_rows + jnp.arange(block_rows, dtype=jnp.int32)

        def lse_update(current):
            scores, allowed = pair_scores(q_heads, k_part, row_ids, col_ids, prefix)
            new_top = jnp.maximum(current[0], jnp.max(scores, axis=-1))
            total = current[1] * jnp.exp(current[0] - new_top) + jnp.sum(
                jnp.exp(scores - new_top[:, :, None]), axis=-1
            )
            return (new_top, total)

        needed = (index * block_rows <= last_row) | (index * block_rows < prefix)
        return (lax.cond(needed, lse_update, lambda current: current, state), None)

    k_blocks = k_all.reshape(block_count, block_rows, heads, HD)
    v_blocks = v_all.reshape(block_count, block_rows, heads, HD)
    lse_start = (
        jnp.full((heads, local_rows), -1e30, jnp.float32),
        jnp.zeros((heads, local_rows), jnp.float32),
    )
    (top_all, total_all), _ = lax.scan(lse_step, lse_start, (k_blocks, block_ids))
    lse = top_all + jnp.log(total_all)

    def out_step(acc, item):
        k_part, v_part, index = item
        col_ids = index * block_rows + jnp.arange(block_rows, dtype=jnp.int32)

        def out_update(current):
            scores, allowed = pair_scores(q_heads, k_part, row_ids, col_ids, prefix)
            attn_prob = jnp.where(allowed[None], jnp.exp(scores - lse[:, :, None]), 0.0).astype(
                jnp.bfloat16
            )
            return current + jnp.einsum(
                "hqk,khd->qhd", attn_prob, v_part, preferred_element_type=jnp.float32
            )

        needed = (index * block_rows <= last_row) | (index * block_rows < prefix)
        return (lax.cond(needed, out_update, lambda current: current, acc), None)

    ctx_acc, _ = lax.scan(
        out_step, jnp.zeros((local_rows, heads, HD), jnp.float32), (k_blocks, v_blocks, block_ids)
    )
    ctx_low = ctx_acc.reshape(local_rows, width).astype(jnp.bfloat16)
    middle = (
        hidden
        + jnp.dot(ctx_low, wo_full, preferred_element_type=jnp.float32)
        + bo_full.astype(jnp.float32)
    )
    normed_two, factor_two = normalize(middle)
    norm_two = (normed_two * gb_full.astype(jnp.float32) + sb_full.astype(jnp.float32)).astype(
        jnp.bfloat16
    )
    pre_act = jnp.dot(norm_two, wu_full, preferred_element_type=jnp.float32) + bu_full.astype(
        jnp.float32
    )
    cdf_part = 0.5 * (1.0 + jax.scipy.special.erf(pre_act * 0.7071067811865476))
    act_low = (pre_act * cdf_part).astype(jnp.bfloat16)
    layer_out = (
        middle
        + jnp.dot(act_low, wd_full, preferred_element_type=jnp.float32)
        + bd_full.astype(jnp.float32)
    ).astype(jnp.bfloat16)
    regathered = (
        lax.all_gather(shards[0], ("seq", "batch"), axis=0, tiled=True),
        lax.all_gather(shards[1], ("seq", "batch"), axis=0, tiled=True),
        lax.all_gather(shards[2], ("seq", "batch"), axis=0, tiled=True),
        lax.all_gather(shards[3], ("seq", "batch"), axis=0, tiled=True),
        lax.all_gather(shards[4], ("seq", "batch"), axis=0, tiled=True),
        lax.all_gather(shards[5], ("seq", "batch"), axis=0, tiled=True),
        lax.all_gather(shards[6], ("seq", "batch"), axis=0, tiled=True),
        lax.all_gather(shards[7], ("seq", "batch"), axis=0, tiled=True),
        lax.all_gather(shards[8], ("seq", "batch"), axis=0, tiled=True),
        lax.all_gather(shards[9], ("seq", "batch"), axis=0, tiled=True),
        lax.all_gather(shards[10], ("seq", "batch"), axis=0, tiled=True),
        lax.all_gather(shards[11], ("seq", "batch"), axis=0, tiled=True),
        lax.all_gather(shards[12], ("seq", "batch"), axis=0, tiled=True),
        lax.all_gather(shards[13], ("seq", "batch"), axis=0, tiled=True),
        lax.all_gather(shards[14], ("seq", "batch"), axis=0, tiled=True),
    )
    (
        ga_back,
        sa_back,
        wq_back,
        bq_back,
        wk_back,
        wv_back,
        bv_back,
        wo_back,
        bo_back,
        gb_back,
        sb_back,
        wu_back,
        bu_back,
        wd_back,
        bd_back,
    ) = regathered
    d_out = cotangent[0]
    grad_wd = over_rows(act_low, d_out)
    grad_bd = jnp.sum(d_out.astype(jnp.float32), axis=0)
    d_act = over_cols(d_out, wd_back)
    slope = cdf_part + pre_act * jnp.exp(-0.5 * pre_act * pre_act) * 0.3989422804014327
    d_pre = (d_act * slope).astype(jnp.bfloat16)
    grad_wu = over_rows(norm_two, d_pre)
    grad_bu = jnp.sum(d_pre.astype(jnp.float32), axis=0)
    d_norm_two = over_cols(d_pre, wu_back)
    d_mid_norm, grad_gb, grad_sb = norm_backward(d_norm_two, normed_two, factor_two, gb_back)
    grad_gb, grad_sb = (grad_gb[0], grad_sb[0])
    d_middle = d_out.astype(jnp.float32) + d_mid_norm
    d_branch = d_middle.astype(jnp.bfloat16)
    grad_wo = over_rows(ctx_low, d_branch)
    grad_bo = jnp.sum(d_branch.astype(jnp.float32), axis=0)
    d_ctx = over_cols(d_branch, wo_back).astype(jnp.bfloat16)
    do_heads = d_ctx.reshape(local_rows, heads, HD)
    delta = jnp.sum(d_ctx.astype(jnp.float32).reshape(local_rows, heads, HD) * ctx_acc, axis=-1).T
    k_back, v_back = (k_blocks, v_blocks)
    zero_heads = jnp.zeros((local_rows, heads, HD), jnp.float32)

    def grad_step(acc, item):
        k_part, v_part, index = item
        col_ids = index * block_rows + jnp.arange(block_rows, dtype=jnp.int32)

        def work(current):
            prob_low, d_score = grad_terms(
                q_heads, do_heads, lse, delta, k_part, v_part, row_ids, col_ids, prefix
            )
            current = current + 0.125 * jnp.einsum(
                "hqk,khd->qhd", d_score, k_part, preferred_element_type=jnp.float32
            )
            d_key = 0.125 * jnp.einsum(
                "hqk,qhd->khd", d_score, q_heads, preferred_element_type=jnp.float32
            )
            d_value = jnp.einsum(
                "hqk,qhd->khd", prob_low, do_heads, preferred_element_type=jnp.float32
            )
            return (current, (d_key, d_value))

        def skip(current):
            empty = jnp.zeros((block_rows, heads, HD), jnp.float32)
            return (current, (empty, empty))

        needed = (index * block_rows <= last_row) | (index * block_rows < prefix)
        return lax.cond(needed, work, skip, acc)

    dq_acc, (dk_blocks, dv_blocks) = lax.scan(grad_step, zero_heads, (k_back, v_back, block_ids))
    dk_local, dv_local = (
        lax.psum_scatter(
            dk_blocks.reshape(length, width).astype(jnp.bfloat16),
            "seq",
            scatter_dimension=0,
            tiled=True,
        ).astype(jnp.float32),
        lax.psum_scatter(
            dv_blocks.reshape(length, width).astype(jnp.bfloat16),
            "seq",
            scatter_dimension=0,
            tiled=True,
        ).astype(jnp.float32),
    )
    dq_low = dq_acc.reshape(local_rows, width).astype(jnp.bfloat16)
    dk_low = dk_local.astype(jnp.bfloat16)
    dv_low = dv_local.astype(jnp.bfloat16)
    grad_wq = over_rows(norm_one, dq_low)
    grad_bq = jnp.sum(dq_low.astype(jnp.float32), axis=0)
    grad_wk = over_rows(norm_one, dk_low)
    grad_wv = over_rows(norm_one, dv_low)
    grad_bv = jnp.sum(dv_low.astype(jnp.float32), axis=0)
    d_norm_one = (
        over_cols(dq_low, wq_back) + over_cols(dk_low, wk_back) + over_cols(dv_low, wv_back)
    )
    d_in_norm, grad_ga, grad_sa = norm_backward(d_norm_one, normed_one, factor_one, ga_back)
    grad_ga, grad_sa = (grad_ga[0], grad_sa[0])
    grad_tokens = d_middle + d_in_norm
    summed = (
        lax.psum_scatter(grad_ga, ("seq", "batch"), scatter_dimension=0, tiled=True),
        lax.psum_scatter(grad_sa, ("seq", "batch"), scatter_dimension=0, tiled=True),
        lax.psum_scatter(grad_wq, ("seq", "batch"), scatter_dimension=0, tiled=True),
        lax.psum_scatter(grad_bq, ("seq", "batch"), scatter_dimension=0, tiled=True),
        lax.psum_scatter(grad_wk, ("seq", "batch"), scatter_dimension=0, tiled=True),
        lax.psum_scatter(grad_wv, ("seq", "batch"), scatter_dimension=0, tiled=True),
        lax.psum_scatter(grad_bv, ("seq", "batch"), scatter_dimension=0, tiled=True),
        lax.psum_scatter(grad_wo, ("seq", "batch"), scatter_dimension=0, tiled=True),
        lax.psum_scatter(grad_bo, ("seq", "batch"), scatter_dimension=0, tiled=True),
        lax.psum_scatter(grad_gb, ("seq", "batch"), scatter_dimension=0, tiled=True),
        lax.psum_scatter(grad_sb, ("seq", "batch"), scatter_dimension=0, tiled=True),
        lax.psum_scatter(grad_wu, ("seq", "batch"), scatter_dimension=0, tiled=True),
        lax.psum_scatter(grad_bu, ("seq", "batch"), scatter_dimension=0, tiled=True),
        lax.psum_scatter(grad_wd, ("seq", "batch"), scatter_dimension=0, tiled=True),
        lax.psum_scatter(grad_bd, ("seq", "batch"), scatter_dimension=0, tiled=True),
    )
    return (
        layer_out[None],
        grad_tokens[None],
        summed[0],
        summed[1],
        summed[2],
        summed[3],
        summed[4],
        summed[5],
        summed[6],
        summed[7],
        summed[8],
        summed[9],
        summed[10],
        summed[11],
        summed[12],
        summed[13],
        summed[14],
    )


def solution(mesh):
    seq, batch = (mesh.shape["seq"], mesh.shape["batch"])
    if batch == 2 and seq == 16:
        fine = Mesh(mesh.devices.reshape(seq // 4, 2, 2, batch), ALL)
        along, run = (SEQ, body)
    else:
        fine, along, run = (mesh, "seq", plain_body)
    every = along + ("batch",) if run is body else ("seq", "batch")
    act, mat, vec = (P("batch", along, None), P(every, None), P(every))
    return jax.shard_map(
        run,
        mesh=fine,
        in_specs=(
            act, act, P("batch"), vec, vec, mat, vec, mat, mat, vec, mat, vec, vec, vec, mat, vec, mat,
            vec,
        ),
        out_specs=(
            act, act, vec, vec, mat, vec, mat, mat, vec, mat, vec, vec, vec, mat, vec, mat, vec,
        ),
        check_vma=False,
    )
```

```python
import functools

import jax
import jax.numpy as jnp
from jax import lax
from jax.experimental import pallas as pl
from jax.experimental.pallas import tpu as pltpu
from jax.sharding import Mesh
from jax.sharding import PartitionSpec as P

HD = 64
EPS = 1e-05
LOG2E = 1.4426950408889634
SEQ = ("z", "y", "x")
ALL = SEQ + ("batch",)
WIDE = 4 * HD
LIMIT = 58
F32 = jnp.float32
BF16 = jnp.bfloat16
NN = ((1,), (0,))
NT = ((1,), (1,))
TN = ((0,), (0,))


def normalize(values):
    centre = jnp.mean(values, axis=-1, keepdims=True)
    centred = values - centre
    spread = jnp.mean(centred * centred, axis=-1, keepdims=True)
    factor = lax.rsqrt(spread + EPS)
    return (centred * factor, factor)


def norm_backward(grad_out, normed, factor, gain):
    grad_gain = jnp.sum(grad_out * normed, axis=0, keepdims=True)
    grad_shift = jnp.sum(grad_out, axis=0, keepdims=True)
    scaled = grad_out * gain.astype(F32)
    grad_in = factor * (
        scaled
        - jnp.mean(scaled, axis=-1, keepdims=True)
        - normed * jnp.mean(scaled * normed, axis=-1, keepdims=True)
    )
    return (grad_in, grad_gain, grad_shift)


def dot(left, right, dims=NN):
    return lax.dot_general(left, right, (dims, ((), ())), preferred_element_type=F32)


def swap(value, axis, step=1):
    size = lax.axis_size(axis)
    return lax.ppermute(value, axis, [(i, i ^ step) for i in range(size)])


def swap_plane(value, step):
    return lax.ppermute(value, ("y", "x"), [(i, i ^ step) for i in range(4)])


def after(value, *others):
    return lax.optimization_barrier((value,) + others)[0]


def split(length, most=512):
    return most if length % most == 0 else length


SMALL = pl.CostEstimate(flops=1, bytes_accessed=1, transcendentals=0)
SMEM_SPEC = pl.BlockSpec(memory_space=pltpu.SMEM)
HBM_SPEC = pl.BlockSpec(memory_space=pltpu.HBM)


def full_block(shape):
    zeros = (0,) * len(shape)
    return pl.BlockSpec(shape, lambda i: zeros, pipeline_mode=pl.Buffered(1))


def like(shape, dtype):
    return jax.ShapeDtypeStruct(shape, dtype)


def once(name, kernel, args, outs, scratch=(), limit=LIMIT, left=()):
    in_specs = [SMEM_SPEC if a.dtype == jnp.int32 else full_block(a.shape) for a in args]
    out_specs = [HBM_SPEC if i in left else full_block(o.shape) for i, o in enumerate(outs)]
    return pl.pallas_call(
        kernel,
        grid=(1,),
        out_shape=tuple(outs),
        in_specs=in_specs,
        out_specs=tuple(out_specs),
        scratch_shapes=list(scratch),
        compiler_params=pltpu.CompilerParams(vmem_limit_bytes=limit << 20),
        cost_estimate=SMALL,
        name=name,
    )(*args)


PLACE, PREFIX, CORE, FLAT, LINE = range(5)


def rank_of(scal, k, d, other):
    line = jnp.bitwise_xor(scal[LINE], k)
    flat = jnp.bitwise_xor(scal[FLAT], d)
    return (line * 4 + flat) * 2 + jnp.bitwise_xor(scal[CORE], other)


def rows_at(index, size):
    return pl.ds(pl.multiple_of(index * size, size), size)


def square_pieces(wq, other):
    outer = other.shape[0] // 4
    for d in range(4):
        for k in range(outer):
            yield (k, d, 0, wq[d].at[k])
            yield (k, d, 1, other.at[d * outer + k])


def pack_kernel(lines, heads, scal, token, w_out, w_up, w_q, w_k, w_v, *refs):
    vectors, (up_own, out_b, out_c, out_d, send) = (refs[:8], refs[8:])
    wide = w_up.shape[1] // (4 * lines)
    rows, cut = (token.shape[0], w_up.shape[0])
    for out in (out_b, out_c, out_d):
        out[:rows, :] = token[...]
        out[rows : rows + cut, :] = w_out[...]
    for z in range(lines):
        pieces = [w_up[:, (z * 4 + t) * wide : (z * 4 + t + 1) * wide] for t in range(4)]
        for k, (out, first) in enumerate(
            ((up_own, 0), (out_b, rows + cut), (out_c, rows + cut), (out_d, rows + cut))
        ):
            target = jnp.bitwise_xor(scal[FLAT], k)
            value = pieces[0]
            for t in range(1, 4):
                value = jnp.where(target == t, pieces[t], value)
            out[first : first + cut, z * wide : (z + 1) * wide] = value
    lane = jnp.concatenate([ref[...].astype(F32) for ref in vectors], axis=0)
    lane = jnp.concatenate([lane, jnp.zeros((8, 2 * HD - cut), F32)], axis=1)
    vec = jnp.concatenate([jnp.transpose(lane)[:cut], jnp.zeros((cut, HD - 8), F32)], axis=1)
    vec = vec.astype(BF16)
    for h in range(send.shape[0]):
        for i, w in enumerate((w_q, w_k, w_v)):
            if h < heads:
                piece = w[:, h * HD : (h + 1) * HD]
            else:
                piece = jnp.zeros((cut, HD), BF16)
            send[h, :, i * HD : (i + 1) * HD] = piece
        send[h, :, 3 * HD :] = vec


def forward_kernel(
    heads, scal, ahead, own_b, own_c, own_d, zc, xc, yc, xya, xyb, w,
    n1_out, n0_out, qkvt, ctxc, ctxt, lse, rows_out, wt_out, wo_out,
    n1, n0, k_s, w_s, sems,
):
    place, prefix = (scal[PLACE], scal[PREFIX])
    outer = zc.shape[0] + 1
    length, width = n1.shape
    rows = length // (4 * outer)
    cut = w.shape[2]
    blk = split(length)
    copies = []
    near = ((ahead, 0), (own_b, 1), (own_c, 2), (own_d, 3))
    along = ((zc, 1, 0), (xc, 1, 1), (yc, 1, 2), (xya, 1, 3), (xyb, outer // 2 + 1, 3))
    for src, d in near:
        pair = (src.at[rows : rows + cut, :], wo_out.at[d * outer])
        copies.append(pltpu.make_async_copy(*pair, sems.at[2 + len(copies)]))
    for src, k, d in along:
        target = wo_out.at[d * outer + k : d * outer + k + src.shape[0]]
        copies.append(pltpu.make_async_copy(src.at[:, rows:, :], target, sems.at[2 + len(copies)]))
    for copy in copies:
        copy.start()
    head = jnp.minimum(place, heads - 1)
    for b in range(2):
        for i in range(w.shape[1]):
            at = (2 * i + b) * cut
            w_s[at : at + cut, :] = w[b, i].astype(F32)
    turned = jnp.transpose(w_s[...])
    wt_out[...] = turned[: 3 * HD].astype(BF16)
    rows_in = turned[3 * HD : 3 * HD + 8]
    rows_out[...] = rows_in
    gain = rows_in[0:1]
    shift = rows_in[1:2]

    def norm_rows(value, k, d):
        normed, _ = normalize(value.astype(F32))
        here = rows_at(jnp.bitwise_xor(place, k * 4 + d), rows)
        n0[here, :] = normed.astype(BF16)
        n1[here, :] = (normed * gain + shift).astype(BF16)

    for src, d in near:
        norm_rows(src[:rows, :], 0, d)
    for src, first, d in along:

        def one(k, carry, src=src, first=first, d=d):
            norm_rows(src[k, :rows, :], first + k, d)
            return carry

        lax.fori_loop(0, src.shape[0], one, 0)
    for i, (src, dst) in enumerate(((n1, n1_out), (n0, n0_out))):
        copy = pltpu.make_async_copy(src, dst, sems.at[i])
        copy.start()
        copies.append(copy)
    bias_q = w_s[rows_at(head, HD), 3 * HD + 2 : 3 * HD + 3]
    bias_v = w_s[rows_at(head, HD), 3 * HD + 3 : 3 * HD + 4]
    for i in range(length // blk):
        sl = slice(i * blk, (i + 1) * blk)
        part = dot(wt_out[...], n1[sl, :], NT)
        k_part = part[HD : 2 * HD].astype(BF16)
        qkvt[:HD, sl] = (part[:HD] + bias_q).astype(BF16)
        qkvt[HD : 2 * HD, sl] = k_part
        qkvt[2 * HD :, sl] = (part[2 * HD :] + bias_v).astype(BF16)
        k_s[sl, :] = jnp.transpose(k_part.astype(F32)).astype(BF16)
    scale = 0.125 * LOG2E

    wide, deep = (split(length, 1024), split(length, 1024))

    def one_query(i, carry):
        first = pl.multiple_of(i * wide, wide)
        q_now = qkvt[:HD, pl.ds(first, wide)]

        def step(masked, j, state):
            top, total, acc = state
            start = pl.multiple_of(j * deep, deep)
            scores = dot(k_s[pl.ds(start, deep), :], q_now) * scale
            if masked:
                key = start + lax.broadcasted_iota(jnp.int32, (deep, wide), 0)
                query = first + lax.broadcasted_iota(jnp.int32, (deep, wide), 1)
                scores = jnp.where((key <= query) | (key < prefix), scores, -1e30)
            new_top = jnp.maximum(top, jnp.max(scores, axis=0, keepdims=True))
            prob = jnp.exp2(scores - new_top)
            fade = jnp.exp2(top - new_top)
            total = total * fade + jnp.sum(prob, axis=0, keepdims=True)
            acc = acc * fade + dot(qkvt[2 * HD :, pl.ds(start, deep)], prob.astype(BF16))
            return (new_top, total, acc)

        state = (
            jnp.full((1, wide), -1e30, F32),
            jnp.zeros((1, wide), F32),
            jnp.zeros((HD, wide), F32),
        )
        full = jnp.maximum(prefix // deep, first // deep)
        needed = jnp.maximum((prefix + deep - 1) // deep, (first + wide + deep - 1) // deep)
        state = lax.fori_loop(0, full, functools.partial(step, False), state)
        top, total, acc = lax.fori_loop(full, needed, functools.partial(step, True), state)
        out = acc / total
        ctxt[:, pl.ds(first, wide)] = out
        lse[:, pl.ds(first, wide)] = top + jnp.log2(total)
        for r in range(wide // rows):
            ctxc[i * (wide // rows) + r] = out[:, r * rows : (r + 1) * rows].astype(BF16)
        return carry

    lax.fori_loop(0, length // wide, one_query, 0)
    for copy in copies:
        copy.wait()


def backward_kernel(
    scal, qkvt, dcr, ctxt, lse, dchunk, dall, q_s, k_s, v_s, dc_s, dct_s, del_s, dq_s, dk_s, dv_s
):
    prefix = scal[PREFIX]
    rows = dcr.shape[2]
    length = qkvt.shape[1]
    blk = split(length)
    count = length // blk
    for i in range(count):
        sl = slice(i * blk, (i + 1) * blk)
        turned = jnp.transpose(qkvt[:, sl].astype(F32)).astype(BF16)
        q_s[sl, :] = turned[:, :HD]
        k_s[sl, :] = turned[:, HD : 2 * HD]
        v_s[sl, :] = turned[:, 2 * HD :]
    for i in range(length // rows):
        sl = slice(i * rows, (i + 1) * rows)
        dct_s[:, sl] = dcr[i]
        dc_s[sl, :] = jnp.transpose(dcr[i].astype(F32)).astype(BF16)
    del_s[...] = jnp.sum(dct_s[...].astype(F32) * ctxt[...], axis=0, keepdims=True)
    dq_s[...] = jnp.zeros_like(dq_s)
    scale = 0.125 * LOG2E

    wide, deep = (split(length, 512), split(length, 512))

    def one_key(j, carry):
        start = pl.multiple_of(j * deep, deep)
        dk_s[...] = jnp.zeros_like(dk_s)
        dv_s[...] = jnp.zeros_like(dv_s)

        def step(masked, i, inner):
            first = pl.multiple_of(i * wide, wide)
            here = pl.ds(first, wide)
            scores = dot(k_s[pl.ds(start, deep), :], qkvt[:HD, here]) * scale
            prob = jnp.exp2(scores - lse[:, here])
            if masked:
                key = start + lax.broadcasted_iota(jnp.int32, (deep, wide), 0)
                query = first + lax.broadcasted_iota(jnp.int32, (deep, wide), 1)
                prob = jnp.where((key <= query) | (key < prefix), prob, 0.0)
            d_prob = dot(v_s[pl.ds(start, deep), :], dct_s[:, here])
            d_score = (prob * (d_prob - del_s[:, here])).astype(BF16)
            dv_s[...] += dot(prob.astype(BF16), dc_s[here, :])
            dk_s[...] += dot(d_score, q_s[here, :])
            dq_s[:, here] += dot(qkvt[HD : 2 * HD, pl.ds(start, deep)], d_score)
            return inner

        begin = jnp.where(start < prefix, 0, start // wide)
        middle = jnp.where(start + deep <= prefix, begin, (start + deep + wide - 2) // wide)
        lax.fori_loop(begin, middle, functools.partial(step, True), 0)
        lax.fori_loop(middle, length // wide, functools.partial(step, False), 0)
        d_key = jnp.transpose(dk_s[...] * 0.125).astype(BF16)
        d_value = jnp.transpose(dv_s[...]).astype(BF16)
        dall[HD : 2 * HD, pl.ds(start, deep)] = d_key
        dall[2 * HD :, pl.ds(start, deep)] = d_value
        for r in range(deep // rows):
            at = j * (deep // rows) + r
            dchunk[at, HD : 2 * HD, :] = d_key[:, r * rows : (r + 1) * rows]
            dchunk[at, 2 * HD :, :] = d_value[:, r * rows : (r + 1) * rows]
        return carry

    lax.fori_loop(0, length // deep, one_key, 0)
    for i in range(count):
        sl = slice(i * blk, (i + 1) * blk)
        d_query = (dq_s[:, sl] * 0.125).astype(BF16)
        dall[:HD, sl] = d_query
        for r in range(blk // rows):
            dchunk[i * (blk // rows) + r, :HD, :] = d_query[:, r * rows : (r + 1) * rows]


def stacked(pieces, first, last):
    return jnp.concatenate([piece[first:last, :].astype(F32) for piece in pieces]).astype(BF16)


def out_pieces(own, other):
    outer = own.shape[0] // 4
    return [
        (i % outer, i // outer, core, ref.at[i])
        for core, ref in ((0, own), (1, other))
        for i in range(own.shape[0])
    ]


def middle_kernel(heads, scal, ctx, own, other, token, rows_in, middle, norm_two, plain, moved):
    pieces = out_pieces(own, other)
    cut = own.shape[1]
    plain[...] = ctx[:heads].reshape(plain.shape).astype(F32)
    for n, (k, d, core, _) in enumerate(pieces):
        moved[n * cut : (n + 1) * cut, :] = plain[rows_at(rank_of(scal, k, d, core), cut), :]
    turned = jnp.transpose(moved[...]).astype(BF16)
    product = dot(turned, stacked([p[3] for p in pieces], 0, cut))
    value = token[...].astype(F32) + product + rows_in[4:5, :]
    middle[...] = value
    normed, _ = normalize(value)
    norm_two[...] = (normed * rows_in[5:6, :] + rows_in[6:7, :]).astype(BF16)


def feed_kernel(
    scal, n2_a, n2_b, n2_c, n2_d, dy_a, dy_b, dy_c, dy_d, ffz, ffc,
    out_keep, out_b, out_c, out_d, dn_keep, dn_b, dn_c, dn_d, send, keep,
    n2, dy, down, up, act, d_pre, down_s, up_s, bias,
):
    outer = ffz.shape[0]
    cut = (ffz.shape[1] - 8) // 8
    half = 4 * cut
    order = (0, 2, 1, 3)
    sources = [
        (src.at[i], k, core) for core, src in ((0, ffz), (1, ffc)) for i, k in enumerate(order)
    ]

    def block_of(k, core):
        line = jnp.bitwise_xor(scal[LINE], k)
        return line * 2 + jnp.bitwise_xor(scal[CORE], core)

    rows = []
    for src, k, core in sources:
        down[rows_at(block_of(k, core), half), :] = src[:half, :]
        for d in range(4):
            here = rows_at(rank_of(scal, k, d, core), cut)
            up_s[here, :] = src[half + d * cut : half + (d + 1) * cut, :].astype(F32)
        rows.append((block_of(k, core), src[2 * half :, :half].astype(F32)[:1]))
    up[...] = up_s[...].astype(BF16)
    for q in range(2 * outer):
        bias[:, q * half : (q + 1) * half] = sum(jnp.where(at == q, row, 0.0) for at, row in rows)
    count = n2_a.shape[0]
    for i, piece in enumerate((n2_a, n2_b, n2_c, n2_d)):
        n2[i * count : (i + 1) * count, :] = piece[...]
    for i, piece in enumerate((dy_a, dy_b, dy_c, dy_d)):
        dy[i * count : (i + 1) * count, :] = piece[piece.shape[0] - count :, :]
    tile = 256
    for c in range(down.shape[0] // tile):
        sl = slice(c * tile, (c + 1) * tile)
        pre = dot(n2[...], up[:, sl]) + bias[:, sl]
        cdf = 0.5 * (1.0 + lax.erf(pre * 0.7071067811865476))
        act[:, sl] = (pre * cdf).astype(BF16)
        slope = cdf + pre * jnp.exp(-0.5 * pre * pre) * 0.3989422804014327
        d_pre[:, sl] = (dot(dy[...], down[sl, :], NT) * slope).astype(BF16)
    back = dot(d_pre[...], up[...], NT)
    for i, ref in enumerate((dn_keep, dn_b, dn_c, dn_d)):
        ref[...] = back[i * count : (i + 1) * count].astype(ref.dtype)
    out = dot(act[...], down[...])
    for i, ref in enumerate((out_keep, out_b, out_c, out_d)):
        ref[...] = out[i * count : (i + 1) * count].astype(ref.dtype)
    down_s[...] = dot(act[...], dy[...], TN)
    up_s[...] = dot(n2[...], d_pre[...], TN)
    total = jnp.sum(d_pre[...].astype(F32), axis=0, keepdims=True)
    width = keep.shape[2]
    for k in range(outer):
        for core, ref in ((0, keep), (1, send)):
            at = block_of(k, core)
            ref[k, :half, :] = down_s[rows_at(at, half), :].astype(ref.dtype)
            for t in range(4):
                line = jnp.bitwise_xor(scal[LINE], k)
                rank = (line * 4 + t) * 2 + jnp.bitwise_xor(scal[CORE], core)
                here = slice(half + t * cut, half + (t + 1) * cut)
                ref[k, here, :] = up_s[rows_at(rank, cut), :].astype(ref.dtype)
            part = sum(
                jnp.where(at == q, total[:, q * half : (q + 1) * half], 0.0)
                for q in range(2 * outer)
            )
            part = jnp.concatenate([part, jnp.zeros((1, width - half), F32)], axis=1)
            ref[k, 2 * half :, :] = jnp.broadcast_to(part, (8, width)).astype(ref.dtype)


def turn_kernel(
    heads, scal, keep, got_b, got_c, got_d, middle, d_out, own, other, rows_in, ctx,
    d_middle, d_branch_out, d_ctx, sums, wo_keep, wo_send, plain, full,
):
    d_norm = keep[...] + (got_b[...].astype(F32) + got_c[...].astype(F32)) + got_d[...].astype(F32)
    normed, factor = normalize(middle[...])
    grad_in, grad_gain, grad_shift = norm_backward(d_norm, normed, factor, rows_in[5:6, :])
    grad_up = d_out[...].astype(F32)
    total = grad_up + grad_in
    low = total.astype(BF16)
    d_middle[...] = total
    d_branch_out[...] = low[:8]
    pieces = out_pieces(own, other)
    cut = own.shape[1]
    back = dot(stacked([p[3] for p in pieces], 0, cut), low, NT)
    for n, (k, d, core, _) in enumerate(pieces):
        plain[rows_at(rank_of(scal, k, d, core), cut), :] = back[n * cut : (n + 1) * cut]
    seq, rows = (d_ctx.shape[0], d_ctx.shape[2])
    d_ctx[:heads] = plain[...].astype(BF16).reshape(heads, HD, rows)
    d_ctx[heads:] = jnp.zeros((seq - heads, HD, rows), BF16)
    sums[0:1, :] = jnp.sum(low.astype(F32), axis=0, keepdims=True)
    sums[1:2, :] = grad_gain
    sums[2:3, :] = grad_shift
    sums[3:4, :] = jnp.sum(grad_up, axis=0, keepdims=True)
    sums[4:, :] = jnp.zeros((4, sums.shape[1]), F32)
    full[...] = dot(ctx[:heads].reshape(heads * HD, rows), low).reshape(full.shape)
    for i in range(seq):
        wo_keep[i] = full[2 * i + scal[CORE]]
        wo_send[i] = full[2 * i + 1 - scal[CORE]].astype(BF16)


def fold_kernel(keep, got, own, away):
    for i, (k, ref) in enumerate(((0, own), (2, own), (1, away), (3, away))):
        ref[i % 2] = (keep[k] + got[k].astype(F32)).astype(ref.dtype)


def second_kernel(keep, got, own, away):
    own[...] = keep[0] + got[0].astype(F32)
    away[...] = (keep[1] + got[1].astype(F32)).astype(BF16)


def finish_kernel(scal, keep, *refs):
    got, (wo_keep, wo_got, out_b, out_c, out_d), outs = (refs[:-13], refs[-13:-8], refs[-8:])
    grad_down, bias, own, wo_own, away_b, away_c, away_d, total = outs
    value = keep[...]
    for ref in got:
        value = value + ref[...].astype(F32)
    total[...] = value
    half = grad_down.shape[0]
    cut = half // 4
    lines = wo_own.shape[0]
    grad_down[...] = value[:half]
    bias[...] = value[2 * half : 2 * half + 1, :half]
    for k, ref in enumerate((own, away_b, away_c, away_d)):
        at = jnp.bitwise_xor(scal[FLAT], k)
        here = pl.ds(pl.multiple_of(half + at * cut, 8), cut)
        ref[:cut, :] = total[here, :].astype(BF16)
        for z in range(lines):
            part = wo_keep[4 * z + at] + wo_got[4 * z + at].astype(F32)
            if k:
                ref[(1 + z) * cut : (2 + z) * cut, :] = part.astype(BF16)
            else:
                wo_own[z] = part
    for src, ref in ((out_b, away_b), (out_c, away_c), (out_d, away_d)):
        ref[(1 + lines) * cut :, :] = src[...]


def close_kernel(
    lines, scal, own, wo_own, got_b, got_c, got_d, middle, out_keep, rows_in,
    layer_out, grad_up, grad_out, *away,
):
    cut = grad_out.shape[0]
    got = (got_b, got_c, got_d)
    value = middle[...] + out_keep[...] + rows_in[7:8, :]
    pieces = [own[...].astype(F32)]
    for ref in got:
        value = value + ref[(1 + lines) * cut :, :].astype(F32)
        pieces.append(ref[:cut, :].astype(F32))
    layer_out[...] = value.astype(BF16)
    for k, out in enumerate((grad_out,) + away):
        at = jnp.bitwise_xor(scal[LINE], k)
        here = pl.ds(pl.multiple_of((1 + at) * cut, 8), cut)
        part = wo_own[at]
        for ref in got:
            part = part + ref[here, :].astype(F32)
        out[...] = part.astype(out.dtype)
    wide = own.shape[1] // lines
    for t in range(4):
        step = jnp.bitwise_xor(scal[FLAT], t)
        piece = pieces[0]
        for k in range(1, 4):
            piece = jnp.where(step == k, pieces[k], piece)
        for z in range(lines):
            at = (z * 4 + t) * wide
            grad_up[:, at : at + wide] = piece[:, z * wide : (z + 1) * wide]


def heads_kernel(heads, scal, dall, n1, n0, wt, sums, keep, send, gh, gm, cs, full):
    step = pl.program_id(0)

    @pl.when(step == 0)
    def _():
        gh[...] = jnp.zeros_like(gh)
        gm[...] = jnp.zeros_like(gm)
        cs[...] = jnp.zeros_like(cs)

    gh[...] += dot(dall[...], n1[...])
    gm[...] += dot(dall[...], n0[...])
    cs[...] += dot(dall[...], jnp.ones((dall.shape[1], 2 * HD), BF16))

    @pl.when(step == pl.num_programs(0) - 1)
    def _():
        place = scal[PLACE]
        width = gh.shape[1]
        live = place < heads
        wide = wt[...].astype(F32)
        gain = jnp.where(live, jnp.sum(wide * gm[...], axis=0, keepdims=True), 0.0)
        shift = jnp.where(live, jnp.sum(wide * cs[:, :1], axis=0, keepdims=True), 0.0)
        line = jnp.transpose(cs[...])[0:1]
        mine = lax.broadcasted_iota(jnp.int32, (1, width), 1) // HD == place
        b_q = jnp.where(mine, jnp.concatenate([line[:, :HD]] * heads, axis=1), 0.0)
        b_v = jnp.where(mine, jnp.concatenate([line[:, 2 * HD :]] * heads, axis=1), 0.0)
        vec = jnp.concatenate([gain, shift, b_q, b_v, sums[:4, :]], axis=0)
        pad = jnp.zeros((width, HD - 8), F32)
        block = jnp.concatenate([jnp.transpose(gh[...]), jnp.transpose(vec), pad], axis=1)
        full[...] = block.reshape(full.shape)
        for i in range(keep.shape[0]):
            keep[i] = full[2 * i + scal[CORE]]
            send[i] = full[2 * i + 1 - scal[CORE]].astype(BF16)


def head_grads(scal, dall, n1, n0, wt, sums, heads, seq):
    length, width = n1.shape
    blk = split(length, 1024)
    cut = width // (2 * seq)
    outs = (like((seq, cut, WIDE), F32), like((seq, cut, WIDE), BF16))
    return pl.pallas_call(
        functools.partial(heads_kernel, heads),
        out_shape=outs,
        grid=(length // blk,),
        in_specs=[
            SMEM_SPEC,
            pl.BlockSpec((3 * HD, blk), lambda i: (0, i)),
            pl.BlockSpec((blk, width), lambda i: (i, 0)),
            pl.BlockSpec((blk, width), lambda i: (i, 0)),
            full_block(wt.shape),
            full_block(sums.shape),
        ],
        out_specs=tuple(full_block(out.shape) for out in outs),
        scratch_shapes=[
            pltpu.VMEM((3 * HD, width), F32),
            pltpu.VMEM((3 * HD, width), F32),
            pltpu.VMEM((3 * HD, 2 * HD), F32),
            pltpu.VMEM((2 * seq, cut, WIDE), F32),
        ],
        compiler_params=pltpu.CompilerParams(vmem_limit_bytes=LIMIT << 20),
        cost_estimate=SMALL,
        name="heads",
    )(scal, dall, n1, n0, wt, sums)


def last_kernel(
    heads, scal, d_rows, wq_a, wq_b, wq_c, wq_d, other, token, d_middle, rows_in, grad_tokens, plain
):
    cut = other.shape[1] // 3
    pieces = list(square_pieces((wq_a, wq_b, wq_c, wq_d), other))
    total = 0.0
    for i in range(3):
        part = jnp.concatenate(
            [d_rows[h, i * HD : (i + 1) * HD, :].astype(F32) for h in range(heads)], axis=0
        )
        weights = stacked([p[3] for p in pieces], i * cut, (i + 1) * cut)
        total = total + dot(weights, part.astype(BF16))
    for n, (k, d, core, _) in enumerate(pieces):
        plain[rows_at(rank_of(scal, k, d, core), cut), :] = total[n * cut : (n + 1) * cut]
    normed, factor = normalize(token[...].astype(F32))
    grad_in, _, _ = norm_backward(jnp.transpose(plain[...]), normed, factor, rows_in[0:1, :])
    grad_tokens[...] = d_middle[...] + grad_in


def unpack_kernel(heads, got, g_q, g_k, g_v, *vec):
    for i, out in enumerate((g_q, g_k, g_v)):
        for h in range(heads):
            out[:, h * HD : (h + 1) * HD] = got[h, :, i * HD : (i + 1) * HD].astype(F32)
    total = got[0, :, 2 * HD :].astype(F32)
    for s in range(1, got.shape[0]):
        total = total + got[s, :, 2 * HD :].astype(F32)
    cut = total.shape[0]
    total = jnp.concatenate([total, jnp.zeros((2 * HD - cut, 2 * HD), F32)], axis=0)
    total = jnp.transpose(total)
    for i, out in enumerate(vec):
        out[...] = total[HD + i : HD + i + 1, :cut]


def body(
    tokens, cotangent, prefix_len, gain_one, shift_one, w_query, b_query, w_key, w_value, b_value,
    w_output, b_output, gain_two, shift_two, w_up, b_up, w_down, b_down,
):
    outer = lax.axis_size("z")
    seq = 4 * outer
    token, d_out = (tokens[0], cotangent[0])
    rows, width = token.shape
    length = seq * rows
    heads = width // HD
    cut = w_query.shape[0]
    half = w_down.shape[0]
    local = w_up.shape[1] // 4
    flat = lax.axis_index(("y", "x"))
    places = (lax.axis_index(SEQ), prefix_len[0], lax.axis_index("batch"), flat, lax.axis_index("z"))
    scal = jnp.stack(places).astype(jnp.int32)

    ahead = jnp.concatenate([token, w_output])
    zc = jnp.stack([swap(ahead, "z", k) for k in range(1, outer)])
    vectors = (
        gain_one, shift_one, b_query, b_value, b_output, gain_two, shift_two, b_down,
    )
    vectors = [value[None] for value in vectors]
    up_own, *first, send = once(
        "pack",
        functools.partial(pack_kernel, outer, heads),
        (scal, token, w_output, w_up, w_query, w_key, w_value, *vectors),
        [like((cut, local), BF16)]
        + [like((rows + 2 * cut, width), BF16)] * 3
        + [like((seq, cut, WIDE), BF16)],
    )
    first = [swap_plane(part, k + 1) for k, part in enumerate(first)]
    zc = after(zc, *first)
    xc = swap(zc, "x")
    yc = swap(zc, "y")
    head_w = lax.all_to_all(after(send, zc), SEQ, split_axis=0, concat_axis=0, tiled=True)
    wq = after(jnp.concatenate([w_query, w_key, w_value]), zc)
    wq_got = [swap(wq, "z", k) for k in range(1, outer)]
    b_up_row = jnp.pad(b_up[None], ((0, 7), (0, width - half)))
    ff = [w_down, up_own] + [part[rows + cut :] for part in first] + [b_up_row]
    ff = after(jnp.concatenate(ff), *wq_got)
    head_w = lax.all_gather(head_w, "batch", axis=0, tiled=False)
    xc, yc, head_w, wq_got = lax.optimization_barrier((xc, yc, head_w, wq_got))
    xya = swap(xc[: outer // 2], "y")
    xyb = swap(yc[outer // 2 :], "x")

    ff = jnp.stack([ff, swap(ff, "z", 2)])
    ff_got = swap(ff, "z", 1)
    wq = after(jnp.stack([wq] + wq_got), xya, xyb)
    wq = [wq] + [swap_plane(wq, k) for k in range(1, 4)]

    norm_one, norm_raw, qkvt, ctxc, ctxt, lse, rows_in, wt, w_out_own = once(
        "forward",
        functools.partial(forward_kernel, heads),
        (scal, ahead, *first, zc, xc, yc, xya, xyb, head_w),
        [
            like((length, width), BF16),
            like((length, width), BF16),
            like((3 * HD, length), BF16),
            like((seq, HD, rows), BF16),
            like((HD, length), F32),
            like((1, length), F32),
            like((8, width), F32),
            like((3 * HD, width), BF16),
            like((seq, cut, width), BF16),
        ],
        [
            pltpu.VMEM((length, width), BF16),
            pltpu.VMEM((length, width), BF16),
            pltpu.VMEM((length, HD), BF16),
            pltpu.VMEM((width, WIDE), F32),
            pltpu.SemaphoreType.DMA((11,)),
        ],
        left=(0, 1, 8),
    )
    w_out_other = swap(w_out_own, "batch")
    ctxc, wq, ff_got = lax.optimization_barrier((ctxc, wq, ff_got))
    ffz = jnp.concatenate([ff, ff_got])
    dy = [d_out] + [swap_plane(after(d_out, ctxc), k) for k in range(1, 4)]
    ctx = lax.all_to_all(ctxc, SEQ, split_axis=0, concat_axis=0, tiled=True)
    ffc = swap(ffz, "batch")
    dy, ctx = lax.optimization_barrier((dy, ctx))
    middle, norm_two = once(
        "middle",
        functools.partial(middle_kernel, heads),
        (scal, ctx, w_out_own, w_out_other, token, rows_in),
        [like((rows, width), F32), like((rows, width), BF16)],
        [pltpu.VMEM((width, rows), F32)] * 2,
    )
    n2 = [norm_two] + [swap_plane(norm_two, k) for k in range(1, 4)]

    part = [like((rows, width), F32)] + [like((rows, width), BF16)] * 3
    fed = once(
        "feed",
        feed_kernel,
        (scal, *n2, *dy, ffz, ffc),
        part + part + [like(ffz.shape, BF16), like(ffz.shape, F32)],
        [
            pltpu.VMEM((4 * rows, width), BF16),
            pltpu.VMEM((4 * rows, width), BF16),
            pltpu.VMEM((local, width), BF16),
            pltpu.VMEM((width, local), BF16),
            pltpu.VMEM((4 * rows, local), BF16),
            pltpu.VMEM((4 * rows, local), BF16),
            pltpu.VMEM((local, width), F32),
            pltpu.VMEM((width, local), F32),
            pltpu.VMEM((1, local), F32),
        ],
    )
    out_keep, *out_send = fed[:4]
    dn_keep, *dn_send = fed[4:8]
    send, keep = fed[8:]
    dn_got = [swap_plane(value, k + 1) for k, value in enumerate(dn_send)]

    count = 2 * half + 8
    pair = like((2, count, width), F32)
    own, away = once(
        "fold",
        fold_kernel,
        (keep, after(swap(send, "batch"), *dn_got)),
        [pair, like(pair.shape, BF16)],
    )
    dn_keep, _ = lax.optimization_barrier((dn_keep, away))
    d_middle, _, d_ctx, sums, wo_keep, wo_send = once(
        "turn",
        functools.partial(turn_kernel, heads),
        (scal, dn_keep, *dn_got, middle, d_out, w_out_own, w_out_other, rows_in, ctx),
        [
            like((rows, width), F32),
            like((8, width), BF16),
            like((seq, HD, rows), BF16),
            like((8, width), F32),
            like((seq, cut, width), F32),
            like((seq, cut, width), BF16),
        ],
        [pltpu.VMEM((width, rows), F32), pltpu.VMEM((2 * seq, cut, width), F32)],
    )
    d_ctx = lax.all_to_all(d_ctx, SEQ, split_axis=0, concat_axis=0, tiled=True)

    wo_got = swap(wo_send, "batch")
    own, away = once(
        "second",
        second_kernel,
        (own, swap(away, "z", 1)),
        [like((count, width), F32), like((count, width), BF16)],
    )
    back = [swap(away, "z", 2)]

    blk = split(length)
    dchunk, dall = once(
        "backward",
        backward_kernel,
        (after(scal, away), qkvt, d_ctx, ctxt, lse),
        [like((seq, 3 * HD, rows), BF16), like((3 * HD, length), BF16)],
        [
            pltpu.VMEM((length, HD), BF16),
            pltpu.VMEM((length, HD), BF16),
            pltpu.VMEM((length, HD), BF16),
            pltpu.VMEM((length, HD), BF16),
            pltpu.VMEM((HD, length), BF16),
            pltpu.VMEM((1, length), F32),
            pltpu.VMEM((HD, length), F32),
            pltpu.VMEM((split(length, 512), HD), F32),
            pltpu.VMEM((split(length, 512), HD), F32),
        ],
    )
    back, dchunk = lax.optimization_barrier((back, dchunk))
    d_rows = lax.all_to_all(dchunk, SEQ, split_axis=0, concat_axis=0, tiled=True)

    grad_w_down, bias, own, wo_own, *away = once(
        "finish",
        finish_kernel,
        (scal, own, *back, wo_keep, wo_got, *out_send),
        [
            like((half, width), F32),
            like((1, half), F32),
            like((cut, width), BF16),
            like((outer, cut, width), F32),
        ]
        + [like(((1 + outer) * cut + rows, width), BF16)] * 3,
        [pltpu.VMEM((count, width), F32)],
    )
    got = [swap_plane(value, k + 1) for k, value in enumerate(away)]
    last, send = head_grads(scal, dall, norm_one, norm_raw, wt, sums, heads, seq)
    last = last + swap(send, "batch").astype(F32)
    last = after(last.astype(BF16), d_rows)
    other = swap(after(jnp.concatenate(wq), dall), "batch")
    grad_tokens = once(
        "last",
        functools.partial(last_kernel, heads),
        (scal, d_rows, *wq, other, token, d_middle, rows_in),
        [like((rows, width), F32)],
        [pltpu.VMEM((width, rows), F32)],
    )[0]
    last = lax.all_to_all(last, SEQ, split_axis=0, concat_axis=0, tiled=True)
    mat = like((cut, width), F32)
    grad_w_query, grad_w_key, grad_w_value, *vec = once(
        "unpack",
        functools.partial(unpack_kernel, heads),
        (last,),
        [mat, mat, mat] + [like((1, cut), F32)] * 8,
    )
    layer_out, grad_w_up, grad_w_output, *away = once(
        "close",
        functools.partial(close_kernel, outer),
        (scal, own, wo_own, *got, after(middle, grad_tokens), out_keep, rows_in),
        [like((rows, width), BF16), like((cut, 4 * local), F32), like((cut, width), F32)]
        + [like((cut, width), BF16)] * (outer - 1),
    )
    grad_w_output = grad_w_output + sum(
        swap(value, "z", k + 1).astype(F32) for k, value in enumerate(away)
    )

    return (
        layer_out[None],
        grad_tokens[None],
        vec[0][0],
        vec[1][0],
        grad_w_query,
        vec[2][0],
        grad_w_key,
        grad_w_value,
        vec[3][0],
        grad_w_output,
        vec[4][0],
        vec[5][0],
        vec[6][0],
        grad_w_up,
        bias[0],
        grad_w_down,
        vec[7][0],
    )


def over_rows(left, right):
    return lax.dot_general(
        left, right, (((0,), (0,)), ((), ())), preferred_element_type=jnp.float32
    )


def over_cols(left, right):
    return lax.dot_general(
        left, right, (((1,), (1,)), ((), ())), preferred_element_type=jnp.float32
    )


def pair_scores(q_part, k_part, row_ids, col_ids, prefix):
    scores = jnp.einsum("qhd,khd->hqk", q_part, k_part, preferred_element_type=jnp.float32) * 0.125
    allowed = (col_ids[None, :] <= row_ids[:, None]) | (col_ids[None, :] < prefix)
    return (jnp.where(allowed[None], scores, -1e30), allowed)


def grad_terms(q_part, do_part, lse_part, delta_part, k_part, v_part, row_ids, col_ids, prefix):
    scores, allowed = pair_scores(q_part, k_part, row_ids, col_ids, prefix)
    attn_prob = jnp.where(allowed[None], jnp.exp(scores - lse_part[:, :, None]), 0.0)
    prob_low = attn_prob.astype(jnp.bfloat16)
    d_prob = jnp.einsum("qhd,khd->hqk", do_part, v_part, preferred_element_type=jnp.float32)
    d_score = (attn_prob * (d_prob - delta_part[:, :, None])).astype(jnp.bfloat16)
    return (prob_low, d_score)


def plain_body(
    tokens,
    cotangent,
    prefix_len,
    gain_one,
    shift_one,
    w_query,
    b_query,
    w_key,
    w_value,
    b_value,
    w_output,
    b_output,
    gain_two,
    shift_two,
    w_up,
    b_up,
    w_down,
    b_down,
):
    shards = (
        gain_one,
        shift_one,
        w_query,
        b_query,
        w_key,
        w_value,
        b_value,
        w_output,
        b_output,
        gain_two,
        shift_two,
        w_up,
        b_up,
        w_down,
        b_down,
    )
    gathered = (
        lax.all_gather(shards[0], ("seq", "batch"), axis=0, tiled=True),
        lax.all_gather(shards[1], ("seq", "batch"), axis=0, tiled=True),
        lax.all_gather(shards[2], ("seq", "batch"), axis=0, tiled=True),
        lax.all_gather(shards[3], ("seq", "batch"), axis=0, tiled=True),
        lax.all_gather(shards[4], ("seq", "batch"), axis=0, tiled=True),
        lax.all_gather(shards[5], ("seq", "batch"), axis=0, tiled=True),
        lax.all_gather(shards[6], ("seq", "batch"), axis=0, tiled=True),
        lax.all_gather(shards[7], ("seq", "batch"), axis=0, tiled=True),
        lax.all_gather(shards[8], ("seq", "batch"), axis=0, tiled=True),
        lax.all_gather(shards[9], ("seq", "batch"), axis=0, tiled=True),
        lax.all_gather(shards[10], ("seq", "batch"), axis=0, tiled=True),
        lax.all_gather(shards[11], ("seq", "batch"), axis=0, tiled=True),
        lax.all_gather(shards[12], ("seq", "batch"), axis=0, tiled=True),
        lax.all_gather(shards[13], ("seq", "batch"), axis=0, tiled=True),
        lax.all_gather(shards[14], ("seq", "batch"), axis=0, tiled=True),
    )
    (
        ga_full,
        sa_full,
        wq_full,
        bq_full,
        wk_full,
        wv_full,
        bv_full,
        wo_full,
        bo_full,
        gb_full,
        sb_full,
        wu_full,
        bu_full,
        wd_full,
        bd_full,
    ) = gathered
    hidden = tokens[0].astype(jnp.float32)
    local_rows = hidden.shape[0]
    width = hidden.shape[1]
    heads = width // HD
    prefix = prefix_len[0]
    start_row = lax.axis_index("seq") * local_rows
    last_row = start_row + local_rows - 1
    length = local_rows * lax.axis_size("seq")
    block_rows = min(512, length)
    block_count = length // block_rows
    row_ids = start_row + jnp.arange(local_rows, dtype=jnp.int32)
    block_ids = jnp.arange(block_count, dtype=jnp.int32)
    normed_one, factor_one = normalize(hidden)
    norm_one = (normed_one * ga_full.astype(jnp.float32) + sa_full.astype(jnp.float32)).astype(
        jnp.bfloat16
    )
    q_low = (
        jnp.dot(norm_one, wq_full, preferred_element_type=jnp.float32) + bq_full.astype(jnp.float32)
    ).astype(jnp.bfloat16)
    k_low = jnp.dot(norm_one, wk_full, preferred_element_type=jnp.float32).astype(jnp.bfloat16)
    v_low = (
        jnp.dot(norm_one, wv_full, preferred_element_type=jnp.float32) + bv_full.astype(jnp.float32)
    ).astype(jnp.bfloat16)
    k_all, v_all = (
        lax.all_gather(k_low, "seq", axis=0, tiled=True),
        lax.all_gather(v_low, "seq", axis=0, tiled=True),
    )
    q_heads = q_low.reshape(local_rows, heads, HD)

    def lse_step(state, item):
        k_part, index = item
        col_ids = index * block_rows + jnp.arange(block_rows, dtype=jnp.int32)

        def lse_update(current):
            scores, allowed = pair_scores(q_heads, k_part, row_ids, col_ids, prefix)
            new_top = jnp.maximum(current[0], jnp.max(scores, axis=-1))
            total = current[1] * jnp.exp(current[0] - new_top) + jnp.sum(
                jnp.exp(scores - new_top[:, :, None]), axis=-1
            )
            return (new_top, total)

        needed = (index * block_rows <= last_row) | (index * block_rows < prefix)
        return (lax.cond(needed, lse_update, lambda current: current, state), None)

    k_blocks = k_all.reshape(block_count, block_rows, heads, HD)
    v_blocks = v_all.reshape(block_count, block_rows, heads, HD)
    lse_start = (
        jnp.full((heads, local_rows), -1e30, jnp.float32),
        jnp.zeros((heads, local_rows), jnp.float32),
    )
    (top_all, total_all), _ = lax.scan(lse_step, lse_start, (k_blocks, block_ids))
    lse = top_all + jnp.log(total_all)

    def out_step(acc, item):
        k_part, v_part, index = item
        col_ids = index * block_rows + jnp.arange(block_rows, dtype=jnp.int32)

        def out_update(current):
            scores, allowed = pair_scores(q_heads, k_part, row_ids, col_ids, prefix)
            attn_prob = jnp.where(allowed[None], jnp.exp(scores - lse[:, :, None]), 0.0).astype(
                jnp.bfloat16
            )
            return current + jnp.einsum(
                "hqk,khd->qhd", attn_prob, v_part, preferred_element_type=jnp.float32
            )

        needed = (index * block_rows <= last_row) | (index * block_rows < prefix)
        return (lax.cond(needed, out_update, lambda current: current, acc), None)

    ctx_acc, _ = lax.scan(
        out_step, jnp.zeros((local_rows, heads, HD), jnp.float32), (k_blocks, v_blocks, block_ids)
    )
    ctx_low = ctx_acc.reshape(local_rows, width).astype(jnp.bfloat16)
    middle = (
        hidden
        + jnp.dot(ctx_low, wo_full, preferred_element_type=jnp.float32)
        + bo_full.astype(jnp.float32)
    )
    normed_two, factor_two = normalize(middle)
    norm_two = (normed_two * gb_full.astype(jnp.float32) + sb_full.astype(jnp.float32)).astype(
        jnp.bfloat16
    )
    pre_act = jnp.dot(norm_two, wu_full, preferred_element_type=jnp.float32) + bu_full.astype(
        jnp.float32
    )
    cdf_part = 0.5 * (1.0 + jax.scipy.special.erf(pre_act * 0.7071067811865476))
    act_low = (pre_act * cdf_part).astype(jnp.bfloat16)
    layer_out = (
        middle
        + jnp.dot(act_low, wd_full, preferred_element_type=jnp.float32)
        + bd_full.astype(jnp.float32)
    ).astype(jnp.bfloat16)
    regathered = (
        lax.all_gather(shards[0], ("seq", "batch"), axis=0, tiled=True),
        lax.all_gather(shards[1], ("seq", "batch"), axis=0, tiled=True),
        lax.all_gather(shards[2], ("seq", "batch"), axis=0, tiled=True),
        lax.all_gather(shards[3], ("seq", "batch"), axis=0, tiled=True),
        lax.all_gather(shards[4], ("seq", "batch"), axis=0, tiled=True),
        lax.all_gather(shards[5], ("seq", "batch"), axis=0, tiled=True),
        lax.all_gather(shards[6], ("seq", "batch"), axis=0, tiled=True),
        lax.all_gather(shards[7], ("seq", "batch"), axis=0, tiled=True),
        lax.all_gather(shards[8], ("seq", "batch"), axis=0, tiled=True),
        lax.all_gather(shards[9], ("seq", "batch"), axis=0, tiled=True),
        lax.all_gather(shards[10], ("seq", "batch"), axis=0, tiled=True),
        lax.all_gather(shards[11], ("seq", "batch"), axis=0, tiled=True),
        lax.all_gather(shards[12], ("seq", "batch"), axis=0, tiled=True),
        lax.all_gather(shards[13], ("seq", "batch"), axis=0, tiled=True),
        lax.all_gather(shards[14], ("seq", "batch"), axis=0, tiled=True),
    )
    (
        ga_back,
        sa_back,
        wq_back,
        bq_back,
        wk_back,
        wv_back,
        bv_back,
        wo_back,
        bo_back,
        gb_back,
        sb_back,
        wu_back,
        bu_back,
        wd_back,
        bd_back,
    ) = regathered
    d_out = cotangent[0]
    grad_wd = over_rows(act_low, d_out)
    grad_bd = jnp.sum(d_out.astype(jnp.float32), axis=0)
    d_act = over_cols(d_out, wd_back)
    slope = cdf_part + pre_act * jnp.exp(-0.5 * pre_act * pre_act) * 0.3989422804014327
    d_pre = (d_act * slope).astype(jnp.bfloat16)
    grad_wu = over_rows(norm_two, d_pre)
    grad_bu = jnp.sum(d_pre.astype(jnp.float32), axis=0)
    d_norm_two = over_cols(d_pre, wu_back)
    d_mid_norm, grad_gb, grad_sb = norm_backward(d_norm_two, normed_two, factor_two, gb_back)
    grad_gb, grad_sb = (grad_gb[0], grad_sb[0])
    d_middle = d_out.astype(jnp.float32) + d_mid_norm
    d_branch = d_middle.astype(jnp.bfloat16)
    grad_wo = over_rows(ctx_low, d_branch)
    grad_bo = jnp.sum(d_branch.astype(jnp.float32), axis=0)
    d_ctx = over_cols(d_branch, wo_back).astype(jnp.bfloat16)
    do_heads = d_ctx.reshape(local_rows, heads, HD)
    delta = jnp.sum(d_ctx.astype(jnp.float32).reshape(local_rows, heads, HD) * ctx_acc, axis=-1).T
    k_back, v_back = (k_blocks, v_blocks)
    zero_heads = jnp.zeros((local_rows, heads, HD), jnp.float32)

    def grad_step(acc, item):
        k_part, v_part, index = item
        col_ids = index * block_rows + jnp.arange(block_rows, dtype=jnp.int32)

        def work(current):
            prob_low, d_score = grad_terms(
                q_heads, do_heads, lse, delta, k_part, v_part, row_ids, col_ids, prefix
            )
            current = current + 0.125 * jnp.einsum(
                "hqk,khd->qhd", d_score, k_part, preferred_element_type=jnp.float32
            )
            d_key = 0.125 * jnp.einsum(
                "hqk,qhd->khd", d_score, q_heads, preferred_element_type=jnp.float32
            )
            d_value = jnp.einsum(
                "hqk,qhd->khd", prob_low, do_heads, preferred_element_type=jnp.float32
            )
            return (current, (d_key, d_value))

        def skip(current):
            empty = jnp.zeros((block_rows, heads, HD), jnp.float32)
            return (current, (empty, empty))

        needed = (index * block_rows <= last_row) | (index * block_rows < prefix)
        return lax.cond(needed, work, skip, acc)

    dq_acc, (dk_blocks, dv_blocks) = lax.scan(grad_step, zero_heads, (k_back, v_back, block_ids))
    dk_local, dv_local = (
        lax.psum_scatter(
            dk_blocks.reshape(length, width).astype(jnp.bfloat16),
            "seq",
            scatter_dimension=0,
            tiled=True,
        ).astype(jnp.float32),
        lax.psum_scatter(
            dv_blocks.reshape(length, width).astype(jnp.bfloat16),
            "seq",
            scatter_dimension=0,
            tiled=True,
        ).astype(jnp.float32),
    )
    dq_low = dq_acc.reshape(local_rows, width).astype(jnp.bfloat16)
    dk_low = dk_local.astype(jnp.bfloat16)
    dv_low = dv_local.astype(jnp.bfloat16)
    grad_wq = over_rows(norm_one, dq_low)
    grad_bq = jnp.sum(dq_low.astype(jnp.float32), axis=0)
    grad_wk = over_rows(norm_one, dk_low)
    grad_wv = over_rows(norm_one, dv_low)
    grad_bv = jnp.sum(dv_low.astype(jnp.float32), axis=0)
    d_norm_one = (
        over_cols(dq_low, wq_back) + over_cols(dk_low, wk_back) + over_cols(dv_low, wv_back)
    )
    d_in_norm, grad_ga, grad_sa = norm_backward(d_norm_one, normed_one, factor_one, ga_back)
    grad_ga, grad_sa = (grad_ga[0], grad_sa[0])
    grad_tokens = d_middle + d_in_norm
    summed = (
        lax.psum_scatter(grad_ga, ("seq", "batch"), scatter_dimension=0, tiled=True),
        lax.psum_scatter(grad_sa, ("seq", "batch"), scatter_dimension=0, tiled=True),
        lax.psum_scatter(grad_wq, ("seq", "batch"), scatter_dimension=0, tiled=True),
        lax.psum_scatter(grad_bq, ("seq", "batch"), scatter_dimension=0, tiled=True),
        lax.psum_scatter(grad_wk, ("seq", "batch"), scatter_dimension=0, tiled=True),
        lax.psum_scatter(grad_wv, ("seq", "batch"), scatter_dimension=0, tiled=True),
        lax.psum_scatter(grad_bv, ("seq", "batch"), scatter_dimension=0, tiled=True),
        lax.psum_scatter(grad_wo, ("seq", "batch"), scatter_dimension=0, tiled=True),
        lax.psum_scatter(grad_bo, ("seq", "batch"), scatter_dimension=0, tiled=True),
        lax.psum_scatter(grad_gb, ("seq", "batch"), scatter_dimension=0, tiled=True),
        lax.psum_scatter(grad_sb, ("seq", "batch"), scatter_dimension=0, tiled=True),
        lax.psum_scatter(grad_wu, ("seq", "batch"), scatter_dimension=0, tiled=True),
        lax.psum_scatter(grad_bu, ("seq", "batch"), scatter_dimension=0, tiled=True),
        lax.psum_scatter(grad_wd, ("seq", "batch"), scatter_dimension=0, tiled=True),
        lax.psum_scatter(grad_bd, ("seq", "batch"), scatter_dimension=0, tiled=True),
    )
    return (
        layer_out[None],
        grad_tokens[None],
        summed[0],
        summed[1],
        summed[2],
        summed[3],
        summed[4],
        summed[5],
        summed[6],
        summed[7],
        summed[8],
        summed[9],
        summed[10],
        summed[11],
        summed[12],
        summed[13],
        summed[14],
    )


def solution(mesh):
    seq, batch = (mesh.shape["seq"], mesh.shape["batch"])
    if batch == 2 and seq == 16:
        fine = Mesh(mesh.devices.reshape(seq // 4, 2, 2, batch), ALL)
        along, run = (SEQ, body)
    else:
        fine, along, run = (mesh, "seq", plain_body)
    every = along + ("batch",) if run is body else ("seq", "batch")
    act, mat, vec = (P("batch", along, None), P(every, None), P(every))
    return jax.shard_map(
        run,
        mesh=fine,
        in_specs=(
            act, act, P("batch"), vec, vec, mat, vec, mat, mat, vec, mat, vec, vec, vec, mat, vec, mat,
            vec,
        ),
        out_specs=(
            act, act, vec, vec, mat, vec, mat, mat, vec, mat, vec, vec, vec, mat, vec, mat, vec,
        ),
        check_vma=False,
    )
```

```python
import functools

import jax
import jax.numpy as jnp
from jax import lax
from jax.experimental import pallas as pl
from jax.experimental.pallas import tpu as pltpu
from jax.sharding import Mesh
from jax.sharding import PartitionSpec as P

HD = 64
EPS = 1e-05
LOG2E = 1.4426950408889634
SEQ = ("z", "y", "x")
ALL = SEQ + ("batch",)
WIDE = 4 * HD
LIMIT = 58
F32 = jnp.float32
BF16 = jnp.bfloat16
NN = ((1,), (0,))
NT = ((1,), (1,))
TN = ((0,), (0,))


def normalize(values):
    centre = jnp.mean(values, axis=-1, keepdims=True)
    centred = values - centre
    spread = jnp.mean(centred * centred, axis=-1, keepdims=True)
    factor = lax.rsqrt(spread + EPS)
    return (centred * factor, factor)


def norm_backward(grad_out, normed, factor, gain):
    grad_gain = jnp.sum(grad_out * normed, axis=0, keepdims=True)
    grad_shift = jnp.sum(grad_out, axis=0, keepdims=True)
    scaled = grad_out * gain.astype(F32)
    grad_in = factor * (
        scaled
        - jnp.mean(scaled, axis=-1, keepdims=True)
        - normed * jnp.mean(scaled * normed, axis=-1, keepdims=True)
    )
    return (grad_in, grad_gain, grad_shift)


def dot(left, right, dims=NN):
    return lax.dot_general(left, right, (dims, ((), ())), preferred_element_type=F32)


def swap(value, axis, step=1):
    size = lax.axis_size(axis)
    return lax.ppermute(value, axis, [(i, i ^ step) for i in range(size)])


def swap_plane(value, step):
    return lax.ppermute(value, ("y", "x"), [(i, i ^ step) for i in range(4)])


def after(value, *others):
    return lax.optimization_barrier((value,) + others)[0]


def split(length):
    return 512 if length % 512 == 0 else length


SMALL = pl.CostEstimate(flops=1, bytes_accessed=1, transcendentals=0)
SMEM_SPEC = pl.BlockSpec(memory_space=pltpu.SMEM)
HBM_SPEC = pl.BlockSpec(memory_space=pltpu.HBM)


def full_block(shape):
    zeros = (0,) * len(shape)
    return pl.BlockSpec(shape, lambda i: zeros, pipeline_mode=pl.Buffered(1))


def like(shape, dtype):
    return jax.ShapeDtypeStruct(shape, dtype)


def once(name, kernel, args, outs, scratch=(), limit=LIMIT, left=()):
    in_specs = [SMEM_SPEC if a.dtype == jnp.int32 else full_block(a.shape) for a in args]
    out_specs = [HBM_SPEC if i in left else full_block(o.shape) for i, o in enumerate(outs)]
    return pl.pallas_call(
        kernel,
        grid=(1,),
        out_shape=tuple(outs),
        in_specs=in_specs,
        out_specs=tuple(out_specs),
        scratch_shapes=list(scratch),
        compiler_params=pltpu.CompilerParams(vmem_limit_bytes=limit << 20),
        cost_estimate=SMALL,
        name=name,
    )(*args)


PLACE, PREFIX, CORE, FLAT, LINE = range(5)


def rank_of(scal, k, d, other):
    line = jnp.bitwise_xor(scal[LINE], k)
    flat = jnp.bitwise_xor(scal[FLAT], d)
    return (line * 4 + flat) * 2 + jnp.bitwise_xor(scal[CORE], other)


def rows_at(index, size):
    return pl.ds(pl.multiple_of(index * size, size), size)


def square_pieces(wq, other):
    outer = other.shape[0] // 4
    for d in range(4):
        for k in range(outer):
            yield (k, d, 0, wq[d].at[k])
            yield (k, d, 1, other.at[d * outer + k])


def pack_kernel(lines, heads, scal, token, w_out, w_up, w_q, w_k, w_v, *refs):
    vectors, (up_own, out_b, out_c, out_d, send) = (refs[:8], refs[8:])
    wide = w_up.shape[1] // (4 * lines)
    rows, cut = (token.shape[0], w_up.shape[0])
    for out in (out_b, out_c, out_d):
        out[:rows, :] = token[...]
        out[rows : rows + cut, :] = w_out[...]
    for z in range(lines):
        pieces = [w_up[:, (z * 4 + t) * wide : (z * 4 + t + 1) * wide] for t in range(4)]
        for k, (out, first) in enumerate(
            ((up_own, 0), (out_b, rows + cut), (out_c, rows + cut), (out_d, rows + cut))
        ):
            target = jnp.bitwise_xor(scal[FLAT], k)
            value = pieces[0]
            for t in range(1, 4):
                value = jnp.where(target == t, pieces[t], value)
            out[first : first + cut, z * wide : (z + 1) * wide] = value
    lane = jnp.concatenate([ref[...].astype(F32) for ref in vectors], axis=0)
    lane = jnp.concatenate([lane, jnp.zeros((8, 2 * HD - cut), F32)], axis=1)
    vec = jnp.concatenate([jnp.transpose(lane)[:cut], jnp.zeros((cut, HD - 8), F32)], axis=1)
    vec = vec.astype(BF16)
    for h in range(send.shape[0]):
        for i, w in enumerate((w_q, w_k, w_v)):
            if h < heads:
                piece = w[:, h * HD : (h + 1) * HD]
            else:
                piece = jnp.zeros((cut, HD), BF16)
            send[h, :, i * HD : (i + 1) * HD] = piece
        send[h, :, 3 * HD :] = vec


def forward_kernel(
    heads, scal, ahead, own_b, own_c, own_d, zc, xc, yc, xya, xyb, w,
    n1_out, n0_out, qkvt, ctxc, ctxt, lse, rows_out, wt_out, wo_out,
    n1, n0, k_s, w_s, sems,
):
    place, prefix = (scal[PLACE], scal[PREFIX])
    outer = zc.shape[0] + 1
    length, width = n1.shape
    rows = length // (4 * outer)
    cut = w.shape[2]
    blk = split(length)
    copies = []
    near = ((ahead, 0), (own_b, 1), (own_c, 2), (own_d, 3))
    along = ((zc, 1, 0), (xc, 1, 1), (yc, 1, 2), (xya, 1, 3), (xyb, outer // 2 + 1, 3))
    for src, d in near:
        pair = (src.at[rows : rows + cut, :], wo_out.at[d * outer])
        copies.append(pltpu.make_async_copy(*pair, sems.at[2 + len(copies)]))
    for src, k, d in along:
        target = wo_out.at[d * outer + k : d * outer + k + src.shape[0]]
        copies.append(pltpu.make_async_copy(src.at[:, rows:, :], target, sems.at[2 + len(copies)]))
    for copy in copies:
        copy.start()
    head = jnp.minimum(place, heads - 1)
    for b in range(2):
        for i in range(w.shape[1]):
            at = (2 * i + b) * cut
            w_s[at : at + cut, :] = w[b, i].astype(F32)
    turned = jnp.transpose(w_s[...])
    wt_out[...] = turned[: 3 * HD].astype(BF16)
    rows_in = turned[3 * HD : 3 * HD + 8]
    rows_out[...] = rows_in
    gain = rows_in[0:1]
    shift = rows_in[1:2]

    def norm_rows(value, k, d):
        normed, _ = normalize(value.astype(F32))
        here = rows_at(jnp.bitwise_xor(place, k * 4 + d), rows)
        n0[here, :] = normed.astype(BF16)
        n1[here, :] = (normed * gain + shift).astype(BF16)

    for src, d in near:
        norm_rows(src[:rows, :], 0, d)
    for src, first, d in along:

        def one(k, carry, src=src, first=first, d=d):
            norm_rows(src[k, :rows, :], first + k, d)
            return carry

        lax.fori_loop(0, src.shape[0], one, 0)
    for i, (src, dst) in enumerate(((n1, n1_out), (n0, n0_out))):
        copy = pltpu.make_async_copy(src, dst, sems.at[i])
        copy.start()
        copies.append(copy)
    bias_q = w_s[rows_at(head, HD), 3 * HD + 2 : 3 * HD + 3]
    bias_v = w_s[rows_at(head, HD), 3 * HD + 3 : 3 * HD + 4]
    for i in range(length // blk):
        sl = slice(i * blk, (i + 1) * blk)
        part = dot(wt_out[...], n1[sl, :], NT)
        k_part = part[HD : 2 * HD].astype(BF16)
        qkvt[:HD, sl] = (part[:HD] + bias_q).astype(BF16)
        qkvt[HD : 2 * HD, sl] = k_part
        qkvt[2 * HD :, sl] = (part[2 * HD :] + bias_v).astype(BF16)
        k_s[sl, :] = jnp.transpose(k_part.astype(F32)).astype(BF16)
    scale = 0.125 * LOG2E

    def one_query(i, carry):
        first = pl.multiple_of(i * blk, blk)
        q_now = qkvt[:HD, pl.ds(first, blk)]

        def step(masked, j, state):
            top, total, acc = state
            start = pl.multiple_of(j * blk, blk)
            scores = dot(k_s[pl.ds(start, blk), :], q_now) * scale
            if masked:
                key = start + lax.broadcasted_iota(jnp.int32, (blk, blk), 0)
                query = first + lax.broadcasted_iota(jnp.int32, (blk, blk), 1)
                scores = jnp.where((key <= query) | (key < prefix), scores, -1e30)
            new_top = jnp.maximum(top, jnp.max(scores, axis=0, keepdims=True))
            prob = jnp.exp2(scores - new_top)
            fade = jnp.exp2(top - new_top)
            total = total * fade + jnp.sum(prob, axis=0, keepdims=True)
            acc = acc * fade + dot(qkvt[2 * HD :, pl.ds(start, blk)], prob.astype(BF16))
            return (new_top, total, acc)

        state = (
            jnp.full((1, blk), -1e30, F32),
            jnp.zeros((1, blk), F32),
            jnp.zeros((HD, blk), F32),
        )
        full = jnp.maximum(prefix // blk, i)
        needed = jnp.maximum((prefix + blk - 1) // blk, i + 1)
        state = lax.fori_loop(0, full, functools.partial(step, False), state)
        top, total, acc = lax.fori_loop(full, needed, functools.partial(step, True), state)
        out = acc / total
        ctxt[:, pl.ds(first, blk)] = out
        lse[:, pl.ds(first, blk)] = top + jnp.log2(total)
        for r in range(blk // rows):
            ctxc[i * (blk // rows) + r] = out[:, r * rows : (r + 1) * rows].astype(BF16)
        return carry

    lax.fori_loop(0, length // blk, one_query, 0)
    for copy in copies:
        copy.wait()


def backward_kernel(
    scal, qkvt, dcr, ctxt, lse, dchunk, dall, q_s, k_s, v_s, dc_s, dct_s, del_s, dq_s, dk_s, dv_s
):
    prefix = scal[PREFIX]
    rows = dcr.shape[2]
    length = qkvt.shape[1]
    blk = split(length)
    count = length // blk
    for i in range(count):
        sl = slice(i * blk, (i + 1) * blk)
        turned = jnp.transpose(qkvt[:, sl].astype(F32)).astype(BF16)
        q_s[sl, :] = turned[:, :HD]
        k_s[sl, :] = turned[:, HD : 2 * HD]
        v_s[sl, :] = turned[:, 2 * HD :]
    for i in range(length // rows):
        sl = slice(i * rows, (i + 1) * rows)
        dct_s[:, sl] = dcr[i]
        dc_s[sl, :] = jnp.transpose(dcr[i].astype(F32)).astype(BF16)
    del_s[...] = jnp.sum(dct_s[...].astype(F32) * ctxt[...], axis=0, keepdims=True)
    dq_s[...] = jnp.zeros_like(dq_s)
    scale = 0.125 * LOG2E

    def one_key(j, carry):
        start = pl.multiple_of(j * blk, blk)
        dk_s[...] = jnp.zeros_like(dk_s)
        dv_s[...] = jnp.zeros_like(dv_s)

        def step(masked, i, inner):
            first = pl.multiple_of(i * blk, blk)
            here = pl.ds(first, blk)
            scores = dot(k_s[pl.ds(start, blk), :], qkvt[:HD, here]) * scale
            prob = jnp.exp2(scores - lse[:, here])
            if masked:
                key = start + lax.broadcasted_iota(jnp.int32, (blk, blk), 0)
                query = first + lax.broadcasted_iota(jnp.int32, (blk, blk), 1)
                prob = jnp.where((key <= query) | (key < prefix), prob, 0.0)
            d_prob = dot(v_s[pl.ds(start, blk), :], dct_s[:, here])
            d_score = (prob * (d_prob - del_s[:, here])).astype(BF16)
            dv_s[...] += dot(prob.astype(BF16), dc_s[here, :])
            dk_s[...] += dot(d_score, q_s[here, :])
            dq_s[:, here] += dot(qkvt[HD : 2 * HD, pl.ds(start, blk)], d_score)
            return inner

        begin = jnp.where(start < prefix, 0, j)
        middle = jnp.where(start + blk <= prefix, begin, j + 1)
        lax.fori_loop(begin, middle, functools.partial(step, True), 0)
        lax.fori_loop(middle, count, functools.partial(step, False), 0)
        d_key = jnp.transpose(dk_s[...] * 0.125).astype(BF16)
        d_value = jnp.transpose(dv_s[...]).astype(BF16)
        dall[HD : 2 * HD, pl.ds(start, blk)] = d_key
        dall[2 * HD :, pl.ds(start, blk)] = d_value
        for r in range(blk // rows):
            at = j * (blk // rows) + r
            dchunk[at, HD : 2 * HD, :] = d_key[:, r * rows : (r + 1) * rows]
            dchunk[at, 2 * HD :, :] = d_value[:, r * rows : (r + 1) * rows]
        return carry

    lax.fori_loop(0, count, one_key, 0)
    for i in range(count):
        sl = slice(i * blk, (i + 1) * blk)
        d_query = (dq_s[:, sl] * 0.125).astype(BF16)
        dall[:HD, sl] = d_query
        for r in range(blk // rows):
            dchunk[i * (blk // rows) + r, :HD, :] = d_query[:, r * rows : (r + 1) * rows]


def stacked(pieces, first, last):
    return jnp.concatenate([piece[first:last, :].astype(F32) for piece in pieces]).astype(BF16)


def out_pieces(own, other):
    outer = own.shape[0] // 4
    return [
        (i % outer, i // outer, core, ref.at[i])
        for core, ref in ((0, own), (1, other))
        for i in range(own.shape[0])
    ]


def middle_kernel(heads, scal, ctx, own, other, token, rows_in, middle, norm_two, plain, moved):
    pieces = out_pieces(own, other)
    cut = own.shape[1]
    plain[...] = ctx[:heads].reshape(plain.shape).astype(F32)
    for n, (k, d, core, _) in enumerate(pieces):
        moved[n * cut : (n + 1) * cut, :] = plain[rows_at(rank_of(scal, k, d, core), cut), :]
    turned = jnp.transpose(moved[...]).astype(BF16)
    product = dot(turned, stacked([p[3] for p in pieces], 0, cut))
    value = token[...].astype(F32) + product + rows_in[4:5, :]
    middle[...] = value
    normed, _ = normalize(value)
    norm_two[...] = (normed * rows_in[5:6, :] + rows_in[6:7, :]).astype(BF16)


def feed_kernel(
    scal, n2_a, n2_b, n2_c, n2_d, dy_a, dy_b, dy_c, dy_d, ffz, ffc,
    out_keep, out_b, out_c, out_d, dn_keep, dn_b, dn_c, dn_d, send, keep,
    n2, dy, down, up, act, d_pre, down_s, up_s, bias,
):
    outer = ffz.shape[0]
    cut = (ffz.shape[1] - 8) // 8
    half = 4 * cut
    order = (0, 2, 1, 3)
    sources = [
        (src.at[i], k, core) for core, src in ((0, ffz), (1, ffc)) for i, k in enumerate(order)
    ]

    def block_of(k, core):
        line = jnp.bitwise_xor(scal[LINE], k)
        return line * 2 + jnp.bitwise_xor(scal[CORE], core)

    rows = []
    for src, k, core in sources:
        down[rows_at(block_of(k, core), half), :] = src[:half, :]
        for d in range(4):
            here = rows_at(rank_of(scal, k, d, core), cut)
            up_s[here, :] = src[half + d * cut : half + (d + 1) * cut, :].astype(F32)
        rows.append((block_of(k, core), src[2 * half :, :half].astype(F32)[:1]))
    up[...] = up_s[...].astype(BF16)
    for q in range(2 * outer):
        bias[:, q * half : (q + 1) * half] = sum(jnp.where(at == q, row, 0.0) for at, row in rows)
    count = n2_a.shape[0]
    for i, piece in enumerate((n2_a, n2_b, n2_c, n2_d)):
        n2[i * count : (i + 1) * count, :] = piece[...]
    for i, piece in enumerate((dy_a, dy_b, dy_c, dy_d)):
        dy[i * count : (i + 1) * count, :] = piece[piece.shape[0] - count :, :]
    tile = 256
    for c in range(down.shape[0] // tile):
        sl = slice(c * tile, (c + 1) * tile)
        pre = dot(n2[...], up[:, sl]) + bias[:, sl]
        cdf = 0.5 * (1.0 + lax.erf(pre * 0.7071067811865476))
        act[:, sl] = (pre * cdf).astype(BF16)
        slope = cdf + pre * jnp.exp(-0.5 * pre * pre) * 0.3989422804014327
        d_pre[:, sl] = (dot(dy[...], down[sl, :], NT) * slope).astype(BF16)
    back = dot(d_pre[...], up[...], NT)
    for i, ref in enumerate((dn_keep, dn_b, dn_c, dn_d)):
        ref[...] = back[i * count : (i + 1) * count].astype(ref.dtype)
    out = dot(act[...], down[...])
    for i, ref in enumerate((out_keep, out_b, out_c, out_d)):
        ref[...] = out[i * count : (i + 1) * count].astype(ref.dtype)
    down_s[...] = dot(act[...], dy[...], TN)
    up_s[...] = dot(n2[...], d_pre[...], TN)
    total = jnp.sum(d_pre[...].astype(F32), axis=0, keepdims=True)
    width = keep.shape[2]
    for k in range(outer):
        for core, ref in ((0, keep), (1, send)):
            at = block_of(k, core)
            ref[k, :half, :] = down_s[rows_at(at, half), :].astype(ref.dtype)
            for t in range(4):
                line = jnp.bitwise_xor(scal[LINE], k)
                rank = (line * 4 + t) * 2 + jnp.bitwise_xor(scal[CORE], core)
                here = slice(half + t * cut, half + (t + 1) * cut)
                ref[k, here, :] = up_s[rows_at(rank, cut), :].astype(ref.dtype)
            part = sum(
                jnp.where(at == q, total[:, q * half : (q + 1) * half], 0.0)
                for q in range(2 * outer)
            )
            part = jnp.concatenate([part, jnp.zeros((1, width - half), F32)], axis=1)
            ref[k, 2 * half :, :] = jnp.broadcast_to(part, (8, width)).astype(ref.dtype)


def turn_kernel(
    heads, scal, keep, got_b, got_c, got_d, middle, d_out, own, other, rows_in, ctx,
    d_middle, d_branch_out, d_ctx, sums, wo_keep, wo_send, plain, full,
):
    d_norm = keep[...] + (got_b[...].astype(F32) + got_c[...].astype(F32)) + got_d[...].astype(F32)
    normed, factor = normalize(middle[...])
    grad_in, grad_gain, grad_shift = norm_backward(d_norm, normed, factor, rows_in[5:6, :])
    grad_up = d_out[...].astype(F32)
    total = grad_up + grad_in
    low = total.astype(BF16)
    d_middle[...] = total
    d_branch_out[...] = low[:8]
    pieces = out_pieces(own, other)
    cut = own.shape[1]
    back = dot(stacked([p[3] for p in pieces], 0, cut), low, NT)
    for n, (k, d, core, _) in enumerate(pieces):
        plain[rows_at(rank_of(scal, k, d, core), cut), :] = back[n * cut : (n + 1) * cut]
    seq, rows = (d_ctx.shape[0], d_ctx.shape[2])
    d_ctx[:heads] = plain[...].astype(BF16).reshape(heads, HD, rows)
    d_ctx[heads:] = jnp.zeros((seq - heads, HD, rows), BF16)
    sums[0:1, :] = jnp.sum(low.astype(F32), axis=0, keepdims=True)
    sums[1:2, :] = grad_gain
    sums[2:3, :] = grad_shift
    sums[3:4, :] = jnp.sum(grad_up, axis=0, keepdims=True)
    sums[4:, :] = jnp.zeros((4, sums.shape[1]), F32)
    full[...] = dot(ctx[:heads].reshape(heads * HD, rows), low).reshape(full.shape)
    for i in range(seq):
        wo_keep[i] = full[2 * i + scal[CORE]]
        wo_send[i] = full[2 * i + 1 - scal[CORE]].astype(BF16)


def fold_kernel(keep, got, own, away):
    for i, (k, ref) in enumerate(((0, own), (2, own), (1, away), (3, away))):
        ref[i % 2] = (keep[k] + got[k].astype(F32)).astype(ref.dtype)


def second_kernel(keep, got, own, away):
    own[...] = keep[0] + got[0].astype(F32)
    away[...] = (keep[1] + got[1].astype(F32)).astype(BF16)


def finish_kernel(scal, keep, *refs):
    got, (wo_keep, wo_got, out_b, out_c, out_d), outs = (refs[:-13], refs[-13:-8], refs[-8:])
    grad_down, bias, own, wo_own, away_b, away_c, away_d, total = outs
    value = keep[...]
    for ref in got:
        value = value + ref[...].astype(F32)
    total[...] = value
    half = grad_down.shape[0]
    cut = half // 4
    lines = wo_own.shape[0]
    grad_down[...] = value[:half]
    bias[...] = value[2 * half : 2 * half + 1, :half]
    for k, ref in enumerate((own, away_b, away_c, away_d)):
        at = jnp.bitwise_xor(scal[FLAT], k)
        here = pl.ds(pl.multiple_of(half + at * cut, 8), cut)
        ref[:cut, :] = total[here, :].astype(BF16)
        for z in range(lines):
            part = wo_keep[4 * z + at] + wo_got[4 * z + at].astype(F32)
            if k:
                ref[(1 + z) * cut : (2 + z) * cut, :] = part.astype(BF16)
            else:
                wo_own[z] = part
    for src, ref in ((out_b, away_b), (out_c, away_c), (out_d, away_d)):
        ref[(1 + lines) * cut :, :] = src[...]


def close_kernel(
    lines, scal, own, wo_own, got_b, got_c, got_d, middle, out_keep, rows_in,
    layer_out, grad_up, grad_out, *away,
):
    cut = grad_out.shape[0]
    got = (got_b, got_c, got_d)
    value = middle[...] + out_keep[...] + rows_in[7:8, :]
    pieces = [own[...].astype(F32)]
    for ref in got:
        value = value + ref[(1 + lines) * cut :, :].astype(F32)
        pieces.append(ref[:cut, :].astype(F32))
    layer_out[...] = value.astype(BF16)
    for k, out in enumerate((grad_out,) + away):
        at = jnp.bitwise_xor(scal[LINE], k)
        here = pl.ds(pl.multiple_of((1 + at) * cut, 8), cut)
        part = wo_own[at]
        for ref in got:
            part = part + ref[here, :].astype(F32)
        out[...] = part.astype(out.dtype)
    wide = own.shape[1] // lines
    for t in range(4):
        step = jnp.bitwise_xor(scal[FLAT], t)
        piece = pieces[0]
        for k in range(1, 4):
            piece = jnp.where(step == k, pieces[k], piece)
        for z in range(lines):
            at = (z * 4 + t) * wide
            grad_up[:, at : at + wide] = piece[:, z * wide : (z + 1) * wide]


def heads_kernel(heads, scal, dall, n1, n0, wt, sums, keep, send, gh, gm, cs, full):
    step = pl.program_id(0)

    @pl.when(step == 0)
    def _():
        gh[...] = jnp.zeros_like(gh)
        gm[...] = jnp.zeros_like(gm)
        cs[...] = jnp.zeros_like(cs)

    gh[...] += dot(dall[...], n1[...])
    gm[...] += dot(dall[...], n0[...])
    cs[...] += dot(dall[...], jnp.ones((dall.shape[1], 2 * HD), BF16))

    @pl.when(step == pl.num_programs(0) - 1)
    def _():
        place = scal[PLACE]
        width = gh.shape[1]
        live = place < heads
        wide = wt[...].astype(F32)
        gain = jnp.where(live, jnp.sum(wide * gm[...], axis=0, keepdims=True), 0.0)
        shift = jnp.where(live, jnp.sum(wide * cs[:, :1], axis=0, keepdims=True), 0.0)
        line = jnp.transpose(cs[...])[0:1]
        mine = lax.broadcasted_iota(jnp.int32, (1, width), 1) // HD == place
        b_q = jnp.where(mine, jnp.concatenate([line[:, :HD]] * heads, axis=1), 0.0)
        b_v = jnp.where(mine, jnp.concatenate([line[:, 2 * HD :]] * heads, axis=1), 0.0)
        vec = jnp.concatenate([gain, shift, b_q, b_v, sums[:4, :]], axis=0)
        pad = jnp.zeros((width, HD - 8), F32)
        block = jnp.concatenate([jnp.transpose(gh[...]), jnp.transpose(vec), pad], axis=1)
        full[...] = block.reshape(full.shape)
        for i in range(keep.shape[0]):
            keep[i] = full[2 * i + scal[CORE]]
            send[i] = full[2 * i + 1 - scal[CORE]].astype(BF16)


def head_grads(scal, dall, n1, n0, wt, sums, heads, seq):
    length, width = n1.shape
    blk = 2 * split(length)
    cut = width // (2 * seq)
    outs = (like((seq, cut, WIDE), F32), like((seq, cut, WIDE), BF16))
    return pl.pallas_call(
        functools.partial(heads_kernel, heads),
        out_shape=outs,
        grid=(length // blk,),
        in_specs=[
            SMEM_SPEC,
            pl.BlockSpec((3 * HD, blk), lambda i: (0, i)),
            pl.BlockSpec((blk, width), lambda i: (i, 0)),
            pl.BlockSpec((blk, width), lambda i: (i, 0)),
            full_block(wt.shape),
            full_block(sums.shape),
        ],
        out_specs=tuple(full_block(out.shape) for out in outs),
        scratch_shapes=[
            pltpu.VMEM((3 * HD, width), F32),
            pltpu.VMEM((3 * HD, width), F32),
            pltpu.VMEM((3 * HD, 2 * HD), F32),
            pltpu.VMEM((2 * seq, cut, WIDE), F32),
        ],
        compiler_params=pltpu.CompilerParams(vmem_limit_bytes=LIMIT << 20),
        cost_estimate=SMALL,
        name="heads",
    )(scal, dall, n1, n0, wt, sums)


def last_kernel(
    heads, scal, d_rows, wq_a, wq_b, wq_c, wq_d, other, token, d_middle, rows_in, grad_tokens, plain
):
    cut = other.shape[1] // 3
    pieces = list(square_pieces((wq_a, wq_b, wq_c, wq_d), other))
    total = 0.0
    for i in range(3):
        part = jnp.concatenate(
            [d_rows[h, i * HD : (i + 1) * HD, :].astype(F32) for h in range(heads)], axis=0
        )
        weights = stacked([p[3] for p in pieces], i * cut, (i + 1) * cut)
        total = total + dot(weights, part.astype(BF16))
    for n, (k, d, core, _) in enumerate(pieces):
        plain[rows_at(rank_of(scal, k, d, core), cut), :] = total[n * cut : (n + 1) * cut]
    normed, factor = normalize(token[...].astype(F32))
    grad_in, _, _ = norm_backward(jnp.transpose(plain[...]), normed, factor, rows_in[0:1, :])
    grad_tokens[...] = d_middle[...] + grad_in


def unpack_kernel(heads, got, g_q, g_k, g_v, *vec):
    for i, out in enumerate((g_q, g_k, g_v)):
        for h in range(heads):
            out[:, h * HD : (h + 1) * HD] = got[h, :, i * HD : (i + 1) * HD].astype(F32)
    total = got[0, :, 2 * HD :].astype(F32)
    for s in range(1, got.shape[0]):
        total = total + got[s, :, 2 * HD :].astype(F32)
    cut = total.shape[0]
    total = jnp.concatenate([total, jnp.zeros((2 * HD - cut, 2 * HD), F32)], axis=0)
    total = jnp.transpose(total)
    for i, out in enumerate(vec):
        out[...] = total[HD + i : HD + i + 1, :cut]


def body(
    tokens, cotangent, prefix_len, gain_one, shift_one, w_query, b_query, w_key, w_value, b_value,
    w_output, b_output, gain_two, shift_two, w_up, b_up, w_down, b_down,
):
    outer = lax.axis_size("z")
    seq = 4 * outer
    token, d_out = (tokens[0], cotangent[0])
    rows, width = token.shape
    length = seq * rows
    heads = width // HD
    cut = w_query.shape[0]
    half = w_down.shape[0]
    local = w_up.shape[1] // 4
    flat = lax.axis_index(("y", "x"))
    places = (lax.axis_index(SEQ), prefix_len[0], lax.axis_index("batch"), flat, lax.axis_index("z"))
    scal = jnp.stack(places).astype(jnp.int32)

    ahead = jnp.concatenate([token, w_output])
    zc = jnp.stack([swap(ahead, "z", k) for k in range(1, outer)])
    vectors = (
        gain_one, shift_one, b_query, b_value, b_output, gain_two, shift_two, b_down,
    )
    vectors = [value[None] for value in vectors]
    up_own, *first, send = once(
        "pack",
        functools.partial(pack_kernel, outer, heads),
        (scal, token, w_output, w_up, w_query, w_key, w_value, *vectors),
        [like((cut, local), BF16)]
        + [like((rows + 2 * cut, width), BF16)] * 3
        + [like((seq, cut, WIDE), BF16)],
    )
    first = [swap_plane(part, k + 1) for k, part in enumerate(first)]
    zc = after(zc, *first)
    xc = swap(zc, "x")
    yc = swap(zc, "y")
    head_w = lax.all_to_all(after(send, zc), SEQ, split_axis=0, concat_axis=0, tiled=True)
    wq = after(jnp.concatenate([w_query, w_key, w_value]), zc)
    wq_got = [swap(wq, "z", k) for k in range(1, outer)]
    head_w = lax.all_gather(head_w, "batch", axis=0, tiled=False)
    xc, yc, head_w, wq_got = lax.optimization_barrier((xc, yc, head_w, wq_got))
    xya = swap(xc[: outer // 2], "y")
    xyb = swap(yc[outer // 2 :], "x")

    b_up_row = jnp.pad(b_up[None], ((0, 7), (0, width - half)))
    ff = [w_down, up_own] + [part[rows + cut :] for part in first] + [b_up_row]
    ff = after(jnp.concatenate(ff), head_w, xc)
    ff = jnp.stack([ff, swap(ff, "z", 2)])
    ff_got = swap(ff, "z", 1)
    wq = after(jnp.stack([wq] + wq_got), xya, xyb)
    wq = [wq] + [swap_plane(wq, k) for k in range(1, 4)]

    norm_one, norm_raw, qkvt, ctxc, ctxt, lse, rows_in, wt, w_out_own = once(
        "forward",
        functools.partial(forward_kernel, heads),
        (scal, ahead, *first, zc, xc, yc, xya, xyb, head_w),
        [
            like((length, width), BF16),
            like((length, width), BF16),
            like((3 * HD, length), BF16),
            like((seq, HD, rows), BF16),
            like((HD, length), F32),
            like((1, length), F32),
            like((8, width), F32),
            like((3 * HD, width), BF16),
            like((seq, cut, width), BF16),
        ],
        [
            pltpu.VMEM((length, width), BF16),
            pltpu.VMEM((length, width), BF16),
            pltpu.VMEM((length, HD), BF16),
            pltpu.VMEM((width, WIDE), F32),
            pltpu.SemaphoreType.DMA((11,)),
        ],
        left=(0, 1, 8),
    )
    w_out_other = swap(w_out_own, "batch")
    ctxc, wq, ff_got = lax.optimization_barrier((ctxc, wq, ff_got))
    ffz = jnp.concatenate([ff, ff_got])
    dy = [d_out] + [swap_plane(after(d_out, ctxc), k) for k in range(1, 4)]
    ctx = lax.all_to_all(ctxc, SEQ, split_axis=0, concat_axis=0, tiled=True)
    ffc = swap(ffz, "batch")
    dy, ctx = lax.optimization_barrier((dy, ctx))
    middle, norm_two = once(
        "middle",
        functools.partial(middle_kernel, heads),
        (scal, ctx, w_out_own, w_out_other, token, rows_in),
        [like((rows, width), F32), like((rows, width), BF16)],
        [pltpu.VMEM((width, rows), F32)] * 2,
    )
    n2 = [norm_two] + [swap_plane(norm_two, k) for k in range(1, 4)]

    part = [like((rows, width), F32)] + [like((rows, width), BF16)] * 3
    fed = once(
        "feed",
        feed_kernel,
        (scal, *n2, *dy, ffz, ffc),
        part + part + [like(ffz.shape, BF16), like(ffz.shape, F32)],
        [
            pltpu.VMEM((4 * rows, width), BF16),
            pltpu.VMEM((4 * rows, width), BF16),
            pltpu.VMEM((local, width), BF16),
            pltpu.VMEM((width, local), BF16),
            pltpu.VMEM((4 * rows, local), BF16),
            pltpu.VMEM((4 * rows, local), BF16),
            pltpu.VMEM((local, width), F32),
            pltpu.VMEM((width, local), F32),
            pltpu.VMEM((1, local), F32),
        ],
    )
    out_keep, *out_send = fed[:4]
    dn_keep, *dn_send = fed[4:8]
    send, keep = fed[8:]
    dn_got = [swap_plane(value, k + 1) for k, value in enumerate(dn_send)]

    count = 2 * half + 8
    pair = like((2, count, width), F32)
    own, away = once(
        "fold",
        fold_kernel,
        (keep, after(swap(send, "batch"), *dn_got)),
        [pair, like(pair.shape, BF16)],
    )
    dn_keep, _ = lax.optimization_barrier((dn_keep, away))
    d_middle, _, d_ctx, sums, wo_keep, wo_send = once(
        "turn",
        functools.partial(turn_kernel, heads),
        (scal, dn_keep, *dn_got, middle, d_out, w_out_own, w_out_other, rows_in, ctx),
        [
            like((rows, width), F32),
            like((8, width), BF16),
            like((seq, HD, rows), BF16),
            like((8, width), F32),
            like((seq, cut, width), F32),
            like((seq, cut, width), BF16),
        ],
        [pltpu.VMEM((width, rows), F32), pltpu.VMEM((2 * seq, cut, width), F32)],
    )
    d_ctx = lax.all_to_all(d_ctx, SEQ, split_axis=0, concat_axis=0, tiled=True)

    wo_got = swap(wo_send, "batch")
    own, away = once(
        "second",
        second_kernel,
        (own, swap(away, "z", 1)),
        [like((count, width), F32), like((count, width), BF16)],
    )
    back = [swap(away, "z", 2)]

    blk = split(length)
    dchunk, dall = once(
        "backward",
        backward_kernel,
        (after(scal, away), qkvt, d_ctx, ctxt, lse),
        [like((seq, 3 * HD, rows), BF16), like((3 * HD, length), BF16)],
        [
            pltpu.VMEM((length, HD), BF16),
            pltpu.VMEM((length, HD), BF16),
            pltpu.VMEM((length, HD), BF16),
            pltpu.VMEM((length, HD), BF16),
            pltpu.VMEM((HD, length), BF16),
            pltpu.VMEM((1, length), F32),
            pltpu.VMEM((HD, length), F32),
            pltpu.VMEM((blk, HD), F32),
            pltpu.VMEM((blk, HD), F32),
        ],
    )
    back, dchunk = lax.optimization_barrier((back, dchunk))
    d_rows = lax.all_to_all(dchunk, SEQ, split_axis=0, concat_axis=0, tiled=True)

    grad_w_down, bias, own, wo_own, *away = once(
        "finish",
        finish_kernel,
        (scal, own, *back, wo_keep, wo_got, *out_send),
        [
            like((half, width), F32),
            like((1, half), F32),
            like((cut, width), BF16),
            like((outer, cut, width), F32),
        ]
        + [like(((1 + outer) * cut + rows, width), BF16)] * 3,
        [pltpu.VMEM((count, width), F32)],
    )
    got = [swap_plane(value, k + 1) for k, value in enumerate(away)]
    last, send = head_grads(scal, dall, norm_one, norm_raw, wt, sums, heads, seq)
    last = last + swap(send, "batch").astype(F32)
    last = after(last.astype(BF16), d_rows)
    other = swap(after(jnp.concatenate(wq), dall), "batch")
    grad_tokens = once(
        "last",
        functools.partial(last_kernel, heads),
        (scal, d_rows, *wq, other, token, d_middle, rows_in),
        [like((rows, width), F32)],
        [pltpu.VMEM((width, rows), F32)],
    )[0]
    last = lax.all_to_all(last, SEQ, split_axis=0, concat_axis=0, tiled=True)
    mat = like((cut, width), F32)
    grad_w_query, grad_w_key, grad_w_value, *vec = once(
        "unpack",
        functools.partial(unpack_kernel, heads),
        (last,),
        [mat, mat, mat] + [like((1, cut), F32)] * 8,
    )
    layer_out, grad_w_up, grad_w_output, *away = once(
        "close",
        functools.partial(close_kernel, outer),
        (scal, own, wo_own, *got, after(middle, grad_tokens), out_keep, rows_in),
        [like((rows, width), BF16), like((cut, 4 * local), F32), like((cut, width), F32)]
        + [like((cut, width), BF16)] * (outer - 1),
    )
    grad_w_output = grad_w_output + sum(
        swap(value, "z", k + 1).astype(F32) for k, value in enumerate(away)
    )

    return (
        layer_out[None],
        grad_tokens[None],
        vec[0][0],
        vec[1][0],
        grad_w_query,
        vec[2][0],
        grad_w_key,
        grad_w_value,
        vec[3][0],
        grad_w_output,
        vec[4][0],
        vec[5][0],
        vec[6][0],
        grad_w_up,
        bias[0],
        grad_w_down,
        vec[7][0],
    )


def over_rows(left, right):
    return lax.dot_general(
        left, right, (((0,), (0,)), ((), ())), preferred_element_type=jnp.float32
    )


def over_cols(left, right):
    return lax.dot_general(
        left, right, (((1,), (1,)), ((), ())), preferred_element_type=jnp.float32
    )


def pair_scores(q_part, k_part, row_ids, col_ids, prefix):
    scores = jnp.einsum("qhd,khd->hqk", q_part, k_part, preferred_element_type=jnp.float32) * 0.125
    allowed = (col_ids[None, :] <= row_ids[:, None]) | (col_ids[None, :] < prefix)
    return (jnp.where(allowed[None], scores, -1e30), allowed)


def grad_terms(q_part, do_part, lse_part, delta_part, k_part, v_part, row_ids, col_ids, prefix):
    scores, allowed = pair_scores(q_part, k_part, row_ids, col_ids, prefix)
    attn_prob = jnp.where(allowed[None], jnp.exp(scores - lse_part[:, :, None]), 0.0)
    prob_low = attn_prob.astype(jnp.bfloat16)
    d_prob = jnp.einsum("qhd,khd->hqk", do_part, v_part, preferred_element_type=jnp.float32)
    d_score = (attn_prob * (d_prob - delta_part[:, :, None])).astype(jnp.bfloat16)
    return (prob_low, d_score)


def plain_body(
    tokens,
    cotangent,
    prefix_len,
    gain_one,
    shift_one,
    w_query,
    b_query,
    w_key,
    w_value,
    b_value,
    w_output,
    b_output,
    gain_two,
    shift_two,
    w_up,
    b_up,
    w_down,
    b_down,
):
    shards = (
        gain_one,
        shift_one,
        w_query,
        b_query,
        w_key,
        w_value,
        b_value,
        w_output,
        b_output,
        gain_two,
        shift_two,
        w_up,
        b_up,
        w_down,
        b_down,
    )
    gathered = (
        lax.all_gather(shards[0], ("seq", "batch"), axis=0, tiled=True),
        lax.all_gather(shards[1], ("seq", "batch"), axis=0, tiled=True),
        lax.all_gather(shards[2], ("seq", "batch"), axis=0, tiled=True),
        lax.all_gather(shards[3], ("seq", "batch"), axis=0, tiled=True),
        lax.all_gather(shards[4], ("seq", "batch"), axis=0, tiled=True),
        lax.all_gather(shards[5], ("seq", "batch"), axis=0, tiled=True),
        lax.all_gather(shards[6], ("seq", "batch"), axis=0, tiled=True),
        lax.all_gather(shards[7], ("seq", "batch"), axis=0, tiled=True),
        lax.all_gather(shards[8], ("seq", "batch"), axis=0, tiled=True),
        lax.all_gather(shards[9], ("seq", "batch"), axis=0, tiled=True),
        lax.all_gather(shards[10], ("seq", "batch"), axis=0, tiled=True),
        lax.all_gather(shards[11], ("seq", "batch"), axis=0, tiled=True),
        lax.all_gather(shards[12], ("seq", "batch"), axis=0, tiled=True),
        lax.all_gather(shards[13], ("seq", "batch"), axis=0, tiled=True),
        lax.all_gather(shards[14], ("seq", "batch"), axis=0, tiled=True),
    )
    (
        ga_full,
        sa_full,
        wq_full,
        bq_full,
        wk_full,
        wv_full,
        bv_full,
        wo_full,
        bo_full,
        gb_full,
        sb_full,
        wu_full,
        bu_full,
        wd_full,
        bd_full,
    ) = gathered
    hidden = tokens[0].astype(jnp.float32)
    local_rows = hidden.shape[0]
    width = hidden.shape[1]
    heads = width // HD
    prefix = prefix_len[0]
    start_row = lax.axis_index("seq") * local_rows
    last_row = start_row + local_rows - 1
    length = local_rows * lax.axis_size("seq")
    block_rows = min(512, length)
    block_count = length // block_rows
    row_ids = start_row + jnp.arange(local_rows, dtype=jnp.int32)
    block_ids = jnp.arange(block_count, dtype=jnp.int32)
    normed_one, factor_one = normalize(hidden)
    norm_one = (normed_one * ga_full.astype(jnp.float32) + sa_full.astype(jnp.float32)).astype(
        jnp.bfloat16
    )
    q_low = (
        jnp.dot(norm_one, wq_full, preferred_element_type=jnp.float32) + bq_full.astype(jnp.float32)
    ).astype(jnp.bfloat16)
    k_low = jnp.dot(norm_one, wk_full, preferred_element_type=jnp.float32).astype(jnp.bfloat16)
    v_low = (
        jnp.dot(norm_one, wv_full, preferred_element_type=jnp.float32) + bv_full.astype(jnp.float32)
    ).astype(jnp.bfloat16)
    k_all, v_all = (
        lax.all_gather(k_low, "seq", axis=0, tiled=True),
        lax.all_gather(v_low, "seq", axis=0, tiled=True),
    )
    q_heads = q_low.reshape(local_rows, heads, HD)

    def lse_step(state, item):
        k_part, index = item
        col_ids = index * block_rows + jnp.arange(block_rows, dtype=jnp.int32)

        def lse_update(current):
            scores, allowed = pair_scores(q_heads, k_part, row_ids, col_ids, prefix)
            new_top = jnp.maximum(current[0], jnp.max(scores, axis=-1))
            total = current[1] * jnp.exp(current[0] - new_top) + jnp.sum(
                jnp.exp(scores - new_top[:, :, None]), axis=-1
            )
            return (new_top, total)

        needed = (index * block_rows <= last_row) | (index * block_rows < prefix)
        return (lax.cond(needed, lse_update, lambda current: current, state), None)

    k_blocks = k_all.reshape(block_count, block_rows, heads, HD)
    v_blocks = v_all.reshape(block_count, block_rows, heads, HD)
    lse_start = (
        jnp.full((heads, local_rows), -1e30, jnp.float32),
        jnp.zeros((heads, local_rows), jnp.float32),
    )
    (top_all, total_all), _ = lax.scan(lse_step, lse_start, (k_blocks, block_ids))
    lse = top_all + jnp.log(total_all)

    def out_step(acc, item):
        k_part, v_part, index = item
        col_ids = index * block_rows + jnp.arange(block_rows, dtype=jnp.int32)

        def out_update(current):
            scores, allowed = pair_scores(q_heads, k_part, row_ids, col_ids, prefix)
            attn_prob = jnp.where(allowed[None], jnp.exp(scores - lse[:, :, None]), 0.0).astype(
                jnp.bfloat16
            )
            return current + jnp.einsum(
                "hqk,khd->qhd", attn_prob, v_part, preferred_element_type=jnp.float32
            )

        needed = (index * block_rows <= last_row) | (index * block_rows < prefix)
        return (lax.cond(needed, out_update, lambda current: current, acc), None)

    ctx_acc, _ = lax.scan(
        out_step, jnp.zeros((local_rows, heads, HD), jnp.float32), (k_blocks, v_blocks, block_ids)
    )
    ctx_low = ctx_acc.reshape(local_rows, width).astype(jnp.bfloat16)
    middle = (
        hidden
        + jnp.dot(ctx_low, wo_full, preferred_element_type=jnp.float32)
        + bo_full.astype(jnp.float32)
    )
    normed_two, factor_two = normalize(middle)
    norm_two = (normed_two * gb_full.astype(jnp.float32) + sb_full.astype(jnp.float32)).astype(
        jnp.bfloat16
    )
    pre_act = jnp.dot(norm_two, wu_full, preferred_element_type=jnp.float32) + bu_full.astype(
        jnp.float32
    )
    cdf_part = 0.5 * (1.0 + jax.scipy.special.erf(pre_act * 0.7071067811865476))
    act_low = (pre_act * cdf_part).astype(jnp.bfloat16)
    layer_out = (
        middle
        + jnp.dot(act_low, wd_full, preferred_element_type=jnp.float32)
        + bd_full.astype(jnp.float32)
    ).astype(jnp.bfloat16)
    regathered = (
        lax.all_gather(shards[0], ("seq", "batch"), axis=0, tiled=True),
        lax.all_gather(shards[1], ("seq", "batch"), axis=0, tiled=True),
        lax.all_gather(shards[2], ("seq", "batch"), axis=0, tiled=True),
        lax.all_gather(shards[3], ("seq", "batch"), axis=0, tiled=True),
        lax.all_gather(shards[4], ("seq", "batch"), axis=0, tiled=True),
        lax.all_gather(shards[5], ("seq", "batch"), axis=0, tiled=True),
        lax.all_gather(shards[6], ("seq", "batch"), axis=0, tiled=True),
        lax.all_gather(shards[7], ("seq", "batch"), axis=0, tiled=True),
        lax.all_gather(shards[8], ("seq", "batch"), axis=0, tiled=True),
        lax.all_gather(shards[9], ("seq", "batch"), axis=0, tiled=True),
        lax.all_gather(shards[10], ("seq", "batch"), axis=0, tiled=True),
        lax.all_gather(shards[11], ("seq", "batch"), axis=0, tiled=True),
        lax.all_gather(shards[12], ("seq", "batch"), axis=0, tiled=True),
        lax.all_gather(shards[13], ("seq", "batch"), axis=0, tiled=True),
        lax.all_gather(shards[14], ("seq", "batch"), axis=0, tiled=True),
    )
    (
        ga_back,
        sa_back,
        wq_back,
        bq_back,
        wk_back,
        wv_back,
        bv_back,
        wo_back,
        bo_back,
        gb_back,
        sb_back,
        wu_back,
        bu_back,
        wd_back,
        bd_back,
    ) = regathered
    d_out = cotangent[0]
    grad_wd = over_rows(act_low, d_out)
    grad_bd = jnp.sum(d_out.astype(jnp.float32), axis=0)
    d_act = over_cols(d_out, wd_back)
    slope = cdf_part + pre_act * jnp.exp(-0.5 * pre_act * pre_act) * 0.3989422804014327
    d_pre = (d_act * slope).astype(jnp.bfloat16)
    grad_wu = over_rows(norm_two, d_pre)
    grad_bu = jnp.sum(d_pre.astype(jnp.float32), axis=0)
    d_norm_two = over_cols(d_pre, wu_back)
    d_mid_norm, grad_gb, grad_sb = norm_backward(d_norm_two, normed_two, factor_two, gb_back)
    grad_gb, grad_sb = (grad_gb[0], grad_sb[0])
    d_middle = d_out.astype(jnp.float32) + d_mid_norm
    d_branch = d_middle.astype(jnp.bfloat16)
    grad_wo = over_rows(ctx_low, d_branch)
    grad_bo = jnp.sum(d_branch.astype(jnp.float32), axis=0)
    d_ctx = over_cols(d_branch, wo_back).astype(jnp.bfloat16)
    do_heads = d_ctx.reshape(local_rows, heads, HD)
    delta = jnp.sum(d_ctx.astype(jnp.float32).reshape(local_rows, heads, HD) * ctx_acc, axis=-1).T
    k_back, v_back = (k_blocks, v_blocks)
    zero_heads = jnp.zeros((local_rows, heads, HD), jnp.float32)

    def grad_step(acc, item):
        k_part, v_part, index = item
        col_ids = index * block_rows + jnp.arange(block_rows, dtype=jnp.int32)

        def work(current):
            prob_low, d_score = grad_terms(
                q_heads, do_heads, lse, delta, k_part, v_part, row_ids, col_ids, prefix
            )
            current = current + 0.125 * jnp.einsum(
                "hqk,khd->qhd", d_score, k_part, preferred_element_type=jnp.float32
            )
            d_key = 0.125 * jnp.einsum(
                "hqk,qhd->khd", d_score, q_heads, preferred_element_type=jnp.float32
            )
            d_value = jnp.einsum(
                "hqk,qhd->khd", prob_low, do_heads, preferred_element_type=jnp.float32
            )
            return (current, (d_key, d_value))

        def skip(current):
            empty = jnp.zeros((block_rows, heads, HD), jnp.float32)
            return (current, (empty, empty))

        needed = (index * block_rows <= last_row) | (index * block_rows < prefix)
        return lax.cond(needed, work, skip, acc)

    dq_acc, (dk_blocks, dv_blocks) = lax.scan(grad_step, zero_heads, (k_back, v_back, block_ids))
    dk_local, dv_local = (
        lax.psum_scatter(
            dk_blocks.reshape(length, width).astype(jnp.bfloat16),
            "seq",
            scatter_dimension=0,
            tiled=True,
        ).astype(jnp.float32),
        lax.psum_scatter(
            dv_blocks.reshape(length, width).astype(jnp.bfloat16),
            "seq",
            scatter_dimension=0,
            tiled=True,
        ).astype(jnp.float32),
    )
    dq_low = dq_acc.reshape(local_rows, width).astype(jnp.bfloat16)
    dk_low = dk_local.astype(jnp.bfloat16)
    dv_low = dv_local.astype(jnp.bfloat16)
    grad_wq = over_rows(norm_one, dq_low)
    grad_bq = jnp.sum(dq_low.astype(jnp.float32), axis=0)
    grad_wk = over_rows(norm_one, dk_low)
    grad_wv = over_rows(norm_one, dv_low)
    grad_bv = jnp.sum(dv_low.astype(jnp.float32), axis=0)
    d_norm_one = (
        over_cols(dq_low, wq_back) + over_cols(dk_low, wk_back) + over_cols(dv_low, wv_back)
    )
    d_in_norm, grad_ga, grad_sa = norm_backward(d_norm_one, normed_one, factor_one, ga_back)
    grad_ga, grad_sa = (grad_ga[0], grad_sa[0])
    grad_tokens = d_middle + d_in_norm
    summed = (
        lax.psum_scatter(grad_ga, ("seq", "batch"), scatter_dimension=0, tiled=True),
        lax.psum_scatter(grad_sa, ("seq", "batch"), scatter_dimension=0, tiled=True),
        lax.psum_scatter(grad_wq, ("seq", "batch"), scatter_dimension=0, tiled=True),
        lax.psum_scatter(grad_bq, ("seq", "batch"), scatter_dimension=0, tiled=True),
        lax.psum_scatter(grad_wk, ("seq", "batch"), scatter_dimension=0, tiled=True),
        lax.psum_scatter(grad_wv, ("seq", "batch"), scatter_dimension=0, tiled=True),
        lax.psum_scatter(grad_bv, ("seq", "batch"), scatter_dimension=0, tiled=True),
        lax.psum_scatter(grad_wo, ("seq", "batch"), scatter_dimension=0, tiled=True),
        lax.psum_scatter(grad_bo, ("seq", "batch"), scatter_dimension=0, tiled=True),
        lax.psum_scatter(grad_gb, ("seq", "batch"), scatter_dimension=0, tiled=True),
        lax.psum_scatter(grad_sb, ("seq", "batch"), scatter_dimension=0, tiled=True),
        lax.psum_scatter(grad_wu, ("seq", "batch"), scatter_dimension=0, tiled=True),
        lax.psum_scatter(grad_bu, ("seq", "batch"), scatter_dimension=0, tiled=True),
        lax.psum_scatter(grad_wd, ("seq", "batch"), scatter_dimension=0, tiled=True),
        lax.psum_scatter(grad_bd, ("seq", "batch"), scatter_dimension=0, tiled=True),
    )
    return (
        layer_out[None],
        grad_tokens[None],
        summed[0],
        summed[1],
        summed[2],
        summed[3],
        summed[4],
        summed[5],
        summed[6],
        summed[7],
        summed[8],
        summed[9],
        summed[10],
        summed[11],
        summed[12],
        summed[13],
        summed[14],
    )


def solution(mesh):
    seq, batch = (mesh.shape["seq"], mesh.shape["batch"])
    if batch == 2 and seq == 16:
        fine = Mesh(mesh.devices.reshape(seq // 4, 2, 2, batch), ALL)
        along, run = (SEQ, body)
    else:
        fine, along, run = (mesh, "seq", plain_body)
    every = along + ("batch",) if run is body else ("seq", "batch")
    act, mat, vec = (P("batch", along, None), P(every, None), P(every))
    return jax.shard_map(
        run,
        mesh=fine,
        in_specs=(
            act, act, P("batch"), vec, vec, mat, vec, mat, mat, vec, mat, vec, vec, vec, mat, vec, mat,
            vec,
        ),
        out_specs=(
            act, act, vec, vec, mat, vec, mat, mat, vec, mat, vec, vec, vec, mat, vec, mat, vec,
        ),
        check_vma=False,
    )
```
